32 devices in a mesh: block: 4 (over y, x), span: 2 (over core), stream: 4 (over z).
Axes of the slice: x: 2, y: 2, z: 4, core: 2. Of those that a mesh axis runs over, the one named last changes fastest.
Arguments:
- flow_state: float32 [4, 256, 16, 5, 1024], P('block', 'stream', None, None, 'span'), may hold values from -6 to 6
- wave_speed: float32 [4, 256, 16, 1024], P('block', 'stream', None, 'span'), may hold values from 0.5 to 2
- char_scale: float32 [5], replicated, may hold values from 0.002 to 4
- span_ratio: float32 [5], replicated, may hold values from 0.3 to 1
- send_tile: int32 [4, 2, 4, 8, 16], P('block', 'span', 'stream'), may hold values from 0 to 1023
- recv_tile: int32 [4, 2, 4, 8, 16], P('block', 'span', 'stream'), may hold values from 0 to 1023, as said below
- recv_live: int32 [4, 2, 4, 8, 16], P('block', 'span', 'stream'), may hold values from 0 to 1, as said below
- interp_weight: float32 [4, 2, 4, 8, 16], P('block', 'span', 'stream'), may hold values from 0.2 to 1
Outputs:
- new_state: float32 [4, 256, 16, 5, 1024], P('block', 'stream', None, None, 'span')
The draws below stay inside these ranges and needn't reach their ends.
Inputs may be any that keep to these rules, and one draw needn't show every extreme that they name: `recv_tile`: the 128 entries of one device are all different. `recv_live`: on each device the live slots from one peer come first; every device has 16 live slots from at least one peer, and one device has 16 from every peer.
All inputs are finite; a program needn't handle non-finite values.
Results may differ from the reference program's by a relative error of at most 0.000088.
Values sent between devices are 32-bit elements; how exact they have to be, the bound alone decides.
No kernel may reach another device: no remote copies, remote signals or barrier semaphores. Data moves between devices by JAX's collectives and lax.ppermute only.
A program may use at most 256 MiB of HBM per device.

```python
import math
import jax
import jax.numpy as jnp
from jax import lax

VARS = 5
CAP = 16
CX = 64
CY = 16
CZ = 512
BLOCKS = 4
SLABS = 2
SECTIONS = 4
PEERS = 8
NX = 256
NZ = 1024


def draw_recv_tile(key, part):
    device_keys = jax.random.split(key, BLOCKS * SLABS * SECTIONS)

    def one_device(device_key):
        return jax.random.permutation(device_key, CX * CY)[:PEERS * CAP].astype(jnp.int32)
    picked = jax.vmap(one_device)(device_keys)
    return picked.reshape(BLOCKS, SLABS, SECTIONS, PEERS, CAP)


def draw_recv_live(key, part):
    key_count, key_heavy, key_full, key_device = jax.random.split(key, 4)
    counts = jax.random.randint(key_count, (BLOCKS, SLABS, SECTIONS, PEERS), 0, CAP + 1)
    heavy_block = jax.random.randint(key_heavy, (), 0, BLOCKS)
    block_index = jnp.arange(BLOCKS, dtype=jnp.int32)[:, None, None, None]
    counts = jnp.minimum(counts + jnp.where(block_index == heavy_block, CAP // 2, 0), CAP)
    full_peer = jax.random.randint(key_full, (BLOCKS, SLABS, SECTIONS, 1), 0, PEERS)
    peer_index = jnp.arange(PEERS, dtype=jnp.int32)
    counts = jnp.where(peer_index == full_peer, CAP, counts)
    full_device = jax.random.randint(key_device, (), 0, BLOCKS * SLABS * SECTIONS)
    device_index = jnp.arange(BLOCKS * SLABS * SECTIONS, dtype=jnp.int32).reshape(BLOCKS, SLABS, SECTIONS, 1)
    counts = jnp.where(device_index == full_device, CAP, counts)
    slot_index = jnp.arange(CAP, dtype=jnp.int32)
    return (slot_index < counts[..., None]).astype(jnp.int32)


def touch_ends(drawn, stream_key, least, high):
    longest = drawn.shape.index(max(drawn.shape))
    spots = []
    for shift in (0, 1):
        where = [jax.random.randint(jax.random.fold_in(stream_key, axis), (), 0, length) for axis, length in enumerate(drawn.shape)]
        where[longest] = (where[longest] + shift) % drawn.shape[longest]
        spots.append(tuple(where))
    return drawn.at[spots[0]].set(least).at[spots[1]].set(high)


def block_levels(stream_key, dims, shards, smallest, high):
    gain = 1.0
    for dim, blocks in shards:
        steps = jax.random.uniform(jax.random.fold_in(jax.random.fold_in(stream_key, 6), dim), (blocks,), jnp.float32, smallest / len(shards), high / len(shards))
        gain = gain * jnp.repeat(jnp.exp(steps), dims[dim] // blocks).reshape((-1,) + (1,) * (len(dims) - 1 - dim))
    return gain


def normal_values(own_key, dims, deviation, reach, cuts=(), held_as=jnp.bfloat16):
    array = jax.random.normal(own_key, dims, jnp.float32) * deviation
    if len(cuts) > 0:
        array = block_levels(own_key, dims, cuts, -0.22, 0.18) * array
    return jnp.clip(array, min=-reach, max=reach).astype(held_as)


def setup_inputs(seed: int = 0) -> dict:
    seeds = jax.random.split(jax.random.key(seed), 9)
    return {
        "flow_state": normal_values(seeds[0], (BLOCKS, NX, CY, VARS, NZ), 1.0, 6.0, ((0, 4), (1, 4), (4, 2)), jnp.float32),
        "wave_speed": jnp.clip(jnp.exp(math.log(2.0) - 1.3862944 * jax.random.uniform(seeds[1], (BLOCKS, NX, CY, NZ), jnp.float32) ** block_levels(seeds[1], (BLOCKS, NX, CY, NZ), ((0, 4), (1, 4), (3, 2)), -0.2, 0.2)), 0.5, 2.0),
        "char_scale": jnp.clip(jnp.exp(jax.random.uniform(seeds[2], (VARS,), jnp.float32, math.log(0.002), math.log(4.0))), 0.002, 4.0),
        "span_ratio": jnp.clip(jnp.exp(jax.random.uniform(seeds[3], (VARS,), jnp.float32, math.log(0.3), math.log(1.0))), 0.3, 1.0),
        "send_tile": touch_ends(jax.random.randint(seeds[4], (BLOCKS, SLABS, SECTIONS, PEERS, CAP), 0, CX * CY), jax.random.fold_in(seeds[4], 1), 0, (CX * CY) - 1).astype(jnp.int32),
        "recv_tile": draw_recv_tile(jax.random.fold_in(seeds[8], 71), 0),
        "recv_live": draw_recv_live(jax.random.fold_in(seeds[8], 71), 0),
        "interp_weight": jnp.clip(0.2 + 0.8 * jax.random.uniform(seeds[7], (BLOCKS, SLABS, SECTIONS, PEERS, CAP), jnp.float32) ** block_levels(seeds[7], (BLOCKS, SLABS, SECTIONS, PEERS, CAP), ((0, 4), (1, 2), (2, 4)), -0.2, 0.2), 0.2, 1.0),
    }


def minmod(first_diff, second_diff):
    return jnp.maximum(jnp.minimum(first_diff, second_diff), 0.0) + jnp.minimum(jnp.maximum(first_diff, second_diff), 0.0)


def face_value(behind, centre, forward):
    return centre + 0.5 * minmod(centre - behind, forward - centre)


def residual_of(padded, here_speed, prior_speed, rate_x, rate_z, width_x, width_z):
    def along_x(offset):
        return padded[:, 2 + offset:2 + offset + width_x, :, :, 2:2 + width_z]

    def along_z(offset):
        return padded[:, 2:2 + width_x, :, :, 2 + offset:2 + offset + width_z]

    right_x = rate_x * here_speed * face_value(along_x(-1), along_x(0), along_x(1))
    left_x = rate_x * prior_speed * face_value(along_x(-2), along_x(-1), along_x(0))
    right_z = rate_z * face_value(along_z(-1), along_z(0), along_z(1))
    left_z = rate_z * face_value(along_z(-2), along_z(-1), along_z(0))
    return left_x - right_x + left_z - right_z


def to_tiles(field):
    shaped = field.reshape(BLOCKS, SECTIONS, CX, CY, VARS, SLABS, CZ)
    shaped = jnp.transpose(shaped, (0, 5, 1, 2, 3, 4, 6))
    return shaped.reshape(BLOCKS * SLABS, SECTIONS, CX * CY, VARS, CZ)


def from_tiles(tile_rows):
    shaped = tile_rows.reshape(BLOCKS, SLABS, SECTIONS, CX, CY, VARS, CZ)
    shaped = jnp.transpose(shaped, (0, 2, 3, 4, 5, 1, 6))
    return shaped.reshape(BLOCKS, SECTIONS * CX, CY, VARS, SLABS * CZ)


def fill_fringe(flow_state, send_tile, recv_tile, recv_live, interp_weight):
    tile_rows = to_tiles(flow_state)
    sender_view = jnp.transpose(send_tile.reshape(PEERS, SECTIONS, PEERS, CAP), (2, 1, 0, 3))
    section_index = jnp.arange(SECTIONS, dtype=jnp.int32)[None, :, None, None]
    peer_index = jnp.arange(PEERS, dtype=jnp.int32)[None, None, :, None]
    owner_index = jnp.arange(PEERS, dtype=jnp.int32)[:, None, None, None]
    donors = tile_rows[peer_index, section_index, sender_view]
    targets = recv_tile.reshape(PEERS, SECTIONS, PEERS, CAP)
    previous = tile_rows[owner_index, section_index, targets]
    weight = interp_weight.reshape(PEERS, SECTIONS, PEERS, CAP)[..., None, None]
    live_mask = recv_live.reshape(PEERS, SECTIONS, PEERS, CAP)[..., None, None]
    blended = jnp.where(live_mask == 1, (1.0 - weight) * previous + weight * donors, previous)
    tile_rows = tile_rows.at[owner_index, section_index, targets].set(blended)
    return from_tiles(tile_rows)


def reference(flow_state, wave_speed, char_scale, span_ratio, send_tile, recv_tile, recv_live, interp_weight):
    filled = fill_fringe(flow_state, send_tile, recv_tile, recv_live, interp_weight)
    padded = jnp.pad(filled, ((0, 0), (2, 2), (0, 0), (0, 0), (2, 2)))
    speed_pad = jnp.pad(wave_speed, ((0, 0), (1, 0), (0, 0), (0, 0)))
    here_speed = wave_speed[:, :, :, None, :]
    prior_speed = speed_pad[:, :-1, :, None, :]
    rate_x = char_scale[:, None]
    rate_z = (char_scale * span_ratio)[:, None]
    residual = residual_of(padded, here_speed, prior_speed, rate_x, rate_z, NX, NZ)
    courant = 100.0 * rate_x * here_speed
    courant_prior = 100.0 * rate_x * prior_speed
    coupling = courant_prior / (1.0 + courant)
    source = 100.0 * residual / (1.0 + courant)

    def advance(running, inputs):
        running = inputs[0] * running + inputs[1]
        return running, running

    start = jnp.zeros((BLOCKS, CY, VARS, NZ), jnp.float32)
    _, marched = lax.scan(advance, start, (jnp.moveaxis(coupling, 1, 0), jnp.moveaxis(source, 1, 0)))
    return filled + jnp.moveaxis(marched, 0, 1)
```

```python
import jax
import jax.numpy as jnp
from jax import lax
from jax.experimental import pallas as pl
from jax.experimental.pallas import tpu as pltpu
from jax.sharding import PartitionSpec as P

LANES = 128
SUB = 8
F32 = jnp.float32


def space(kind):
    return pl.BlockSpec(memory_space=kind)


SMEM, VMEM, HBM = pltpu.SMEM, pltpu.VMEM, pltpu.HBM

RING = ("block", "span")


def limited(first, second):
    return jnp.maximum(
        jnp.minimum(second, jnp.maximum(first, 0.0)), jnp.minimum(first, 0.0)
    )


def call(kernel, ins, outs, out_shape, scratch=(), aliases=None, limit=8 << 20, micros=0):
    return pl.pallas_call(
        kernel,
        out_shape=out_shape,
        in_specs=[space(k) for k in ins],
        out_specs=[space(k) for k in outs],
        scratch_shapes=list(scratch),
        input_output_aliases=aliases or {},
        compiler_params=pltpu.CompilerParams(vmem_limit_bytes=limit),
        cost_estimate=pl.CostEstimate(flops=0, transcendentals=0, bytes_accessed=int(micros * 3.0e6)),
    )


def present(ref, axis, distance):
    source = lax.axis_index(axis) - distance
    inside = (source >= 0) & (source < lax.axis_size(axis))
    return ref[...] * jnp.where(inside, 1.0, 0.0)


def gather_kernel(send_ref, flow_ref, *refs):
    *out_refs, sem = refs
    _, capacity, _ = out_refs[0].shape
    rows_y = flow_ref.shape[2]
    place = lax.axis_index(RING)

    def copy_of(turn, slot):
        tile = send_ref[place ^ turn, slot]
        return pltpu.make_async_copy(
            flow_ref.at[tile // rows_y, :, pl.ds(tile % rows_y, 1), :],
            out_refs[turn].at[:, pl.ds(slot, 1), :],
            sem,
        )

    for turn in range(len(out_refs)):

        @pl.loop(0, capacity)
        def _(slot):
            copy_of(turn, slot).start()

    for turn in range(len(out_refs)):

        @pl.loop(0, capacity)
        def _(slot):
            copy_of(turn, slot).wait()


def growth_kernel(scale_ref, flow_hbm, speed_hbm, flow_ref, speed_ref, ratio_ref, growth_ref, total_ref, last_ref, sem):
    width_x, components, rows_y, width_z = growth_ref.shape
    speed_copy = pltpu.make_async_copy(speed_hbm, speed_ref, sem.at[0])
    flow_copy = pltpu.make_async_copy(flow_hbm, flow_ref, sem.at[1])
    speed_copy.start()
    flow_copy.start()
    speed_copy.wait()
    halves = rows_y // SUB

    @pl.loop(0, components * halves)
    def _(group):
        v = group // halves
        y = pl.ds(pl.multiple_of((group % halves) * SUB, SUB), SUB)
        scale = 100.0 * scale_ref[v]

        def step(x, run):
            rate = scale * speed_ref[x, y, :]
            ratio = 1.0 / (1.0 + rate)
            grown = ratio * run
            ratio_ref[x, v, y, :] = ratio
            growth_ref[x, v, y, :] = grown
            return rate * grown

        total_ref[v, y, :] = lax.fori_loop(0, width_x, step, jnp.ones((SUB, width_z), F32), unroll=4)
        last_ref[v, y, :] = scale * speed_ref[width_x - 1, y, :] * ratio_ref[width_x - 1, v, y, :]

    flow_copy.wait()


def fill_kernel(tile_ref, live_ref, weight_ref, flow_ref, *refs):
    *arrived_refs, filled_ref, rows_ref, tail_ref, head_ref = refs
    width_x, components, rows_y, width_z = filled_ref.shape
    _, capacity, _ = arrived_refs[0].shape

    place = lax.axis_index(RING)
    for turn, arrived_ref in enumerate(arrived_refs):
        peer = place ^ turn

        @pl.loop(0, capacity)
        def _(slot):
            @pl.when(live_ref[peer, slot] == 1)
            def _():
                tile = tile_ref[peer, slot]
                weight = weight_ref[peer, slot]
                x = tile // rows_y
                y = pl.ds(tile % rows_y, 1)
                for v in range(components):
                    old = filled_ref[x, v, y, :]
                    new = arrived_ref[v, pl.ds(slot, 1), :]
                    filled_ref[x, v, y, :] = (1.0 - weight) * old + weight * new

    lane = lax.broadcasted_iota(jnp.int32, (rows_y, LANES), 1)
    for v in range(components):

        def pack(x, packed):
            tail, head = packed
            here = lane // 2 == x
            tail = jnp.where(
                here, pltpu.roll(filled_ref[x, v, :, width_z - LANES :], 2 * x + 2, 1), tail
            )
            head = jnp.where(here, pltpu.roll(filled_ref[x, v, :, :LANES], 2 * x + 1, 1), head)
            return tail, head

        zero = jnp.zeros((rows_y, LANES), F32)
        tail_ref[v], head_ref[v] = lax.fori_loop(0, width_x, pack, (zero, zero), unroll=4)
        for spot, x in enumerate((0, 1, width_x - 2, width_x - 1)):
            rows_ref[spot, v] = filled_ref[x, v]


def scan_kernel(
    scale_ref, span_ref, filled_ref, ratio_ref, speed_ref, tail_ref, head_ref, before_ref, after_ref,
    local_ref, out_ref, prior_ref, face_ref, diff_ref
):
    width_x, components, rows_y, width_z = local_ref.shape
    halves = rows_y // SUB
    blocks = width_z // LANES
    before = present(before_ref, "span", 1)
    after = present(after_ref, "span", -1)
    tail = tail_ref[...]
    head = head_ref[...]
    outer = 0.5 * (before - pltpu.roll(before, 1, 2))
    inner = 0.5 * (head - before)
    prior_ref[...] = before
    face_ref[...] = before + limited(outer, inner)
    diff_ref[...] = 0.5 * (after - tail)
    lane = lax.broadcasted_iota(jnp.int32, (SUB, LANES), 1)
    first = lane == 0
    final = lane == LANES - 1

    @pl.loop(0, components * halves)
    def _(group):
        v = group // halves
        y = pl.ds(pl.multiple_of((group % halves) * SUB, SUB), SUB)
        scale = 100.0 * scale_ref[v]
        scale_z = 100.0 * (scale_ref[v] * span_ref[v])
        prior = prior_ref[v, y, :]
        face = face_ref[v, y, :]
        diff = diff_ref[v, y, :]

        def load(ref, *at):
            return [ref[(*at, y, slice(b * LANES, (b + 1) * LANES))] for b in range(blocks)]

        def step(x, carry, has_ahead=True, has_behind=True):
            here, rise, inflow = carry
            turn = LANES - 2 * x - 1
            back = [pltpu.roll(prior, turn, 1)] + [pltpu.roll(u, 1, 1) for u in here]
            half = [0.5 * (here[b] - jnp.where(first, back[b], back[b + 1])) for b in range(blocks)]
            ahead = [pltpu.roll(d, LANES - 1, 1) for d in half] + [pltpu.roll(diff, turn - 1, 1)]
            faces = [
                here[b] + limited(half[b], jnp.where(final, ahead[b + 1], ahead[b]))
                for b in range(blocks)
            ]
            shifted = [pltpu.roll(face, turn, 1)] + [pltpu.roll(g, 1, 1) for g in faces]
            cross = [
                scale_z * (jnp.where(first, shifted[b], shifted[b + 1]) - faces[b])
                for b in range(blocks)
            ]
            ratio = load(ratio_ref, x, v)
            speed = load(speed_ref, x)
            if has_ahead:
                later = load(filled_ref, x + 1, v)
                rise_later = [0.5 * (later[b] - here[b]) for b in range(blocks)]
            else:
                later = rise_later = here
            flux = []
            for b in range(blocks):
                known = inflow[b] + here[b] + cross[b]
                if has_ahead and has_behind:
                    slope = limited(rise[b], rise_later[b])
                    value = ratio[b] * (known + slope)
                    out = value - slope
                else:
                    out = value = ratio[b] * known
                local_ref[x, v, y, slice(b * LANES, (b + 1) * LANES)] = out
                flux.append((scale * speed[b]) * value)
            return later, rise_later, flux

        zeros = [jnp.zeros((SUB, LANES), F32)] * blocks
        carry = step(0, (load(filled_ref, 0, v), zeros, zeros), has_behind=False)
        carry = lax.fori_loop(1, width_x - 1, step, carry, unroll=2)
        _, _, flux = step(width_x - 1, carry, has_ahead=False)
        for b in range(blocks):
            out_ref[v, y, slice(b * LANES, (b + 1) * LANES)] = flux[b]


def edge_kernel(
    flux_ref, total_ref, last_ref, rows_ref, behind_ref, ahead_ref, flux_out, first_out, last_out
):
    behind = present(behind_ref, "stream", 1)
    ahead = present(ahead_ref, "stream", -1)
    row = [rows_ref[k] for k in range(4)]
    slope_first = limited(0.5 * (row[0] - behind), 0.5 * (row[1] - row[0]))
    slope_last = limited(0.5 * (row[3] - row[2]), 0.5 * (ahead - row[3]))
    kept = last_ref[...] * slope_last
    flux_out[...] = flux_ref[...] + total_ref[...] * slope_first + kept
    first_out[...] = slope_first
    last_out[...] = kept


def combine_kernel(local_ref, growth_ref, first_ref, last_ref, *refs):
    *line_refs, out_hbm, done_ref, inflow_ref, sem = refs
    width_x, components, rows_y, width_z = local_ref.shape
    count = (len(line_refs) + 1) // 2
    flux_refs, total_refs = line_refs[:count], line_refs[count:]
    inflow = first_ref[...]
    product = None
    for distance in range(1, count + 1):
        flux = present(flux_refs[distance - 1], "stream", distance)
        inflow = inflow + (flux if product is None else product * flux)
        if distance < count:
            total = total_refs[distance - 1][...]
            product = total if product is None else product * total
    inflow_ref[...] = inflow
    part = 4

    def copy_of(k):
        rows = pl.ds(k * part, part)
        return pltpu.make_async_copy(done_ref.at[rows], out_hbm.at[rows], sem)

    @pl.loop(0, width_x // part)
    def _(k):
        for v in range(components):
            inflow = inflow_ref[v]
            for i in range(part):
                x = k * part + i
                done_ref[x, v] = local_ref[x, v] + growth_ref[x, v] * inflow

        @pl.when(k == 0)
        def _():
            done_ref[0] = done_ref[0] - first_ref[...]

        @pl.when(k == width_x // part - 1)
        def _():
            done_ref[width_x - 1] = done_ref[width_x - 1] - last_ref[...]

        copy_of(k).start()

    @pl.loop(0, width_x // part)
    def _(k):
        copy_of(k).wait()


def moved(value, axis, distance):
    count = lax.axis_size(axis)
    return lax.ppermute(value, axis, [(i, (i + distance) % count) for i in range(count)])


def on_device(
    flow_state, wave_speed, char_scale, span_ratio, send_tile, recv_tile, recv_live, interp_weight
):
    _, width_x, rows_y, components, width_z = flow_state.shape
    peers, capacity = send_tile.shape[-2:]
    sections = lax.axis_size("stream")
    flow = pltpu.with_memory_space_constraint(jnp.transpose(flow_state[0], (0, 2, 1, 3)), HBM)
    speed = wave_speed[0]
    state = (width_x, components, rows_y, width_z)
    line = (components, rows_y, width_z)
    edge = (components, rows_y, LANES)
    hold = lambda shape: pltpu.VMEM(shape, F32)
    send, tile, live, weight = (
        t.reshape(peers, capacity) for t in (send_tile, recv_tile, recv_live, interp_weight)
    )
    assert peers & (peers - 1) == 0

    outgoing = call(
        gather_kernel,
        (SMEM, HBM), (VMEM,) * peers,
        [jax.ShapeDtypeStruct((components, capacity, width_z), F32)] * peers,
        [pltpu.SemaphoreType.DMA],
    )(send, flow)
    arrived = [outgoing[0]]
    for turn in range(1, peers):
        arrived.append(lax.ppermute(outgoing[turn], RING, [(i, i ^ turn) for i in range(peers)]))
    flow_in, speed_in, ratio, growth, total, last = call(
        growth_kernel,
        (SMEM, HBM, HBM), (VMEM,) * 6,
        [hold(state), hold(speed.shape), hold(state), hold(state), hold(line), hold(line)],
        [pltpu.SemaphoreType.DMA((2,))],
        micros=6,
    )(char_scale, flow, speed)
    filled, rows, tail, head = call(
        fill_kernel,
        (SMEM,) * 3 + (VMEM,) * (1 + peers), (VMEM,) * 4,
        [hold(state), hold((4, *line)), hold(edge), hold(edge)],
        aliases={3: 0},
        micros=5,
    )(tile, live, weight, flow_in, *arrived)
    before = moved(tail, "span", 1)
    after = moved(head, "span", -1)
    behind = moved(rows[3], "stream", 1)
    ahead = moved(rows[0], "stream", -1)
    local, flux = call(
        scan_kernel,
        (SMEM, SMEM) + (VMEM,) * 7, (VMEM,) * 2,
        [hold(state), hold(line)],
        [pltpu.VMEM(edge, F32)] * 3,
        aliases={2: 0},
        micros=12,
    )(char_scale, span_ratio, filled, ratio, speed_in, tail, head, before, after)
    flux, first_slope, last_slope = call(
        edge_kernel, (VMEM,) * 6, (VMEM,) * 3, [jax.ShapeDtypeStruct(line, F32)] * 3
    )(flux, total, last, rows, behind, ahead)
    fluxes = [moved(flux, "stream", d) for d in range(1, sections)]
    totals = [moved(total, "stream", d) for d in range(1, sections - 1)]
    (done,) = call(
        combine_kernel,
        (VMEM,) * (2 * sections + 1), (HBM,),
        [jax.ShapeDtypeStruct(state, F32)],
        [pltpu.VMEM(state, F32), pltpu.VMEM(line, F32), pltpu.SemaphoreType.DMA],
        limit=14 << 20,
        micros=5,
    )(local, growth, first_slope, last_slope, *fluxes, *totals)
    return jnp.transpose(done, (0, 2, 1, 3))[None]


def solution(mesh):
    return jax.shard_map(
        on_device,
        mesh=mesh,
        in_specs=(
            P("block", "stream", None, None, "span"),
            P("block", "stream", None, "span"),
            P(),
            P(),
            P("block", "span", "stream", None, None),
            P("block", "span", "stream", None, None),
            P("block", "span", "stream", None, None),
            P("block", "span", "stream", None, None),
        ),
        out_specs=P("block", "stream", None, None, "span"),
        check_vma=False,
    )
```

```python
import jax
import jax.numpy as jnp
from jax import lax
from jax.experimental import pallas as pl
from jax.experimental.pallas import tpu as pltpu
from jax.sharding import PartitionSpec as P

LANES = 128
SUB = 8
STEPS = 16
F32 = jnp.float32


def space(kind):
    return pl.BlockSpec(memory_space=kind)


SMEM, VMEM, HBM = pltpu.SMEM, pltpu.VMEM, pltpu.HBM

RING = ("block", "span")


def limited(first, second):
    return jnp.maximum(
        jnp.minimum(second, jnp.maximum(first, 0.0)), jnp.minimum(first, 0.0)
    )


def call(kernel, ins, outs, out_shape, scratch=(), aliases=None, limit=8 << 20, micros=0):
    return pl.pallas_call(
        kernel,
        out_shape=out_shape,
        in_specs=[space(k) for k in ins],
        out_specs=[space(k) for k in outs],
        scratch_shapes=list(scratch),
        input_output_aliases=aliases or {},
        compiler_params=pltpu.CompilerParams(vmem_limit_bytes=limit),
        cost_estimate=pl.CostEstimate(flops=0, transcendentals=0, bytes_accessed=int(micros * 3.0e6)),
    )


def present(ref, axis, distance):
    source = lax.axis_index(axis) - distance
    inside = (source >= 0) & (source < lax.axis_size(axis))
    return ref[...] * jnp.where(inside, 1.0, 0.0)


def gather_kernel(send_ref, flow_ref, *refs):
    *out_refs, sem = refs
    _, capacity, _ = out_refs[0].shape
    rows_y = flow_ref.shape[2]
    place = lax.axis_index(RING)

    def copy_of(turn, slot):
        tile = send_ref[place ^ turn, slot]
        return pltpu.make_async_copy(
            flow_ref.at[tile // rows_y, :, pl.ds(tile % rows_y, 1), :],
            out_refs[turn].at[:, pl.ds(slot, 1), :],
            sem,
        )

    for turn in range(len(out_refs)):

        @pl.loop(0, capacity)
        def _(slot):
            copy_of(turn, slot).start()

    for turn in range(len(out_refs)):

        @pl.loop(0, capacity)
        def _(slot):
            copy_of(turn, slot).wait()


def growth_kernel(scale_ref, flow_hbm, speed_hbm, flow_ref, speed_ref, ratio_ref, growth_ref, total_ref, last_ref, sem):
    width_x, components, rows_y, width_z = growth_ref.shape
    speed_copy = pltpu.make_async_copy(speed_hbm, speed_ref, sem.at[0])
    flow_copy = pltpu.make_async_copy(flow_hbm, flow_ref, sem.at[1])
    speed_copy.start()
    flow_copy.start()
    speed_copy.wait()
    halves = rows_y // SUB

    @pl.loop(0, components * halves)
    def _(group):
        v = group // halves
        y = pl.ds(pl.multiple_of((group % halves) * SUB, SUB), SUB)
        scale = 100.0 * scale_ref[v]

        def step(x, run):
            rate = scale * speed_ref[x, y, :]
            ratio = 1.0 / (1.0 + rate)
            grown = ratio * run
            ratio_ref[x, v, y, :] = ratio
            growth_ref[x, v, y, :] = grown
            return rate * grown

        total_ref[v, y, :] = lax.fori_loop(0, width_x, step, jnp.ones((SUB, width_z), F32), unroll=4)
        last_ref[v, y, :] = scale * speed_ref[width_x - 1, y, :] * ratio_ref[width_x - 1, v, y, :]

    flow_copy.wait()


def fill_kernel(tile_ref, live_ref, weight_ref, flow_ref, *refs):
    *arrived_refs, filled_ref, rows_ref, tail_ref, head_ref = refs
    width_x, components, rows_y, width_z = filled_ref.shape
    _, capacity, _ = arrived_refs[0].shape

    place = lax.axis_index(RING)
    for turn, arrived_ref in enumerate(arrived_refs):
        peer = place ^ turn

        @pl.loop(0, capacity)
        def _(slot):
            @pl.when(live_ref[peer, slot] == 1)
            def _():
                tile = tile_ref[peer, slot]
                weight = weight_ref[peer, slot]
                x = tile // rows_y
                y = pl.ds(tile % rows_y, 1)
                for v in range(components):
                    old = filled_ref[x, v, y, :]
                    new = arrived_ref[v, pl.ds(slot, 1), :]
                    filled_ref[x, v, y, :] = (1.0 - weight) * old + weight * new

    lane = lax.broadcasted_iota(jnp.int32, (rows_y, LANES), 1)
    for v in range(components):

        def pack(x, packed):
            tail, head = packed
            here = lane // 2 == x
            tail = jnp.where(
                here, pltpu.roll(filled_ref[x, v, :, width_z - LANES :], 2 * x + 2, 1), tail
            )
            head = jnp.where(here, pltpu.roll(filled_ref[x, v, :, :LANES], 2 * x + 1, 1), head)
            return tail, head

        zero = jnp.zeros((rows_y, LANES), F32)
        tail_ref[v], head_ref[v] = lax.fori_loop(0, width_x, pack, (zero, zero), unroll=32)
        for spot, x in enumerate((0, 1, width_x - 2, width_x - 1)):
            rows_ref[spot, v] = filled_ref[x, v]


def scan_kernel(
    scale_ref, span_ref, filled_ref, ratio_ref, speed_ref, tail_ref, head_ref, before_ref, after_ref,
    local_ref, out_ref, prior_ref, face_ref, diff_ref
):
    width_x, components, rows_y, width_z = local_ref.shape
    halves = rows_y // SUB
    blocks = width_z // LANES
    before = present(before_ref, "span", 1)
    after = present(after_ref, "span", -1)
    tail = tail_ref[...]
    head = head_ref[...]
    outer = 0.5 * (before - pltpu.roll(before, 1, 2))
    inner = 0.5 * (head - before)
    prior_ref[...] = before
    face_ref[...] = before + limited(outer, inner)
    diff_ref[...] = 0.5 * (after - tail)
    lane = lax.broadcasted_iota(jnp.int32, (SUB, LANES), 1)
    first = lane == 0
    final = lane == LANES - 1

    @pl.loop(0, components * halves)
    def _(group):
        v = group // halves
        y = pl.ds(pl.multiple_of((group % halves) * SUB, SUB), SUB)
        scale = 100.0 * scale_ref[v]
        scale_z = 100.0 * (scale_ref[v] * span_ref[v])
        prior = prior_ref[v, y, :]
        face = face_ref[v, y, :]
        diff = diff_ref[v, y, :]
        every = range(blocks)

        def load(ref, *at):
            return [ref[(*at, y, slice(b * LANES, (b + 1) * LANES))] for b in every]

        def right(values, edge):
            moved_right = [edge] + [pltpu.roll(u, 1, 1) for u in values]
            return [jnp.where(first, moved_right[b], moved_right[b + 1]) for b in every]

        def left(values, edge):
            moved_left = [pltpu.roll(u, LANES - 1, 1) for u in values] + [edge]
            return [jnp.where(final, moved_left[b + 1], moved_left[b]) for b in every]

        def steps(k, carry):
            here, rise, inflow = carry
            start = k * STEPS
            rows = [here] + [load(filled_ref, start + i, v) for i in range(1, STEPS)]
            rows.append(load(filled_ref, jnp.minimum(start + STEPS, width_x - 1), v))
            ratios = [load(ratio_ref, start + i, v) for i in range(STEPS)]
            rates = [[scale * a for a in load(speed_ref, start + i)] for i in range(STEPS)]
            known, slopes = [], []
            for i in range(STEPS):
                u = rows[i]
                turn = LANES - 2 * (start + i) - 1
                back = right(u, pltpu.roll(prior, turn, 1))
                fall = [0.5 * (u[b] - back[b]) for b in every]
                grow = left(fall, pltpu.roll(diff, turn - 1, 1))
                faces = [u[b] + limited(fall[b], grow[b]) for b in every]
                shifted = right(faces, pltpu.roll(face, turn, 1))
                rise_later = [0.5 * (rows[i + 1][b] - u[b]) for b in every]
                slope = [limited(rise[b], rise_later[b]) for b in every]
                known.append([u[b] + slope[b] + scale_z * (shifted[b] - faces[b]) for b in every])
                slopes.append(slope)
                rise = rise_later
            outs = []
            for i in range(STEPS):
                value = [ratios[i][b] * (inflow[b] + known[i][b]) for b in every]
                outs.append([value[b] - slopes[i][b] for b in every])
                inflow = [rates[i][b] * value[b] for b in every]
            for i in range(STEPS):
                for b in every:
                    local_ref[start + i, v, y, slice(b * LANES, (b + 1) * LANES)] = outs[i][b]
            return rows[STEPS], rise, inflow

        zeros = [jnp.zeros((SUB, LANES), F32)] * blocks
        _, _, flux = lax.fori_loop(0, width_x // STEPS, steps, (load(filled_ref, 0, v), zeros, zeros))
        for b in every:
            out_ref[v, y, slice(b * LANES, (b + 1) * LANES)] = flux[b]


def edge_kernel(
    flux_ref, total_ref, last_ref, rows_ref, behind_ref, ahead_ref, flux_out, first_out, last_out
):
    behind = present(behind_ref, "stream", 1)
    ahead = present(ahead_ref, "stream", -1)
    row = [rows_ref[k] for k in range(4)]
    slope_first = limited(0.5 * (row[0] - behind), 0.5 * (row[1] - row[0]))
    slope_last = limited(0.5 * (row[3] - row[2]), 0.5 * (ahead - row[3]))
    kept = last_ref[...] * slope_last
    flux_out[...] = flux_ref[...] + total_ref[...] * slope_first + kept
    first_out[...] = slope_first
    last_out[...] = kept


def combine_kernel(local_ref, growth_ref, first_ref, last_ref, *refs):
    *line_refs, out_hbm, done_ref, inflow_ref, sem = refs
    width_x, components, rows_y, width_z = local_ref.shape
    count = (len(line_refs) + 1) // 2
    flux_refs, total_refs = line_refs[:count], line_refs[count:]
    inflow = first_ref[...]
    product = None
    for distance in range(1, count + 1):
        flux = present(flux_refs[distance - 1], "stream", distance)
        inflow = inflow + (flux if product is None else product * flux)
        if distance < count:
            total = total_refs[distance - 1][...]
            product = total if product is None else product * total
    inflow_ref[...] = inflow
    part = 4

    def copy_of(k):
        rows = pl.ds(k * part, part)
        return pltpu.make_async_copy(done_ref.at[rows], out_hbm.at[rows], sem)

    @pl.loop(0, width_x // part)
    def _(k):
        for v in range(components):
            inflow = inflow_ref[v]
            for i in range(part):
                x = k * part + i
                done_ref[x, v] = local_ref[x, v] + growth_ref[x, v] * inflow

        @pl.when(k == 0)
        def _():
            done_ref[0] = done_ref[0] - first_ref[...]

        @pl.when(k == width_x // part - 1)
        def _():
            done_ref[width_x - 1] = done_ref[width_x - 1] - last_ref[...]

        copy_of(k).start()

    @pl.loop(0, width_x // part)
    def _(k):
        copy_of(k).wait()


def moved(value, axis, distance):
    count = lax.axis_size(axis)
    return lax.ppermute(value, axis, [(i, (i + distance) % count) for i in range(count)])


def on_device(
    flow_state, wave_speed, char_scale, span_ratio, send_tile, recv_tile, recv_live, interp_weight
):
    _, width_x, rows_y, components, width_z = flow_state.shape
    peers, capacity = send_tile.shape[-2:]
    sections = lax.axis_size("stream")
    flow = pltpu.with_memory_space_constraint(jnp.transpose(flow_state[0], (0, 2, 1, 3)), HBM)
    speed = wave_speed[0]
    state = (width_x, components, rows_y, width_z)
    line = (components, rows_y, width_z)
    edge = (components, rows_y, LANES)
    hold = lambda shape: pltpu.VMEM(shape, F32)
    send, tile, live, weight = (
        t.reshape(peers, capacity) for t in (send_tile, recv_tile, recv_live, interp_weight)
    )
    assert peers & (peers - 1) == 0

    outgoing = call(
        gather_kernel,
        (SMEM, HBM), (VMEM,) * peers,
        [jax.ShapeDtypeStruct((components, capacity, width_z), F32)] * peers,
        [pltpu.SemaphoreType.DMA],
    )(send, flow)
    arrived = [outgoing[0]]
    for turn in range(1, peers):
        arrived.append(lax.ppermute(outgoing[turn], RING, [(i, i ^ turn) for i in range(peers)]))
    flow_in, speed_in, ratio, growth, total, last = call(
        growth_kernel,
        (SMEM, HBM, HBM), (VMEM,) * 6,
        [hold(state), hold(speed.shape), hold(state), hold(state), hold(line), hold(line)],
        [pltpu.SemaphoreType.DMA((2,))],
        micros=6,
    )(char_scale, flow, speed)
    filled, rows, tail, head = call(
        fill_kernel,
        (SMEM,) * 3 + (VMEM,) * (1 + peers), (VMEM,) * 4,
        [hold(state), hold((4, *line)), hold(edge), hold(edge)],
        aliases={3: 0},
        micros=5,
    )(tile, live, weight, flow_in, *arrived)
    before = moved(tail, "span", 1)
    after = moved(head, "span", -1)
    behind = moved(rows[3], "stream", 1)
    ahead = moved(rows[0], "stream", -1)
    local, flux = call(
        scan_kernel,
        (SMEM, SMEM) + (VMEM,) * 7, (VMEM,) * 2,
        [hold(state), hold(line)],
        [pltpu.VMEM(edge, F32)] * 3,
        aliases={2: 0},
        micros=12,
    )(char_scale, span_ratio, filled, ratio, speed_in, tail, head, before, after)
    flux, first_slope, last_slope = call(
        edge_kernel, (VMEM,) * 6, (VMEM,) * 3, [jax.ShapeDtypeStruct(line, F32)] * 3
    )(flux, total, last, rows, behind, ahead)
    fluxes = [moved(flux, "stream", d) for d in range(1, sections)]
    totals = [moved(total, "stream", d) for d in range(1, sections - 1)]
    (done,) = call(
        combine_kernel,
        (VMEM,) * (2 * sections + 1), (HBM,),
        [jax.ShapeDtypeStruct(state, F32)],
        [pltpu.VMEM(state, F32), pltpu.VMEM(line, F32), pltpu.SemaphoreType.DMA],
        limit=14 << 20,
        micros=5,
    )(local, growth, first_slope, last_slope, *fluxes, *totals)
    return jnp.transpose(done, (0, 2, 1, 3))[None]


def solution(mesh):
    return jax.shard_map(
        on_device,
        mesh=mesh,
        in_specs=(
            P("block", "stream", None, None, "span"),
            P("block", "stream", None, "span"),
            P(),
            P(),
            P("block", "span", "stream", None, None),
            P("block", "span", "stream", None, None),
            P("block", "span", "stream", None, None),
            P("block", "span", "stream", None, None),
        ),
        out_specs=P("block", "stream", None, None, "span"),
        check_vma=False,
    )
```

```python
import functools
import jax
import jax.numpy as jnp
from jax import lax
from jax.experimental import pallas as pl
from jax.experimental.pallas import tpu as pltpu
from jax.sharding import PartitionSpec as P

LANES = 128
SUB = 8
STEPS = 16
F32 = jnp.float32


def space(kind):
    return pl.BlockSpec(memory_space=kind)


SMEM, VMEM, HBM = pltpu.SMEM, pltpu.VMEM, pltpu.HBM

RING = ("block", "span")


def limited(first, second):
    return jnp.maximum(
        jnp.minimum(second, jnp.maximum(first, 0.0)), jnp.minimum(first, 0.0)
    )


def call(kernel, ins, outs, out_shape, scratch=(), aliases=None, limit=8 << 20, micros=0):
    return pl.pallas_call(
        kernel,
        out_shape=out_shape,
        in_specs=[space(k) for k in ins],
        out_specs=[space(k) for k in outs],
        scratch_shapes=list(scratch),
        input_output_aliases=aliases or {},
        compiler_params=pltpu.CompilerParams(vmem_limit_bytes=limit),
        cost_estimate=pl.CostEstimate(flops=0, transcendentals=0, bytes_accessed=int(micros * 3.0e6)),
    )


def present(ref, axis, distance):
    source = lax.axis_index(axis) - distance
    inside = (source >= 0) & (source < lax.axis_size(axis))
    return ref[...] * jnp.where(inside, 1.0, 0.0)


def gather_kernel(send_ref, flow_ref, *refs):
    *out_refs, sem = refs
    _, capacity, _ = out_refs[0].shape
    rows_y = flow_ref.shape[2]
    place = lax.axis_index(RING)

    def copy_of(turn, slot):
        tile = send_ref[place ^ turn, slot]
        return pltpu.make_async_copy(
            flow_ref.at[tile // rows_y, :, pl.ds(tile % rows_y, 1), :],
            out_refs[turn].at[:, pl.ds(slot, 1), :],
            sem,
        )

    for turn in range(len(out_refs)):

        @pl.loop(0, capacity)
        def _(slot):
            copy_of(turn, slot).start()

    for turn in range(len(out_refs)):

        @pl.loop(0, capacity)
        def _(slot):
            copy_of(turn, slot).wait()


def growth_kernel(scale_ref, flow_hbm, speed_hbm, flow_ref, speed_ref, ratio_ref, growth_ref, total_ref, last_ref, sem):
    width_x, components, rows_y, width_z = growth_ref.shape
    speed_copy = pltpu.make_async_copy(speed_hbm, speed_ref, sem.at[0])
    flow_copy = pltpu.make_async_copy(flow_hbm, flow_ref, sem.at[1])
    speed_copy.start()
    flow_copy.start()
    speed_copy.wait()
    halves = rows_y // SUB

    @pl.loop(0, components * halves)
    def _(group):
        v = group // halves
        y = pl.ds(pl.multiple_of((group % halves) * SUB, SUB), SUB)
        scale = 100.0 * scale_ref[v]

        def step(x, run):
            rate = scale * speed_ref[x, y, :]
            ratio = 1.0 / (1.0 + rate)
            grown = ratio * run
            ratio_ref[x, v, y, :] = ratio
            growth_ref[x, v, y, :] = grown
            return rate * grown

        total_ref[v, y, :] = lax.fori_loop(0, width_x, step, jnp.ones((SUB, width_z), F32), unroll=4)
        last_ref[v, y, :] = scale * speed_ref[width_x - 1, y, :] * ratio_ref[width_x - 1, v, y, :]

    flow_copy.wait()


def fill_kernel(turns, extra, tile_ref, live_ref, weight_ref, flow_ref, *refs):
    arrived_refs = refs[: len(turns)]
    filled_ref = refs[len(turns) + extra]
    rows_y = filled_ref.shape[2]
    components, capacity, _ = arrived_refs[0].shape
    place = lax.axis_index(RING)

    for turn, arrived_ref in zip(turns, arrived_refs):
        peer = place ^ turn

        @pl.loop(0, capacity)
        def _(slot):
            @pl.when(live_ref[peer, slot] == 1)
            def _():
                tile = tile_ref[peer, slot]
                weight = weight_ref[peer, slot]
                x = tile // rows_y
                y = pl.ds(tile % rows_y, 1)
                for v in range(components):
                    old = filled_ref[x, v, y, :]
                    new = arrived_ref[v, pl.ds(slot, 1), :]
                    filled_ref[x, v, y, :] = (1.0 - weight) * old + weight * new


def last_fill_kernel(turns, extra, *refs):
    *fill_refs, rows_ref, tail_ref, head_ref = refs
    fill_kernel(turns, extra, *fill_refs)
    filled_ref = fill_refs[-1]
    width_x, components, rows_y, width_z = filled_ref.shape
    lane = lax.broadcasted_iota(jnp.int32, (rows_y, LANES), 1)
    for v in range(components):

        def pack(x, packed):
            tail, head = packed
            here = lane // 2 == x
            tail = jnp.where(
                here, pltpu.roll(filled_ref[x, v, :, width_z - LANES :], 2 * x + 2, 1), tail
            )
            head = jnp.where(here, pltpu.roll(filled_ref[x, v, :, :LANES], 2 * x + 1, 1), head)
            return tail, head

        zero = jnp.zeros((rows_y, LANES), F32)
        tail_ref[v], head_ref[v] = lax.fori_loop(0, width_x, pack, (zero, zero), unroll=32)
        for spot, x in enumerate((0, 1, width_x - 2, width_x - 1)):
            rows_ref[spot, v] = filled_ref[x, v]


def scan_kernel(
    scale_ref, span_ref, filled_ref, ratio_ref, speed_ref, tail_ref, head_ref, before_ref, after_ref,
    local_ref, out_ref, prior_ref, face_ref, diff_ref
):
    width_x, components, rows_y, width_z = local_ref.shape
    halves = rows_y // SUB
    blocks = width_z // LANES
    before = present(before_ref, "span", 1)
    after = present(after_ref, "span", -1)
    tail = tail_ref[...]
    head = head_ref[...]
    outer = 0.5 * (before - pltpu.roll(before, 1, 2))
    inner = 0.5 * (head - before)
    prior_ref[...] = before
    face_ref[...] = before + limited(outer, inner)
    diff_ref[...] = 0.5 * (after - tail)
    lane = lax.broadcasted_iota(jnp.int32, (SUB, LANES), 1)
    first = lane == 0
    final = lane == LANES - 1

    @pl.loop(0, components * halves)
    def _(group):
        v = group // halves
        y = pl.ds(pl.multiple_of((group % halves) * SUB, SUB), SUB)
        scale = 100.0 * scale_ref[v]
        scale_z = 100.0 * (scale_ref[v] * span_ref[v])
        prior = prior_ref[v, y, :]
        face = face_ref[v, y, :]
        diff = diff_ref[v, y, :]
        every = range(blocks)

        def load(ref, *at):
            return [ref[(*at, y, slice(b * LANES, (b + 1) * LANES))] for b in every]

        def right(values, edge):
            moved_right = [edge] + [pltpu.roll(u, 1, 1) for u in values]
            return [jnp.where(first, moved_right[b], moved_right[b + 1]) for b in every]

        def left(values, edge):
            moved_left = [pltpu.roll(u, LANES - 1, 1) for u in values] + [edge]
            return [jnp.where(final, moved_left[b + 1], moved_left[b]) for b in every]

        def steps(k, carry):
            here, rise, inflow = carry
            start = k * STEPS
            rows = [here] + [load(filled_ref, start + i, v) for i in range(1, STEPS)]
            rows.append(load(filled_ref, jnp.minimum(start + STEPS, width_x - 1), v))
            ratios = [load(ratio_ref, start + i, v) for i in range(STEPS)]
            rates = [[scale * a for a in load(speed_ref, start + i)] for i in range(STEPS)]
            known, slopes = [], []
            for i in range(STEPS):
                u = rows[i]
                turn = LANES - 2 * (start + i) - 1
                back = right(u, pltpu.roll(prior, turn, 1))
                fall = [0.5 * (u[b] - back[b]) for b in every]
                grow = left(fall, pltpu.roll(diff, turn - 1, 1))
                faces = [u[b] + limited(fall[b], grow[b]) for b in every]
                shifted = right(faces, pltpu.roll(face, turn, 1))
                rise_later = [0.5 * (rows[i + 1][b] - u[b]) for b in every]
                slope = [limited(rise[b], rise_later[b]) for b in every]
                known.append([u[b] + slope[b] + scale_z * (shifted[b] - faces[b]) for b in every])
                slopes.append(slope)
                rise = rise_later
            outs = []
            for i in range(STEPS):
                value = [ratios[i][b] * (inflow[b] + known[i][b]) for b in every]
                outs.append([value[b] - slopes[i][b] for b in every])
                inflow = [rates[i][b] * value[b] for b in every]
            for i in range(STEPS):
                for b in every:
                    local_ref[start + i, v, y, slice(b * LANES, (b + 1) * LANES)] = outs[i][b]
            return rows[STEPS], rise, inflow

        zeros = [jnp.zeros((SUB, LANES), F32)] * blocks
        _, _, flux = lax.fori_loop(0, width_x // STEPS, steps, (load(filled_ref, 0, v), zeros, zeros))
        for b in every:
            out_ref[v, y, slice(b * LANES, (b + 1) * LANES)] = flux[b]


def edge_kernel(
    flux_ref, total_ref, last_ref, rows_ref, behind_ref, ahead_ref, flux_out, first_out, last_out
):
    behind = present(behind_ref, "stream", 1)
    ahead = present(ahead_ref, "stream", -1)
    row = [rows_ref[k] for k in range(4)]
    slope_first = limited(0.5 * (row[0] - behind), 0.5 * (row[1] - row[0]))
    slope_last = limited(0.5 * (row[3] - row[2]), 0.5 * (ahead - row[3]))
    kept = last_ref[...] * slope_last
    flux_out[...] = flux_ref[...] + total_ref[...] * slope_first + kept
    first_out[...] = slope_first
    last_out[...] = kept


def combine_kernel(local_ref, growth_ref, first_ref, last_ref, *refs):
    *line_refs, out_hbm, done_ref, inflow_ref, sem = refs
    width_x, components, rows_y, width_z = local_ref.shape
    count = (len(line_refs) + 1) // 2
    flux_refs, total_refs = line_refs[:count], line_refs[count:]
    inflow = first_ref[...]
    product = None
    for distance in range(1, count + 1):
        flux = present(flux_refs[distance - 1], "stream", distance)
        inflow = inflow + (flux if product is None else product * flux)
        if distance < count:
            total = total_refs[distance - 1][...]
            product = total if product is None else product * total
    inflow_ref[...] = inflow
    part = 4

    def copy_of(k):
        rows = pl.ds(k * part, part)
        return pltpu.make_async_copy(done_ref.at[rows], out_hbm.at[rows], sem)

    @pl.loop(0, width_x // part)
    def _(k):
        for v in range(components):
            inflow = inflow_ref[v]
            for i in range(part):
                x = k * part + i
                done_ref[x, v] = local_ref[x, v] + growth_ref[x, v] * inflow

        @pl.when(k == 0)
        def _():
            done_ref[0] = done_ref[0] - first_ref[...]

        @pl.when(k == width_x // part - 1)
        def _():
            done_ref[width_x - 1] = done_ref[width_x - 1] - last_ref[...]

        copy_of(k).start()

    @pl.loop(0, width_x // part)
    def _(k):
        copy_of(k).wait()


def moved(value, axis, distance):
    count = lax.axis_size(axis)
    return lax.ppermute(value, axis, [(i, (i + distance) % count) for i in range(count)])


def on_device(
    flow_state, wave_speed, char_scale, span_ratio, send_tile, recv_tile, recv_live, interp_weight
):
    _, width_x, rows_y, components, width_z = flow_state.shape
    peers, capacity = send_tile.shape[-2:]
    sections = lax.axis_size("stream")
    flow = pltpu.with_memory_space_constraint(jnp.transpose(flow_state[0], (0, 2, 1, 3)), HBM)
    speed = wave_speed[0]
    state = (width_x, components, rows_y, width_z)
    line = (components, rows_y, width_z)
    edge = (components, rows_y, LANES)
    hold = lambda shape: pltpu.VMEM(shape, F32)
    send, tile, live, weight = (
        t.reshape(peers, capacity) for t in (send_tile, recv_tile, recv_live, interp_weight)
    )
    assert peers & (peers - 1) == 0

    outgoing = call(
        gather_kernel,
        (SMEM, HBM), (VMEM,) * peers,
        [jax.ShapeDtypeStruct((components, capacity, width_z), F32)] * peers,
        [pltpu.SemaphoreType.DMA],
    )(send, flow)
    order = sorted(range(1, peers), key=lambda turn: (turn == 1, turn & 1, turn))
    arrived = {0: outgoing[0]}
    for turn in order:
        arrived[turn] = lax.ppermute(outgoing[turn], RING, [(i, i ^ turn) for i in range(peers)])
    flow_in, speed_in, ratio, growth, total, last = call(
        growth_kernel,
        (SMEM, HBM, HBM), (VMEM,) * 6,
        [hold(state), hold(speed.shape), hold(state), hold(state), hold(line), hold(line)],
        [pltpu.SemaphoreType.DMA((2,))],
        micros=6,
    )(char_scale, flow, speed)
    totals = [moved(total, "stream", d) for d in range(1, sections - 1)]
    early = [0] + order[: peers // 2 - 1]
    late = order[peers // 2 - 1 :]
    (partly,) = call(
        functools.partial(fill_kernel, early, 0),
        (SMEM,) * 3 + (VMEM,) * (1 + len(early)), (VMEM,),
        [hold(state)],
        aliases={3: 0},
        micros=2,
    )(tile, live, weight, flow_in, *(arrived[turn] for turn in early))
    filled, rows, tail, head = call(
        functools.partial(last_fill_kernel, late, len(totals)),
        (SMEM,) * 3 + (VMEM,) * (1 + len(late)) + (pl.ANY,) * len(totals), (VMEM,) * 4,
        [hold(state), hold((4, *line)), hold(edge), hold(edge)],
        aliases={3: 0},
        micros=4,
    )(tile, live, weight, partly, *(arrived[turn] for turn in late), *totals)
    before = moved(tail, "span", 1)
    after = moved(head, "span", -1)
    behind = moved(rows[3], "stream", 1)
    ahead = moved(rows[0], "stream", -1)
    local, flux = call(
        scan_kernel,
        (SMEM, SMEM) + (VMEM,) * 7, (VMEM,) * 2,
        [hold(state), hold(line)],
        [pltpu.VMEM(edge, F32)] * 3,
        aliases={2: 0},
        micros=12,
    )(char_scale, span_ratio, filled, ratio, speed_in, tail, head, before, after)
    flux, first_slope, last_slope = call(
        edge_kernel, (VMEM,) * 6, (VMEM,) * 3, [jax.ShapeDtypeStruct(line, F32)] * 3
    )(flux, total, last, rows, behind, ahead)
    fluxes = [moved(flux, "stream", d) for d in range(1, sections)]
    (done,) = call(
        combine_kernel,
        (VMEM,) * (2 * sections + 1), (HBM,),
        [jax.ShapeDtypeStruct(state, F32)],
        [pltpu.VMEM(state, F32), pltpu.VMEM(line, F32), pltpu.SemaphoreType.DMA],
        limit=14 << 20,
        micros=5,
    )(local, growth, first_slope, last_slope, *fluxes, *totals)
    return jnp.transpose(done, (0, 2, 1, 3))[None]


def solution(mesh):
    return jax.shard_map(
        on_device,
        mesh=mesh,
        in_specs=(
            P("block", "stream", None, None, "span"),
            P("block", "stream", None, "span"),
            P(),
            P(),
            P("block", "span", "stream", None, None),
            P("block", "span", "stream", None, None),
            P("block", "span", "stream", None, None),
            P("block", "span", "stream", None, None),
        ),
        out_specs=P("block", "stream", None, None, "span"),
        check_vma=False,
    )
```

```python
import functools
import jax
import jax.numpy as jnp
from jax import lax
from jax.experimental import pallas as pl
from jax.experimental.pallas import tpu as pltpu
from jax.sharding import PartitionSpec as P


LANES = 128
SUB = 8
STEPS = 16
F32 = jnp.float32


def space(kind):
    return pl.BlockSpec(memory_space=kind)


SMEM, VMEM, HBM = pltpu.SMEM, pltpu.VMEM, pltpu.HBM

RING = ("block", "span")


def limited(first, second):
    return jnp.maximum(
        jnp.minimum(second, jnp.maximum(first, 0.0)), jnp.minimum(first, 0.0)
    )


def call(kernel, ins, outs, out_shape, scratch=(), aliases=None, limit=8 << 20, micros=0):
    return pl.pallas_call(
        kernel,
        out_shape=out_shape,
        in_specs=[space(k) for k in ins],
        out_specs=[space(k) for k in outs],
        scratch_shapes=list(scratch),
        input_output_aliases=aliases or {},
        compiler_params=pltpu.CompilerParams(vmem_limit_bytes=limit),
        cost_estimate=pl.CostEstimate(flops=0, transcendentals=0, bytes_accessed=int(micros * 3.0e6)),
    )


def present(ref, axis, distance):
    source = lax.axis_index(axis) - distance
    inside = (source >= 0) & (source < lax.axis_size(axis))
    return ref[...] * jnp.where(inside, 1.0, 0.0)


def gather_kernel(turns, send_ref, flow_ref, *refs):
    *out_refs, sem = refs
    _, capacity, _ = out_refs[0].shape
    rows_y = flow_ref.shape[2]
    place = lax.axis_index(RING)

    def copy_of(out_ref, turn, slot):
        tile = send_ref[place ^ turn, slot]
        return pltpu.make_async_copy(
            flow_ref.at[tile // rows_y, :, pl.ds(tile % rows_y, 1), :],
            out_ref.at[:, pl.ds(slot, 1), :],
            sem,
        )

    for out_ref, turn in zip(out_refs, turns):

        @pl.loop(0, capacity)
        def _(slot):
            copy_of(out_ref, turn, slot).start()

    for out_ref, turn in zip(out_refs, turns):

        @pl.loop(0, capacity)
        def _(slot):
            copy_of(out_ref, turn, slot).wait()


def growth_kernel(scale_ref, flow_hbm, speed_hbm, flow_ref, speed_ref, ratio_ref, growth_ref, total_ref, last_ref, sem):
    width_x, components, rows_y, width_z = growth_ref.shape
    speed_copy = pltpu.make_async_copy(speed_hbm, speed_ref, sem.at[0])
    flow_copy = pltpu.make_async_copy(flow_hbm, flow_ref, sem.at[1])
    speed_copy.start()
    flow_copy.start()
    speed_copy.wait()
    halves = rows_y // SUB

    @pl.loop(0, components * halves)
    def _(group):
        v = group // halves
        y = pl.ds(pl.multiple_of((group % halves) * SUB, SUB), SUB)
        scale = 100.0 * scale_ref[v]

        def step(x, run):
            rate = scale * speed_ref[x, y, :]
            ratio = 1.0 / (1.0 + rate)
            grown = ratio * run
            ratio_ref[x, v, y, :] = ratio
            growth_ref[x, v, y, :] = grown
            return rate * grown

        total_ref[v, y, :] = lax.fori_loop(0, width_x, step, jnp.ones((SUB, width_z), F32), unroll=4)
        last_ref[v, y, :] = scale * speed_ref[width_x - 1, y, :] * ratio_ref[width_x - 1, v, y, :]

    flow_copy.wait()


def fill_kernel(turns, extra, tile_ref, live_ref, weight_ref, flow_ref, *refs):
    arrived_refs = refs[: len(turns)]
    filled_ref = refs[len(turns) + extra]
    rows_y = filled_ref.shape[2]
    components, capacity, _ = arrived_refs[0].shape
    place = lax.axis_index(RING)

    for turn, arrived_ref in zip(turns, arrived_refs):
        peer = place ^ turn

        @pl.loop(0, capacity)
        def _(slot):
            @pl.when(live_ref[peer, slot] == 1)
            def _():
                tile = tile_ref[peer, slot]
                weight = weight_ref[peer, slot]
                x = tile // rows_y
                y = pl.ds(tile % rows_y, 1)
                for v in range(components):
                    old = filled_ref[x, v, y, :]
                    new = arrived_ref[v, pl.ds(slot, 1), :]
                    filled_ref[x, v, y, :] = (1.0 - weight) * old + weight * new


def last_fill_kernel(turns, extra, *refs):
    *fill_refs, rows_ref, tail_ref, head_ref = refs
    fill_kernel(turns, extra, *fill_refs)
    filled_ref = fill_refs[-1]
    width_x, components, rows_y, width_z = filled_ref.shape
    lane = lax.broadcasted_iota(jnp.int32, (rows_y, LANES), 1)
    for v in range(components):

        def pack(x, packed):
            tail, head = packed
            here = lane // 2 == x
            tail = jnp.where(
                here, pltpu.roll(filled_ref[x, v, :, width_z - LANES :], 2 * x + 2, 1), tail
            )
            head = jnp.where(here, pltpu.roll(filled_ref[x, v, :, :LANES], 2 * x + 1, 1), head)
            return tail, head

        zero = jnp.zeros((rows_y, LANES), F32)
        tail_ref[v], head_ref[v] = lax.fori_loop(0, width_x, pack, (zero, zero), unroll=32)
        for spot, x in enumerate((0, 1, width_x - 2, width_x - 1)):
            rows_ref[spot, v] = filled_ref[x, v]


def scan_kernel(
    lowest, scale_ref, span_ref, filled_ref, ratio_ref, speed_ref, tail_ref, head_ref, before_ref, after_ref,
    local_ref, out_ref, prior_ref, face_ref, diff_ref
):
    width_x, _, rows_y, width_z = local_ref.shape
    components = out_ref.shape[0]
    halves = rows_y // SUB
    blocks = width_z // LANES
    before = present(before_ref, "span", 1)
    after = present(after_ref, "span", -1)
    tail = tail_ref[...]
    head = head_ref[...]
    outer = 0.5 * (before - pltpu.roll(before, 1, 2))
    inner = 0.5 * (head - before)
    prior_ref[...] = before
    face_ref[...] = before + limited(outer, inner)
    diff_ref[...] = 0.5 * (after - tail)
    lane = lax.broadcasted_iota(jnp.int32, (SUB, LANES), 1)
    first = lane == 0
    final = lane == LANES - 1

    @pl.loop(0, components * halves)
    def _(group):
        v = lowest + group // halves
        y = pl.ds(pl.multiple_of((group % halves) * SUB, SUB), SUB)
        scale_z = 100.0 * (scale_ref[v] * span_ref[v])
        prior = prior_ref[v, y, :]
        face = face_ref[v, y, :]
        diff = diff_ref[v, y, :]
        every = range(blocks)

        def load(ref, *at):
            return [ref[(*at, y, slice(b * LANES, (b + 1) * LANES))] for b in every]

        def right(values, edge):
            moved_right = [edge] + [pltpu.roll(u, 1, 1) for u in values]
            return [jnp.where(first, moved_right[b], moved_right[b + 1]) for b in every]

        def left(values, edge):
            moved_left = [pltpu.roll(u, LANES - 1, 1) for u in values] + [edge]
            return [jnp.where(final, moved_left[b + 1], moved_left[b]) for b in every]

        def steps(k, carry):
            here, rise, inflow = carry
            start = k * STEPS
            span = range(STEPS)
            turn = [LANES - 2 * (start + i) - 1 for i in span]
            rows = [here] + [load(filled_ref, start + i, v) for i in range(1, STEPS)]
            rows.append(load(filled_ref, jnp.minimum(start + STEPS, width_x - 1), v))
            back = [right(rows[i], pltpu.roll(prior, turn[i], 1)) for i in span]
            fall = [[0.5 * (rows[i][b] - back[i][b]) for b in every] for i in span]
            grow = [left(fall[i], pltpu.roll(diff, turn[i] - 1, 1)) for i in span]
            faces = [[rows[i][b] + limited(fall[i][b], grow[i][b]) for b in every] for i in span]
            shifted = [right(faces[i], pltpu.roll(face, turn[i], 1)) for i in span]
            known = [[rows[i][b] + scale_z * (shifted[i][b] - faces[i][b]) for b in every] for i in span]
            outs = []
            for i in span:
                u = rows[i]
                ratio = load(ratio_ref, start + i, v)
                rise_later = [0.5 * (rows[i + 1][b] - u[b]) for b in every]
                slope = [limited(rise[b], rise_later[b]) for b in every]
                total = [inflow[b] + (known[i][b] + slope[b]) for b in every]
                value = [ratio[b] * total[b] for b in every]
                inflow = [total[b] - value[b] for b in every]
                rise = rise_later
                outs.append([value[b] - slope[b] for b in every])
            for i in span:
                for b in every:
                    local_ref[start + i, v, y, slice(b * LANES, (b + 1) * LANES)] = outs[i][b]
            return rows[STEPS], rise, inflow

        zeros = [jnp.zeros((SUB, LANES), F32)] * blocks
        _, _, flux = lax.fori_loop(0, width_x // STEPS, steps, (load(filled_ref, 0, v), zeros, zeros))
        for b in every:
            out_ref[v - lowest, y, slice(b * LANES, (b + 1) * LANES)] = flux[b]


def edge_kernel(
    lowest, flux_ref, total_ref, last_ref, rows_ref, behind_ref, ahead_ref, flux_out, first_out, last_out
):
    part = pl.ds(lowest, flux_ref.shape[0])
    behind = present(behind_ref.at[part], "stream", 1)
    ahead = present(ahead_ref.at[part], "stream", -1)
    row = [rows_ref[k, part] for k in range(4)]
    slope_first = limited(0.5 * (row[0] - behind), 0.5 * (row[1] - row[0]))
    slope_last = limited(0.5 * (row[3] - row[2]), 0.5 * (ahead - row[3]))
    kept = last_ref[part] * slope_last
    flux_out[...] = flux_ref[...] + total_ref[part] * slope_first + kept
    first_out[...] = slope_first
    last_out[...] = kept


def combine_kernel(lowest, begun, local_ref, growth_ref, first_ref, last_ref, *refs):
    *line_refs, out_hbm, done_ref, inflow_ref, sem = refs[begun:]
    width_x, _, _, _ = local_ref.shape
    components = first_ref.shape[0]
    count = (len(line_refs) + 1) // 2
    flux_refs, total_refs = line_refs[:count], line_refs[count:]
    inflow = first_ref[...]
    product = None
    for distance in range(1, count + 1):
        flux = present(flux_refs[distance - 1], "stream", distance)
        inflow = inflow + (flux if product is None else product * flux)
        if distance < count:
            total = total_refs[distance - 1][pl.ds(lowest, components)]
            product = total if product is None else product * total
    inflow_ref[...] = inflow
    part = 4

    def copy_of(k):
        rows = pl.ds(k * part, part)
        return pltpu.make_async_copy(
            done_ref.at[rows], out_hbm.at[rows, pl.ds(lowest, components)], sem
        )

    @pl.loop(0, width_x // part)
    def _(k):
        for v in range(components):
            inflow = inflow_ref[v]
            for i in range(part):
                x = k * part + i
                done_ref[x, v] = local_ref[x, lowest + v] + growth_ref[x, lowest + v] * inflow

        @pl.when(k == 0)
        def _():
            done_ref[0] = done_ref[0] - first_ref[...]

        @pl.when(k == width_x // part - 1)
        def _():
            done_ref[width_x - 1] = done_ref[width_x - 1] - last_ref[...]

        copy_of(k).start()

    @pl.loop(0, width_x // part)
    def _(k):
        copy_of(k).wait()


def moved(value, axis, distance):
    count = lax.axis_size(axis)
    return lax.ppermute(value, axis, [(i, (i + distance) % count) for i in range(count)])


def on_device(
    flow_state, wave_speed, char_scale, span_ratio, send_tile, recv_tile, recv_live, interp_weight
):
    _, width_x, rows_y, components, width_z = flow_state.shape
    peers, capacity = send_tile.shape[-2:]
    sections = lax.axis_size("stream")
    flow = pltpu.with_memory_space_constraint(jnp.transpose(flow_state[0], (0, 2, 1, 3)), HBM)
    speed = wave_speed[0]
    state = (width_x, components, rows_y, width_z)
    line = (components, rows_y, width_z)
    edge = (components, rows_y, LANES)
    hold = lambda shape: pltpu.VMEM(shape, F32)
    send, tile, live, weight = (
        t.reshape(peers, capacity) for t in (send_tile, recv_tile, recv_live, interp_weight)
    )
    assert peers & (peers - 1) == 0

    order = sorted(range(1, peers), key=lambda turn: (turn == 1, turn & 1, turn))
    early, late = order[: peers // 2 - 1], order[peers // 2 - 1 :] + [0]
    arrived = {}
    for turns in (early, late):
        outgoing = call(
            functools.partial(gather_kernel, turns),
            (SMEM, HBM), (VMEM,) * len(turns),
            [jax.ShapeDtypeStruct((components, capacity, width_z), F32)] * len(turns),
            [pltpu.SemaphoreType.DMA],
            micros=2,
        )(send, flow)
        for turn, tiles in zip(turns, outgoing):
            route = [(i, i ^ turn) for i in range(peers)]
            arrived[turn] = lax.ppermute(tiles, RING, route) if turn else tiles
    flow_in, speed_in, ratio, growth, total, last = call(
        growth_kernel,
        (SMEM, HBM, HBM), (VMEM,) * 6,
        [hold(state), hold(speed.shape), hold(state), hold(state), hold(line), hold(line)],
        [pltpu.SemaphoreType.DMA((2,))],
        micros=6,
    )(char_scale, flow, speed)
    totals = [moved(total, "stream", d) for d in range(1, sections - 1)]
    (partly,) = call(
        functools.partial(fill_kernel, early, 0),
        (SMEM,) * 3 + (VMEM,) * (1 + len(early)), (VMEM,),
        [hold(state)],
        aliases={3: 0},
        micros=2,
    )(tile, live, weight, flow_in, *(arrived[turn] for turn in early))
    filled, rows, tail, head = call(
        functools.partial(last_fill_kernel, late, 0),
        (SMEM,) * 3 + (VMEM,) * (1 + len(late)), (VMEM,) * 4,
        [hold(state), hold((4, *line)), hold(edge), hold(edge)],
        aliases={3: 0},
        micros=4,
    )(tile, live, weight, partly, *(arrived[turn] for turn in late))
    before = moved(tail, "span", 1)
    after = moved(head, "span", -1)
    behind = moved(rows[3], "stream", 1)
    ahead = moved(rows[0], "stream", -1)
    split = (components + 1) // 2
    state_now, parts = filled, []
    for lowest, size in ((0, split), (split, components - split)):
        some = (size, rows_y, width_z)
        state_now, flux = call(
            functools.partial(scan_kernel, lowest),
            (SMEM, SMEM) + (VMEM,) * 7, (VMEM,) * 2,
            [hold(state), hold(some)],
            [pltpu.VMEM(edge, F32)] * 3,
            aliases={2: 0},
            micros=3 * size,
        )(char_scale, span_ratio, state_now, ratio, speed_in, tail, head, before, after)
        flux, first_slope, last_slope = call(
            functools.partial(edge_kernel, lowest),
            (VMEM,) * 6, (VMEM,) * 3,
            [jax.ShapeDtypeStruct(some, F32)] * 3,
        )(flux, total, last, rows, behind, ahead)
        fluxes = [moved(flux, "stream", d) for d in range(1, sections)]
        parts.append((lowest, some, first_slope, last_slope, fluxes))
    begun = ()
    for lowest, some, first_slope, last_slope, fluxes in parts:
        begun = call(
            functools.partial(combine_kernel, lowest, len(begun)),
            (VMEM,) * 4 + (HBM,) * len(begun) + (VMEM,) * (2 * sections - 3), (HBM,),
            [jax.ShapeDtypeStruct(state, F32)],
            [
                pltpu.VMEM((width_x, *some), F32),
                pltpu.VMEM(some, F32),
                pltpu.SemaphoreType.DMA,
            ],
            aliases={4: 0} if begun else None,
            limit=10 << 20,
            micros=some[0],
        )(state_now, growth, first_slope, last_slope, *begun, *fluxes, *totals)
    (done,) = begun
    return jnp.transpose(done, (0, 2, 1, 3))[None]


def solution(mesh):
    return jax.shard_map(
        on_device,
        mesh=mesh,
        in_specs=(
            P("block", "stream", None, None, "span"),
            P("block", "stream", None, "span"),
            P(),
            P(),
            P("block", "span", "stream", None, None),
            P("block", "span", "stream", None, None),
            P("block", "span", "stream", None, None),
            P("block", "span", "stream", None, None),
        ),
        out_specs=P("block", "stream", None, None, "span"),
        check_vma=False,
    )
```

```python
import functools
import jax
import jax.numpy as jnp
from jax import lax
from jax.experimental import pallas as pl
from jax.experimental.pallas import tpu as pltpu
from jax.sharding import PartitionSpec as P


LANES = 128
SUB = 8
STEPS = 16
F32 = jnp.float32


def space(kind):
    return pl.BlockSpec(memory_space=kind)


SMEM, VMEM, HBM = pltpu.SMEM, pltpu.VMEM, pltpu.HBM

RING = ("block", "span")


def limited(first, second):
    return jnp.maximum(
        jnp.minimum(second, jnp.maximum(first, 0.0)), jnp.minimum(first, 0.0)
    )


def call(kernel, ins, outs, out_shape, scratch=(), aliases=None, limit=8 << 20, micros=0):
    return pl.pallas_call(
        kernel,
        out_shape=out_shape,
        in_specs=[space(k) for k in ins],
        out_specs=[space(k) for k in outs],
        scratch_shapes=list(scratch),
        input_output_aliases=aliases or {},
        compiler_params=pltpu.CompilerParams(vmem_limit_bytes=limit),
        cost_estimate=pl.CostEstimate(flops=0, transcendentals=0, bytes_accessed=int(micros * 3.0e6)),
    )


def present(ref, axis, distance):
    source = lax.axis_index(axis) - distance
    inside = (source >= 0) & (source < lax.axis_size(axis))
    return ref[...] * jnp.where(inside, 1.0, 0.0)


def gather_kernel(turns, send_ref, flow_ref, *refs):
    *out_refs, sem = refs
    _, capacity, _ = out_refs[0].shape
    rows_y = flow_ref.shape[2]
    place = lax.axis_index(RING)

    for k, (out_ref, turn) in enumerate(zip(out_refs, turns)):
        for slot in range(capacity):
            tile = send_ref[place ^ turn, slot]
            pltpu.make_async_copy(
                flow_ref.at[tile // rows_y, :, pl.ds(tile % rows_y, 1), :],
                out_ref.at[:, slot : slot + 1, :],
                sem.at[k],
            ).start()
    for k, out_ref in enumerate(out_refs):
        pltpu.make_async_copy(out_ref, out_ref, sem.at[k]).wait()


def growth_kernel(scale_ref, flow_hbm, speed_hbm, flow_ref, speed_ref, ratio_ref, total_ref, last_ref, sem):
    width_x, components, rows_y, width_z = ratio_ref.shape
    speed_copy = pltpu.make_async_copy(speed_hbm, speed_ref, sem.at[0])
    flow_copy = pltpu.make_async_copy(flow_hbm, flow_ref, sem.at[1])
    speed_copy.start()
    flow_copy.start()
    speed_copy.wait()
    halves = rows_y // SUB

    @pl.loop(0, components * halves)
    def _(group):
        v = group // halves
        y = pl.ds(pl.multiple_of((group % halves) * SUB, SUB), SUB)
        scale = 100.0 * scale_ref[v]

        def step(k, run):
            speeds = [speed_ref[k * STEPS + i, y, :] for i in range(STEPS)]
            ratios = [1.0 / (1.0 + scale * speed) for speed in speeds]
            for ratio in ratios:
                run = run - ratio * run
            for i in range(STEPS):
                ratio_ref[k * STEPS + i, v, y, :] = ratios[i]
            return run

        start = jnp.ones((SUB, width_z), F32)
        total_ref[v, y, :] = lax.fori_loop(0, width_x // STEPS, step, start)
        last_ref[v, y, :] = 1.0 - ratio_ref[width_x - 1, v, y, :]

    flow_copy.wait()


def fill_kernel(turns, tile_ref, live_ref, weight_ref, flow_ref, *refs):
    arrived_refs = refs[: len(turns)]
    filled_ref = refs[len(turns)]
    rows_y = filled_ref.shape[2]
    components, capacity, _ = arrived_refs[0].shape
    place = lax.axis_index(RING)

    for turn, arrived_ref in zip(turns, arrived_refs):
        peer = place ^ turn

        count = live_ref[peer, 0]
        for slot in range(1, capacity):
            count = count + live_ref[peer, slot]

        @pl.loop(0, (count + 1) // 2)
        def _(pair):
            slots = [2 * pair, 2 * pair + 1]
            tiles = [tile_ref[peer, slot] for slot in slots]
            spots = [(tile // rows_y, pl.ds(tile % rows_y, 1)) for tile in tiles]
            weights = [
                jnp.where(live_ref[peer, slot] == 1, weight_ref[peer, slot], 0.0) for slot in slots
            ]
            mixed = [
                (1.0 - weight) * filled_ref[x, v, y, :] + weight * arrived_ref[v, pl.ds(slot, 1), :]
                for v in range(components)
                for slot, (x, y), weight in zip(slots, spots, weights)
            ]
            for v in range(components):
                for i, (x, y) in enumerate(spots):
                    filled_ref[x, v, y, :] = mixed[2 * v + i]


def last_fill_kernel(turns, total_ref, *refs):
    *fill_refs, rows_ref, up_ref, down_ref, tail_ref, head_ref = refs
    fill_kernel(turns, *fill_refs)
    filled_ref = fill_refs[-1]
    width_x, components, rows_y, width_z = filled_ref.shape
    up_ref[0] = filled_ref[width_x - 1]
    up_ref[1] = total_ref[...]
    down_ref[0] = filled_ref[0]
    down_ref[1] = total_ref[...]
    lane = lax.broadcasted_iota(jnp.int32, (rows_y, LANES), 1)
    for v in range(components):

        def pack(x, packed):
            tail, head = packed
            here = lane // 2 == x
            tail = jnp.where(
                here, pltpu.roll(filled_ref[x, v, :, width_z - LANES :], 2 * x + 2, 1), tail
            )
            head = jnp.where(here, pltpu.roll(filled_ref[x, v, :, :LANES], 2 * x + 1, 1), head)
            return tail, head

        zero = jnp.zeros((rows_y, LANES), F32)
        tail_ref[v], head_ref[v] = lax.fori_loop(0, width_x, pack, (zero, zero), unroll=32)
        for spot, x in enumerate((0, 1, width_x - 2, width_x - 1)):
            rows_ref[spot, v] = filled_ref[x, v]


def scan_kernel(
    lowest, scale_ref, span_ref, filled_ref, ratio_ref, speed_ref, tail_ref, head_ref, before_ref, after_ref,
    local_ref, out_ref, prior_ref, face_ref, diff_ref
):
    width_x, _, rows_y, width_z = local_ref.shape
    components = out_ref.shape[0]
    halves = rows_y // SUB
    blocks = width_z // LANES
    before = present(before_ref, "span", 1)
    after = present(after_ref, "span", -1)
    tail = tail_ref[...]
    head = head_ref[...]
    outer = 0.5 * (before - pltpu.roll(before, 1, 2))
    inner = 0.5 * (head - before)
    prior_ref[...] = before
    face_ref[...] = before + limited(outer, inner)
    diff_ref[...] = 0.5 * (after - tail)
    lane = lax.broadcasted_iota(jnp.int32, (SUB, LANES), 1)
    first = lane == 0
    final = lane == LANES - 1

    @pl.loop(0, components * halves)
    def _(group):
        v = lowest + group // halves
        y = pl.ds(pl.multiple_of((group % halves) * SUB, SUB), SUB)
        scale_z = 100.0 * (scale_ref[v] * span_ref[v])
        prior = prior_ref[v, y, :]
        face = face_ref[v, y, :]
        diff = diff_ref[v, y, :]
        every = range(blocks)

        def load(ref, *at):
            return [ref[(*at, y, slice(b * LANES, (b + 1) * LANES))] for b in every]

        def right(values, edge):
            moved_right = [edge] + [pltpu.roll(u, 1, 1) for u in values]
            return [jnp.where(first, moved_right[b], moved_right[b + 1]) for b in every]

        def left(values, edge):
            moved_left = [pltpu.roll(u, LANES - 1, 1) for u in values] + [edge]
            return [jnp.where(final, moved_left[b + 1], moved_left[b]) for b in every]

        def steps(k, carry):
            here, rise, inflow = carry
            start = k * STEPS
            span = range(STEPS)
            turn = [LANES - 2 * (start + i) - 1 for i in span]
            rows = [here] + [load(filled_ref, start + i, v) for i in range(1, STEPS)]
            rows.append(load(filled_ref, jnp.minimum(start + STEPS, width_x - 1), v))
            back = [right(rows[i], pltpu.roll(prior, turn[i], 1)) for i in span]
            fall = [[0.5 * (rows[i][b] - back[i][b]) for b in every] for i in span]
            grow = [left(fall[i], pltpu.roll(diff, turn[i] - 1, 1)) for i in span]
            faces = [[rows[i][b] + limited(fall[i][b], grow[i][b]) for b in every] for i in span]
            shifted = [right(faces[i], pltpu.roll(face, turn[i], 1)) for i in span]
            known = [[rows[i][b] + scale_z * (shifted[i][b] - faces[i][b]) for b in every] for i in span]
            outs = []
            for i in span:
                u = rows[i]
                ratio = load(ratio_ref, start + i, v)
                rise_later = [0.5 * (rows[i + 1][b] - u[b]) for b in every]
                slope = [limited(rise[b], rise_later[b]) for b in every]
                total = [inflow[b] + (known[i][b] + slope[b]) for b in every]
                value = [ratio[b] * total[b] for b in every]
                inflow = [total[b] - value[b] for b in every]
                rise = rise_later
                outs.append([value[b] - slope[b] for b in every])
            for i in span:
                for b in every:
                    local_ref[start + i, v, y, slice(b * LANES, (b + 1) * LANES)] = outs[i][b]
            return rows[STEPS], rise, inflow

        zeros = [jnp.zeros((SUB, LANES), F32)] * blocks
        _, _, flux = lax.fori_loop(0, width_x // STEPS, steps, (load(filled_ref, 0, v), zeros, zeros))
        for b in every:
            out_ref[v - lowest, y, slice(b * LANES, (b + 1) * LANES)] = flux[b]


def edge_kernel(
    lowest, flux_ref, total_ref, last_ref, rows_ref, behind_ref, ahead_ref,
    flux_out, beyond_out, first_out, last_out,
):
    part = pl.ds(lowest, flux_ref.shape[0])
    behind = present(behind_ref.at[0, part], "stream", 1)
    ahead = present(ahead_ref.at[0, part], "stream", -1)
    row = [rows_ref[k, part] for k in range(4)]
    slope_first = limited(0.5 * (row[0] - behind), 0.5 * (row[1] - row[0]))
    slope_last = limited(0.5 * (row[3] - row[2]), 0.5 * (ahead - row[3]))
    kept = last_ref[part] * slope_last
    flux = flux_ref[...] + total_ref[part] * slope_first + kept
    flux_out[...] = flux
    beyond_out[...] = ahead_ref[1, part] * flux
    first_out[...] = slope_first
    last_out[...] = kept


def combine_kernel(lowest, begun, local_ref, ratio_ref, first_ref, last_ref, behind_ref, *refs):
    *flux_refs, out_hbm, done_ref, inflow_ref, sem = refs[begun:]
    width_x, _, _, _ = local_ref.shape
    components = first_ref.shape[0]
    flux = [present(ref, "stream", i + 1) for i, ref in enumerate(flux_refs)]
    beyond = sum(flux[2:], flux[1]) if len(flux) > 1 else 0.0
    inflow_ref[...] = first_ref[...] + flux[0] + behind_ref[1, pl.ds(lowest, components)] * beyond
    part = 4

    def copy_of(k):
        rows = pl.ds(k * part, part)
        return pltpu.make_async_copy(
            done_ref.at[rows], out_hbm.at[rows, pl.ds(lowest, components)], sem
        )

    @pl.loop(0, width_x // part)
    def _(k):
        for v in range(components):
            inflow = inflow_ref[v]
            outs = []
            for i in range(part):
                gain = ratio_ref[k * part + i, lowest + v] * inflow
                outs.append(local_ref[k * part + i, lowest + v] + gain)
                inflow = inflow - gain
            for i in range(part):
                done_ref[k * part + i, v] = outs[i]
            inflow_ref[v] = inflow

        @pl.when(k == 0)
        def _():
            done_ref[0] = done_ref[0] - first_ref[...]

        @pl.when(k == width_x // part - 1)
        def _():
            done_ref[width_x - 1] = done_ref[width_x - 1] - last_ref[...]

        copy_of(k).start()

    @pl.loop(0, width_x // part)
    def _(k):
        copy_of(k).wait()


def moved(value, axis, distance):
    count = lax.axis_size(axis)
    return lax.ppermute(value, axis, [(i, (i + distance) % count) for i in range(count)])


def on_device(
    flow_state, wave_speed, char_scale, span_ratio, send_tile, recv_tile, recv_live, interp_weight
):
    _, width_x, rows_y, components, width_z = flow_state.shape
    peers, capacity = send_tile.shape[-2:]
    sections = lax.axis_size("stream")
    flow = pltpu.with_memory_space_constraint(jnp.transpose(flow_state[0], (0, 2, 1, 3)), HBM)
    speed = wave_speed[0]
    state = (width_x, components, rows_y, width_z)
    line = (components, rows_y, width_z)
    edge = (components, rows_y, LANES)
    hold = lambda shape: pltpu.VMEM(shape, F32)
    send, tile, live, weight = (
        t.reshape(peers, capacity) for t in (send_tile, recv_tile, recv_live, interp_weight)
    )
    assert peers & (peers - 1) == 0

    order = sorted(range(1, peers), key=lambda turn: (turn == 1, turn & 1, turn))
    early, late = order[: peers // 2 - 1], order[peers // 2 - 1 :] + [0]
    arrived = {}
    for turns in (early, late):
        outgoing = call(
            functools.partial(gather_kernel, turns),
            (SMEM, HBM), (VMEM,) * len(turns),
            [jax.ShapeDtypeStruct((components, capacity, width_z), F32)] * len(turns),
            [pltpu.SemaphoreType.DMA((len(turns),))],
            micros=2,
        )(send, flow)
        for turn, tiles in zip(turns, outgoing):
            route = [(i, i ^ turn) for i in range(peers)]
            arrived[turn] = lax.ppermute(tiles, RING, route) if turn else tiles
    flow_in, speed_in, ratio, total, last = call(
        growth_kernel,
        (SMEM, HBM, HBM), (VMEM,) * 5,
        [hold(state), hold(speed.shape), hold(state), hold(line), hold(line)],
        [pltpu.SemaphoreType.DMA((2,))],
        micros=6,
    )(char_scale, flow, speed)
    (partly,) = call(
        functools.partial(fill_kernel, early),
        (SMEM,) * 3 + (VMEM,) * (1 + len(early)), (VMEM,),
        [hold(state)],
        aliases={3: 0},
        micros=2,
    )(tile, live, weight, flow_in, *(arrived[turn] for turn in early))
    filled, rows, up, down, tail, head = call(
        functools.partial(last_fill_kernel, late),
        (VMEM,) + (SMEM,) * 3 + (VMEM,) * (1 + len(late)), (VMEM,) * 6,
        [hold(state), hold((4, *line)), hold((2, *line)), hold((2, *line)), hold(edge), hold(edge)],
        aliases={4: 0},
        micros=4,
    )(total, tile, live, weight, partly, *(arrived[turn] for turn in late))
    behind = moved(up, "stream", 1)
    ahead = moved(down, "stream", -1)
    before = moved(tail, "span", 1)
    after = moved(head, "span", -1)
    assert sections <= 4
    split = (components + 1) // 2
    state_now, parts = filled, []
    for lowest, size in ((0, split), (split, components - split)):
        some = (size, rows_y, width_z)
        state_now, flux = call(
            functools.partial(scan_kernel, lowest),
            (SMEM, SMEM) + (VMEM,) * 7, (VMEM,) * 2,
            [hold(state), hold(some)],
            [pltpu.VMEM(edge, F32)] * 3,
            aliases={2: 0},
            micros=3 * size,
        )(char_scale, span_ratio, state_now, ratio, speed_in, tail, head, before, after)
        flux, beyond, first_slope, last_slope = call(
            functools.partial(edge_kernel, lowest),
            (VMEM,) * 6, (VMEM,) * 4,
            [jax.ShapeDtypeStruct(some, F32)] * 4,
        )(flux, total, last, rows, behind, ahead)
        fluxes = [moved(flux if d < 3 else beyond, "stream", d) for d in range(1, sections)]
        parts.append((lowest, some, first_slope, last_slope, fluxes))
    begun = ()
    for lowest, some, first_slope, last_slope, fluxes in parts:
        begun = call(
            functools.partial(combine_kernel, lowest, len(begun)),
            (VMEM,) * 5 + (HBM,) * len(begun) + (VMEM,) * (sections - 1), (HBM,),
            [jax.ShapeDtypeStruct(state, F32)],
            [
                pltpu.VMEM((width_x, *some), F32),
                pltpu.VMEM(some, F32),
                pltpu.SemaphoreType.DMA,
            ],
            aliases={5: 0} if begun else None,
            limit=10 << 20,
            micros=some[0],
        )(state_now, ratio, first_slope, last_slope, behind, *begun, *fluxes)
    (done,) = begun
    return jnp.transpose(done, (0, 2, 1, 3))[None]


def solution(mesh):
    return jax.shard_map(
        on_device,
        mesh=mesh,
        in_specs=(
            P("block", "stream", None, None, "span"),
            P("block", "stream", None, "span"),
            P(),
            P(),
            P("block", "span", "stream", None, None),
            P("block", "span", "stream", None, None),
            P("block", "span", "stream", None, None),
            P("block", "span", "stream", None, None),
        ),
        out_specs=P("block", "stream", None, None, "span"),
        check_vma=False,
    )
```

```python
import functools
import jax
import jax.numpy as jnp
from jax import lax
from jax.experimental import pallas as pl
from jax.experimental.pallas import tpu as pltpu
from jax.sharding import PartitionSpec as P


LANES = 128
SUB = 8
STEPS = 16
F32 = jnp.float32


def space(kind):
    return pl.BlockSpec(memory_space=kind)


SMEM, VMEM, HBM = pltpu.SMEM, pltpu.VMEM, pltpu.HBM

RING = ("block", "span")


def limited(first, second):
    return jnp.maximum(
        jnp.minimum(second, jnp.maximum(first, 0.0)), jnp.minimum(first, 0.0)
    )


def call(kernel, ins, outs, out_shape, scratch=(), aliases=None, limit=8 << 20, micros=0):
    return pl.pallas_call(
        kernel,
        out_shape=out_shape,
        in_specs=[space(k) for k in ins],
        out_specs=[space(k) for k in outs],
        scratch_shapes=list(scratch),
        input_output_aliases=aliases or {},
        compiler_params=pltpu.CompilerParams(vmem_limit_bytes=limit),
        cost_estimate=pl.CostEstimate(flops=0, transcendentals=0, bytes_accessed=int(micros * 3.0e6)),
    )


def inside(axis, distance):
    source = lax.axis_index(axis) - distance
    return jnp.where((source >= 0) & (source < lax.axis_size(axis)), 1.0, 0.0)


def present(ref, axis, distance):
    return ref[...] * inside(axis, distance)


def beside(side, even_ref, odd_ref):
    odd = lax.axis_index("stream") % 2
    return jnp.where(odd == (1 if side == "behind" else 0), even_ref[...], odd_ref[...])


def gather_kernel(turns, send_ref, flow_ref, *refs):
    *out_refs, sem = refs
    _, capacity, _ = out_refs[0].shape
    rows_y = flow_ref.shape[2]
    place = lax.axis_index(RING)

    for k, (out_ref, turn) in enumerate(zip(out_refs, turns)):
        for slot in range(capacity):
            tile = send_ref[place ^ turn, slot]
            pltpu.make_async_copy(
                flow_ref.at[tile // rows_y, :, pl.ds(tile % rows_y, 1), :],
                out_ref.at[:, slot : slot + 1, :],
                sem.at[k],
            ).start()
    for k, out_ref in enumerate(out_refs):
        pltpu.make_async_copy(out_ref, out_ref, sem.at[k]).wait()


def growth_kernel(scale_ref, flow_hbm, speed_hbm, flow_ref, speed_ref, ratio_ref, total_ref, last_ref, sem):
    width_x, components, rows_y, width_z = ratio_ref.shape
    speed_copy = pltpu.make_async_copy(speed_hbm, speed_ref, sem.at[0])
    flow_copy = pltpu.make_async_copy(flow_hbm, flow_ref, sem.at[1])
    speed_copy.start()
    flow_copy.start()
    speed_copy.wait()
    halves = rows_y // SUB

    @pl.loop(0, components * halves)
    def _(group):
        v = group // halves
        y = pl.ds(pl.multiple_of((group % halves) * SUB, SUB), SUB)
        scale = 100.0 * scale_ref[v]

        def step(k, run):
            speeds = [speed_ref[k * STEPS + i, y, :] for i in range(STEPS)]
            ratios = [1.0 / (1.0 + scale * speed) for speed in speeds]
            for ratio in ratios:
                run = run - ratio * run
            for i in range(STEPS):
                ratio_ref[k * STEPS + i, v, y, :] = ratios[i]
            return run

        start = jnp.ones((SUB, width_z), F32)
        total_ref[v, y, :] = lax.fori_loop(0, width_x // STEPS, step, start)
        last_ref[v, y, :] = 1.0 - ratio_ref[width_x - 1, v, y, :]

    flow_copy.wait()


def fill_kernel(turns, tile_ref, live_ref, weight_ref, flow_ref, *refs):
    arrived_refs = refs[: len(turns)]
    filled_ref = refs[len(turns)]
    rows_y = filled_ref.shape[2]
    components, capacity, _ = arrived_refs[0].shape
    place = lax.axis_index(RING)

    for turn, arrived_ref in zip(turns, arrived_refs):
        peer = place ^ turn

        count = live_ref[peer, 0]
        for slot in range(1, capacity):
            count = count + live_ref[peer, slot]

        @pl.loop(0, (count + 1) // 2)
        def _(pair):
            slots = [2 * pair, 2 * pair + 1]
            tiles = [tile_ref[peer, slot] for slot in slots]
            spots = [(tile // rows_y, pl.ds(tile % rows_y, 1)) for tile in tiles]
            weights = [
                jnp.where(live_ref[peer, slot] == 1, weight_ref[peer, slot], 0.0) for slot in slots
            ]
            mixed = [
                (1.0 - weight) * filled_ref[x, v, y, :] + weight * arrived_ref[v, pl.ds(slot, 1), :]
                for v in range(components)
                for slot, (x, y), weight in zip(slots, spots, weights)
            ]
            for v in range(components):
                for i, (x, y) in enumerate(spots):
                    filled_ref[x, v, y, :] = mixed[2 * v + i]


def last_fill_kernel(turns, total_ref, *refs):
    *fill_refs, rows_ref, even_ref, odd_ref, tail_ref, head_ref = refs
    fill_kernel(turns, *fill_refs)
    filled_ref = fill_refs[-1]
    width_x, components, rows_y, width_z = filled_ref.shape
    odd = lax.axis_index("stream") % 2
    even_ref[0] = filled_ref[(width_x - 1) * (1 - odd)]
    odd_ref[0] = filled_ref[(width_x - 1) * odd]
    even_ref[1] = total_ref[...]
    odd_ref[1] = total_ref[...]
    lane = lax.broadcasted_iota(jnp.int32, (rows_y, LANES), 1)
    for v in range(components):

        def pack(x, packed):
            tail, head = packed
            here = lane // 2 == x
            tail = jnp.where(
                here, pltpu.roll(filled_ref[x, v, :, width_z - LANES :], 2 * x + 2, 1), tail
            )
            head = jnp.where(here, pltpu.roll(filled_ref[x, v, :, :LANES], 2 * x + 1, 1), head)
            return tail, head

        zero = jnp.zeros((rows_y, LANES), F32)
        tail_ref[v], head_ref[v] = lax.fori_loop(0, width_x, pack, (zero, zero), unroll=32)
        for spot, x in enumerate((0, 1, width_x - 2, width_x - 1)):
            rows_ref[spot, v] = filled_ref[x, v]


def scan_kernel(
    lowest, scale_ref, span_ref, filled_ref, ratio_ref, speed_ref, tail_ref, head_ref, before_ref, after_ref,
    local_ref, out_ref, prior_ref, face_ref, diff_ref
):
    width_x, _, rows_y, width_z = local_ref.shape
    components = out_ref.shape[0]
    halves = rows_y // SUB
    blocks = width_z // LANES
    before = present(before_ref, "span", 1)
    after = present(after_ref, "span", -1)
    tail = tail_ref[...]
    head = head_ref[...]
    outer = 0.5 * (before - pltpu.roll(before, 1, 2))
    inner = 0.5 * (head - before)
    prior_ref[...] = before
    face_ref[...] = before + limited(outer, inner)
    diff_ref[...] = 0.5 * (after - tail)
    lane = lax.broadcasted_iota(jnp.int32, (SUB, LANES), 1)
    first = lane == 0
    final = lane == LANES - 1

    @pl.loop(0, components * halves)
    def _(group):
        v = lowest + group // halves
        y = pl.ds(pl.multiple_of((group % halves) * SUB, SUB), SUB)
        scale_z = 100.0 * (scale_ref[v] * span_ref[v])
        prior = prior_ref[v, y, :]
        face = face_ref[v, y, :]
        diff = diff_ref[v, y, :]
        every = range(blocks)

        def load(ref, *at):
            return [ref[(*at, y, slice(b * LANES, (b + 1) * LANES))] for b in every]

        def right(values, edge):
            moved_right = [edge] + [pltpu.roll(u, 1, 1) for u in values]
            return [jnp.where(first, moved_right[b], moved_right[b + 1]) for b in every]

        def left(values, edge):
            moved_left = [pltpu.roll(u, LANES - 1, 1) for u in values] + [edge]
            return [jnp.where(final, moved_left[b + 1], moved_left[b]) for b in every]

        def steps(k, carry):
            here, rise, inflow = carry
            start = k * STEPS
            span = range(STEPS)
            turn = [LANES - 2 * (start + i) - 1 for i in span]
            rows = [here] + [load(filled_ref, start + i, v) for i in range(1, STEPS)]
            rows.append(load(filled_ref, jnp.minimum(start + STEPS, width_x - 1), v))
            back = [right(rows[i], pltpu.roll(prior, turn[i], 1)) for i in span]
            fall = [[0.5 * (rows[i][b] - back[i][b]) for b in every] for i in span]
            grow = [left(fall[i], pltpu.roll(diff, turn[i] - 1, 1)) for i in span]
            faces = [[rows[i][b] + limited(fall[i][b], grow[i][b]) for b in every] for i in span]
            shifted = [right(faces[i], pltpu.roll(face, turn[i], 1)) for i in span]
            known = [[rows[i][b] + scale_z * (shifted[i][b] - faces[i][b]) for b in every] for i in span]
            outs = []
            for i in span:
                u = rows[i]
                ratio = load(ratio_ref, start + i, v)
                rise_later = [0.5 * (rows[i + 1][b] - u[b]) for b in every]
                slope = [limited(rise[b], rise_later[b]) for b in every]
                total = [inflow[b] + (known[i][b] + slope[b]) for b in every]
                value = [ratio[b] * total[b] for b in every]
                inflow = [total[b] - value[b] for b in every]
                rise = rise_later
                outs.append([value[b] - slope[b] for b in every])
            for i in span:
                for b in every:
                    local_ref[start + i, v, y, slice(b * LANES, (b + 1) * LANES)] = outs[i][b]
            return rows[STEPS], rise, inflow

        zeros = [jnp.zeros((SUB, LANES), F32)] * blocks
        _, _, flux = lax.fori_loop(0, width_x // STEPS, steps, (load(filled_ref, 0, v), zeros, zeros))
        for b in every:
            out_ref[v - lowest, y, slice(b * LANES, (b + 1) * LANES)] = flux[b]


def edge_kernel(
    lowest, flux_ref, total_ref, last_ref, rows_ref, even_ref, odd_ref,
    flux_out, beyond_out, first_out, last_out,
):
    part = pl.ds(lowest, flux_ref.shape[0])
    behind = beside("behind", even_ref.at[0, part], odd_ref.at[0, part]) * inside("stream", 1)
    ahead = beside("ahead", even_ref.at[0, part], odd_ref.at[0, part]) * inside("stream", -1)
    row = [rows_ref[k, part] for k in range(4)]
    slope_first = limited(0.5 * (row[0] - behind), 0.5 * (row[1] - row[0]))
    slope_last = limited(0.5 * (row[3] - row[2]), 0.5 * (ahead - row[3]))
    kept = last_ref[part] * slope_last
    flux = flux_ref[...] + total_ref[part] * slope_first + kept
    flux_out[...] = flux
    beyond_out[...] = beside("ahead", even_ref.at[1, part], odd_ref.at[1, part]) * flux
    first_out[...] = slope_first
    last_out[...] = kept


def combine_kernel(lowest, begun, local_ref, ratio_ref, first_ref, last_ref, even_ref, odd_ref, *refs):
    *flux_refs, out_hbm, done_ref, inflow_ref, sem = refs[begun:]
    width_x, _, _, _ = local_ref.shape
    components = first_ref.shape[0]
    flux = [present(ref, "stream", i + 1) for i, ref in enumerate(flux_refs)]
    beyond = sum(flux[2:], flux[1]) if len(flux) > 1 else 0.0
    behind = beside("behind", *(ref.at[1, pl.ds(lowest, components)] for ref in (even_ref, odd_ref)))
    inflow_ref[...] = first_ref[...] + flux[0] + behind * beyond
    part = 4

    def copy_of(k):
        rows = pl.ds(k * part, part)
        return pltpu.make_async_copy(
            done_ref.at[rows], out_hbm.at[rows, pl.ds(lowest, components)], sem
        )

    @pl.loop(0, width_x // part)
    def _(k):
        for v in range(components):
            inflow = inflow_ref[v]
            outs = []
            for i in range(part):
                gain = ratio_ref[k * part + i, lowest + v] * inflow
                outs.append(local_ref[k * part + i, lowest + v] + gain)
                inflow = inflow - gain
            for i in range(part):
                done_ref[k * part + i, v] = outs[i]
            inflow_ref[v] = inflow

        @pl.when(k == 0)
        def _():
            done_ref[0] = done_ref[0] - first_ref[...]

        @pl.when(k == width_x // part - 1)
        def _():
            done_ref[width_x - 1] = done_ref[width_x - 1] - last_ref[...]

        copy_of(k).start()

    @pl.loop(0, width_x // part)
    def _(k):
        copy_of(k).wait()


def moved(value, axis, distance):
    count = lax.axis_size(axis)
    return lax.ppermute(value, axis, [(i, (i + distance) % count) for i in range(count)])


def on_device(
    flow_state, wave_speed, char_scale, span_ratio, send_tile, recv_tile, recv_live, interp_weight
):
    _, width_x, rows_y, components, width_z = flow_state.shape
    peers, capacity = send_tile.shape[-2:]
    sections = lax.axis_size("stream")
    flow = pltpu.with_memory_space_constraint(jnp.transpose(flow_state[0], (0, 2, 1, 3)), HBM)
    speed = wave_speed[0]
    state = (width_x, components, rows_y, width_z)
    line = (components, rows_y, width_z)
    edge = (components, rows_y, LANES)
    hold = lambda shape: pltpu.VMEM(shape, F32)
    send, tile, live, weight = (
        t.reshape(peers, capacity) for t in (send_tile, recv_tile, recv_live, interp_weight)
    )
    assert peers & (peers - 1) == 0

    order = sorted(range(1, peers), key=lambda turn: (turn == 1, turn & 1, turn))
    near = peers // 2 - 1
    arrived = {}
    groups = [order[:1], order[1:near], order[near:] + [0]]
    for turns in groups:
        outgoing = call(
            functools.partial(gather_kernel, turns),
            (SMEM, HBM), (VMEM,) * len(turns),
            [jax.ShapeDtypeStruct((components, capacity, width_z), F32)] * len(turns),
            [pltpu.SemaphoreType.DMA((len(turns),))],
            micros=1,
        )(send, flow)
        for turn, tiles in zip(turns, outgoing):
            route = [(i, i ^ turn) for i in range(peers)]
            arrived[turn] = lax.ppermute(tiles, RING, route) if turn else tiles
    early, late = order[:near] + [1, 0], order[near:-1]
    flow_in, speed_in, ratio, total, last = call(
        growth_kernel,
        (SMEM, HBM, HBM), (VMEM,) * 5,
        [hold(state), hold(speed.shape), hold(state), hold(line), hold(line)],
        [pltpu.SemaphoreType.DMA((2,))],
        micros=5,
    )(char_scale, flow, speed)
    (partly,) = call(
        functools.partial(fill_kernel, early),
        (SMEM,) * 3 + (VMEM,) * (1 + len(early)), (VMEM,),
        [hold(state)],
        aliases={3: 0},
        micros=2,
    )(tile, live, weight, flow_in, *(arrived[turn] for turn in early))
    filled, rows, even, odd, tail, head = call(
        functools.partial(last_fill_kernel, late),
        (VMEM,) + (SMEM,) * 3 + (VMEM,) * (1 + len(late)), (VMEM,) * 6,
        [hold(state), hold((4, *line)), hold((2, *line)), hold((2, *line)), hold(edge), hold(edge)],
        aliases={4: 0},
        micros=4,
    )(total, tile, live, weight, partly, *(arrived[turn] for turn in late))
    pairs = [[i ^ 1 for i in range(sections)], [((i + 1) ^ 1) - 1 for i in range(sections)]]
    even, odd = (
        lax.ppermute(
            message,
            "stream",
            [(i, other if 0 <= other < sections else i) for i, other in enumerate(others)],
        )
        for message, others in zip((even, odd), pairs)
    )
    before = moved(tail, "span", 1)
    after = moved(head, "span", -1)
    assert sections <= 4
    split = (components + 1) // 2
    state_now, parts = filled, []
    for lowest, size in ((0, split), (split, components - split)):
        some = (size, rows_y, width_z)
        state_now, flux = call(
            functools.partial(scan_kernel, lowest),
            (SMEM, SMEM) + (VMEM,) * 7, (VMEM,) * 2,
            [hold(state), hold(some)],
            [pltpu.VMEM(edge, F32)] * 3,
            aliases={2: 0},
            micros=3 * size,
        )(char_scale, span_ratio, state_now, ratio, speed_in, tail, head, before, after)
        flux, beyond, first_slope, last_slope = call(
            functools.partial(edge_kernel, lowest),
            (VMEM,) * 6, (VMEM,) * 4,
            [jax.ShapeDtypeStruct(some, F32)] * 4,
        )(flux, total, last, rows, even, odd)
        fluxes = [moved(flux if d < 3 else beyond, "stream", d) for d in range(1, sections)]
        parts.append((lowest, some, first_slope, last_slope, fluxes))
    begun = ()
    for lowest, some, first_slope, last_slope, fluxes in parts:
        begun = call(
            functools.partial(combine_kernel, lowest, len(begun)),
            (VMEM,) * 6 + (HBM,) * len(begun) + (VMEM,) * (sections - 1), (HBM,),
            [jax.ShapeDtypeStruct(state, F32)],
            [
                pltpu.VMEM((width_x, *some), F32),
                pltpu.VMEM(some, F32),
                pltpu.SemaphoreType.DMA,
            ],
            aliases={6: 0} if begun else None,
            limit=10 << 20,
            micros=some[0],
        )(state_now, ratio, first_slope, last_slope, even, odd, *begun, *fluxes)
    (done,) = begun
    return jnp.transpose(done, (0, 2, 1, 3))[None]


def solution(mesh):
    return jax.shard_map(
        on_device,
        mesh=mesh,
        in_specs=(
            P("block", "stream", None, None, "span"),
            P("block", "stream", None, "span"),
            P(),
            P(),
            P("block", "span", "stream", None, None),
            P("block", "span", "stream", None, None),
            P("block", "span", "stream", None, None),
            P("block", "span", "stream", None, None),
        ),
        out_specs=P("block", "stream", None, None, "span"),
        check_vma=False,
    )
```

```python
import functools
import jax
import jax.numpy as jnp
from jax import lax
from jax.experimental import pallas as pl
from jax.experimental.pallas import tpu as pltpu
from jax.sharding import PartitionSpec as P


LANES = 128
SUB = 8
STEPS = 16
F32 = jnp.float32


def space(kind):
    return pl.BlockSpec(memory_space=kind)


SMEM, VMEM, HBM = pltpu.SMEM, pltpu.VMEM, pltpu.HBM

RING = ("block", "span")


def limited(first, second):
    return jnp.maximum(
        jnp.minimum(second, jnp.maximum(first, 0.0)), jnp.minimum(first, 0.0)
    )


def call(kernel, ins, outs, out_shape, scratch=(), aliases=None, limit=8 << 20, micros=0):
    return pl.pallas_call(
        kernel,
        out_shape=out_shape,
        in_specs=[space(k) for k in ins],
        out_specs=[space(k) for k in outs],
        scratch_shapes=list(scratch),
        input_output_aliases=aliases or {},
        compiler_params=pltpu.CompilerParams(vmem_limit_bytes=limit),
        cost_estimate=pl.CostEstimate(flops=0, transcendentals=0, bytes_accessed=int(micros * 3.0e6)),
    )


def inside(axis, distance):
    source = lax.axis_index(axis) - distance
    return jnp.where((source >= 0) & (source < lax.axis_size(axis)), 1.0, 0.0)


def present(ref, axis, distance):
    return ref[...] * inside(axis, distance)


def beside(side, even_ref, odd_ref):
    odd = lax.axis_index("stream") % 2
    return jnp.where(odd == (1 if side == "behind" else 0), even_ref[...], odd_ref[...])


def gather_kernel(turns, send_ref, flow_ref, *refs):
    *out_refs, sem = refs
    _, capacity, _ = out_refs[0].shape
    rows_y = flow_ref.shape[2]
    place = lax.axis_index(RING)

    for k, (out_ref, turn) in enumerate(zip(out_refs, turns)):
        for slot in range(capacity):
            tile = send_ref[place ^ turn, slot]
            pltpu.make_async_copy(
                flow_ref.at[tile // rows_y, :, pl.ds(tile % rows_y, 1), :],
                out_ref.at[:, slot : slot + 1, :],
                sem.at[k],
            ).start()
    for k, out_ref in enumerate(out_refs):
        pltpu.make_async_copy(out_ref, out_ref, sem.at[k]).wait()


def growth_kernel(scale_ref, flow_hbm, speed_hbm, flow_ref, speed_ref, ratio_ref, total_ref, last_ref, sem):
    width_x, components, rows_y, width_z = ratio_ref.shape
    speed_copy = pltpu.make_async_copy(speed_hbm, speed_ref, sem.at[0])
    flow_copy = pltpu.make_async_copy(flow_hbm, flow_ref, sem.at[1])
    speed_copy.start()
    flow_copy.start()
    speed_copy.wait()
    halves = rows_y // SUB

    @pl.loop(0, components * halves)
    def _(group):
        v = group // halves
        y = pl.ds(pl.multiple_of((group % halves) * SUB, SUB), SUB)
        scale = 100.0 * scale_ref[v]

        def step(k, run):
            speeds = [speed_ref[k * STEPS + i, y, :] for i in range(STEPS)]
            ratios = [1.0 / (1.0 + scale * speed) for speed in speeds]
            for ratio in ratios:
                run = run - ratio * run
            for i in range(STEPS):
                ratio_ref[k * STEPS + i, v, y, :] = ratios[i]
            return run

        start = jnp.ones((SUB, width_z), F32)
        total_ref[v, y, :] = lax.fori_loop(0, width_x // STEPS, step, start)
        last_ref[v, y, :] = 1.0 - ratio_ref[width_x - 1, v, y, :]

    flow_copy.wait()


def fill_kernel(turns, tile_ref, live_ref, weight_ref, flow_ref, *refs):
    arrived_refs = refs[: len(turns)]
    filled_ref = refs[len(turns)]
    rows_y = filled_ref.shape[2]
    components, capacity, _ = arrived_refs[0].shape
    place = lax.axis_index(RING)

    for turn, arrived_ref in zip(turns, arrived_refs):
        peer = place ^ turn

        count = live_ref[peer, 0]
        for slot in range(1, capacity):
            count = count + live_ref[peer, slot]

        @pl.loop(0, (count + 1) // 2)
        def _(pair):
            slots = [2 * pair, 2 * pair + 1]
            tiles = [tile_ref[peer, slot] for slot in slots]
            spots = [(tile // rows_y, pl.ds(tile % rows_y, 1)) for tile in tiles]
            weights = [
                jnp.where(live_ref[peer, slot] == 1, weight_ref[peer, slot], 0.0) for slot in slots
            ]
            mixed = [
                (1.0 - weight) * filled_ref[x, v, y, :] + weight * arrived_ref[v, pl.ds(slot, 1), :]
                for v in range(components)
                for slot, (x, y), weight in zip(slots, spots, weights)
            ]
            for v in range(components):
                for i, (x, y) in enumerate(spots):
                    filled_ref[x, v, y, :] = mixed[2 * v + i]


def last_fill_kernel(turns, total_ref, *refs):
    *fill_refs, rows_ref, even_ref, odd_ref, tail_ref, head_ref = refs
    fill_kernel(turns, *fill_refs)
    filled_ref = fill_refs[-1]
    width_x, components, rows_y, width_z = filled_ref.shape
    odd = lax.axis_index("stream") % 2
    even_ref[0] = filled_ref[(width_x - 1) * (1 - odd)]
    odd_ref[0] = filled_ref[(width_x - 1) * odd]
    even_ref[1] = total_ref[...]
    odd_ref[1] = total_ref[...]
    lane = lax.broadcasted_iota(jnp.int32, (rows_y, LANES), 1)
    for v in range(components):

        def pack(x, packed):
            tail, head = packed
            here = lane // 2 == x
            tail = jnp.where(
                here, pltpu.roll(filled_ref[x, v, :, width_z - LANES :], 2 * x + 2, 1), tail
            )
            head = jnp.where(here, pltpu.roll(filled_ref[x, v, :, :LANES], 2 * x + 1, 1), head)
            return tail, head

        zero = jnp.zeros((rows_y, LANES), F32)
        tail_ref[v], head_ref[v] = lax.fori_loop(0, width_x, pack, (zero, zero), unroll=32)
        for spot, x in enumerate((0, 1, width_x - 2, width_x - 1)):
            rows_ref[spot, v] = filled_ref[x, v]


def scan_kernel(
    lowest, scale_ref, span_ref, filled_ref, ratio_ref, speed_ref, tail_ref, head_ref, before_ref, after_ref,
    local_ref, out_ref, prior_ref, face_ref, diff_ref
):
    width_x, _, rows_y, width_z = local_ref.shape
    components = out_ref.shape[0]
    halves = rows_y // SUB
    blocks = width_z // LANES
    before = present(before_ref, "span", 1)
    after = present(after_ref, "span", -1)
    tail = tail_ref[...]
    head = head_ref[...]
    outer = 0.5 * (before - pltpu.roll(before, 1, 2))
    inner = 0.5 * (head - before)
    prior_ref[...] = before
    face_ref[...] = before + limited(outer, inner)
    diff_ref[...] = 0.5 * (after - tail)
    lane = lax.broadcasted_iota(jnp.int32, (SUB, LANES), 1)
    first = lane == 0
    final = lane == LANES - 1

    @pl.loop(0, components * halves)
    def _(group):
        v = lowest + group // halves
        y = pl.ds(pl.multiple_of((group % halves) * SUB, SUB), SUB)
        scale_z = 100.0 * (scale_ref[v] * span_ref[v])
        prior = prior_ref[v, y, :]
        face = face_ref[v, y, :]
        diff = diff_ref[v, y, :]
        every = range(blocks)

        def load(ref, *at):
            return [ref[(*at, y, slice(b * LANES, (b + 1) * LANES))] for b in every]

        def right(values, edge):
            moved_right = [edge] + [pltpu.roll(u, 1, 1) for u in values]
            return [jnp.where(first, moved_right[b], moved_right[b + 1]) for b in every]

        def left(values, edge):
            moved_left = [pltpu.roll(u, LANES - 1, 1) for u in values] + [edge]
            return [jnp.where(final, moved_left[b + 1], moved_left[b]) for b in every]

        def steps(k, carry):
            here, rise, inflow = carry
            start = k * STEPS
            span = range(STEPS)
            turn = [LANES - 2 * (start + i) - 1 for i in span]
            rows = [here] + [load(filled_ref, start + i, v) for i in range(1, STEPS)]
            rows.append(load(filled_ref, jnp.minimum(start + STEPS, width_x - 1), v))
            back = [right(rows[i], pltpu.roll(prior, turn[i], 1)) for i in span]
            fall = [[0.5 * (rows[i][b] - back[i][b]) for b in every] for i in span]
            grow = [left(fall[i], pltpu.roll(diff, turn[i] - 1, 1)) for i in span]
            faces = [[rows[i][b] + limited(fall[i][b], grow[i][b]) for b in every] for i in span]
            shifted = [right(faces[i], pltpu.roll(face, turn[i], 1)) for i in span]
            known = [[rows[i][b] + scale_z * (shifted[i][b] - faces[i][b]) for b in every] for i in span]
            outs = []
            for i in span:
                u = rows[i]
                ratio = load(ratio_ref, start + i, v)
                rise_later = [0.5 * (rows[i + 1][b] - u[b]) for b in every]
                slope = [limited(rise[b], rise_later[b]) for b in every]
                total = [inflow[b] + (known[i][b] + slope[b]) for b in every]
                value = [ratio[b] * total[b] for b in every]
                inflow = [total[b] - value[b] for b in every]
                rise = rise_later
                outs.append([value[b] - slope[b] for b in every])
            for i in span:
                for b in every:
                    local_ref[start + i, v, y, slice(b * LANES, (b + 1) * LANES)] = outs[i][b]
            return rows[STEPS], rise, inflow

        zeros = [jnp.zeros((SUB, LANES), F32)] * blocks
        _, _, flux = lax.fori_loop(0, width_x // STEPS, steps, (load(filled_ref, 0, v), zeros, zeros))
        for b in every:
            out_ref[v - lowest, y, slice(b * LANES, (b + 1) * LANES)] = flux[b]


def edge_kernel(
    lowest, flux_ref, total_ref, last_ref, rows_ref, even_ref, odd_ref,
    flux_out, beyond_out, first_out, last_out,
):
    part = pl.ds(lowest, flux_ref.shape[0])
    behind = beside("behind", even_ref.at[0, part], odd_ref.at[0, part]) * inside("stream", 1)
    ahead = beside("ahead", even_ref.at[0, part], odd_ref.at[0, part]) * inside("stream", -1)
    row = [rows_ref[k, part] for k in range(4)]
    slope_first = limited(0.5 * (row[0] - behind), 0.5 * (row[1] - row[0]))
    slope_last = limited(0.5 * (row[3] - row[2]), 0.5 * (ahead - row[3]))
    kept = last_ref[part] * slope_last
    flux = flux_ref[...] + total_ref[part] * slope_first + kept
    flux_out[...] = flux
    beyond_out[...] = beside("ahead", even_ref.at[1, part], odd_ref.at[1, part]) * flux
    first_out[...] = slope_first
    last_out[...] = kept


def combine_kernel(lowest, begun, local_ref, ratio_ref, first_ref, last_ref, even_ref, odd_ref, *refs):
    *flux_refs, out_hbm, done_ref, inflow_ref, sem = refs[begun:]
    width_x, _, _, _ = local_ref.shape
    components = first_ref.shape[0]
    flux = [present(ref, "stream", i + 1) for i, ref in enumerate(flux_refs)]
    beyond = sum(flux[2:], flux[1]) if len(flux) > 1 else 0.0
    behind = beside("behind", *(ref.at[1, pl.ds(lowest, components)] for ref in (even_ref, odd_ref)))
    inflow_ref[...] = first_ref[...] + flux[0] + behind * beyond
    part = 4

    def copy_of(k):
        rows = pl.ds(k * part, part)
        return pltpu.make_async_copy(
            done_ref.at[rows], out_hbm.at[rows, pl.ds(lowest, components)], sem
        )

    @pl.loop(0, width_x // part)
    def _(k):
        for v in range(components):
            inflow = inflow_ref[v]
            outs = []
            for i in range(part):
                gain = ratio_ref[k * part + i, lowest + v] * inflow
                outs.append(local_ref[k * part + i, lowest + v] + gain)
                inflow = inflow - gain
            for i in range(part):
                done_ref[k * part + i, v] = outs[i]
            inflow_ref[v] = inflow

        @pl.when(k == 0)
        def _():
            done_ref[0] = done_ref[0] - first_ref[...]

        @pl.when(k == width_x // part - 1)
        def _():
            done_ref[width_x - 1] = done_ref[width_x - 1] - last_ref[...]

        copy_of(k).start()

    @pl.loop(0, width_x // part)
    def _(k):
        copy_of(k).wait()


def moved(value, axis, distance):
    count = lax.axis_size(axis)
    return lax.ppermute(value, axis, [(i, (i + distance) % count) for i in range(count)])


def on_device(
    flow_state, wave_speed, char_scale, span_ratio, send_tile, recv_tile, recv_live, interp_weight
):
    _, width_x, rows_y, components, width_z = flow_state.shape
    peers, capacity = send_tile.shape[-2:]
    sections = lax.axis_size("stream")
    flow = pltpu.with_memory_space_constraint(jnp.transpose(flow_state[0], (0, 2, 1, 3)), HBM)
    speed = wave_speed[0]
    state = (width_x, components, rows_y, width_z)
    line = (components, rows_y, width_z)
    edge = (components, rows_y, LANES)
    hold = lambda shape: pltpu.VMEM(shape, F32)
    send, tile, live, weight = (
        t.reshape(peers, capacity) for t in (send_tile, recv_tile, recv_live, interp_weight)
    )
    assert peers & (peers - 1) == 0

    order = sorted(range(1, peers), key=lambda turn: (turn == 1, turn & 1, turn))
    near = peers // 2 - 1
    arrived = {}
    groups = [order[:near], order[near:] + [0]]
    for turns in groups:
        outgoing = call(
            functools.partial(gather_kernel, turns),
            (SMEM, HBM), (VMEM,) * len(turns),
            [jax.ShapeDtypeStruct((components, capacity, width_z), F32)] * len(turns),
            [pltpu.SemaphoreType.DMA((len(turns),))],
            micros=1,
        )(send, flow)
        for turn, tiles in zip(turns, outgoing):
            route = [(i, i ^ turn) for i in range(peers)]
            arrived[turn] = lax.ppermute(tiles, RING, route) if turn else tiles
    late = order[near:-1][-2:]
    early = [turn for turn in order + [0] if turn not in late]
    flow_in, speed_in, ratio, total, last = call(
        growth_kernel,
        (SMEM, HBM, HBM), (VMEM,) * 5,
        [hold(state), hold(speed.shape), hold(state), hold(line), hold(line)],
        [pltpu.SemaphoreType.DMA((2,))],
        micros=5,
    )(char_scale, flow, speed)
    (partly,) = call(
        functools.partial(fill_kernel, early),
        (SMEM,) * 3 + (VMEM,) * (1 + len(early)), (VMEM,),
        [hold(state)],
        aliases={3: 0},
        micros=2,
    )(tile, live, weight, flow_in, *(arrived[turn] for turn in early))
    filled, rows, even, odd, tail, head = call(
        functools.partial(last_fill_kernel, late),
        (VMEM,) + (SMEM,) * 3 + (VMEM,) * (1 + len(late)), (VMEM,) * 6,
        [hold(state), hold((4, *line)), hold((2, *line)), hold((2, *line)), hold(edge), hold(edge)],
        aliases={4: 0},
        micros=4,
    )(total, tile, live, weight, partly, *(arrived[turn] for turn in late))
    before = moved(tail, "span", 1)
    after = moved(head, "span", -1)
    pairs = [[i ^ 1 for i in range(sections)], [((i + 1) ^ 1) - 1 for i in range(sections)]]
    even, odd = (
        lax.ppermute(
            message,
            "stream",
            [(i, other if 0 <= other < sections else i) for i, other in enumerate(others)],
        )
        for message, others in zip((even, odd), pairs)
    )
    assert sections <= 4
    split = (components + 1) // 2
    state_now, parts = filled, []
    for lowest, size in ((0, split), (split, components - split)):
        some = (size, rows_y, width_z)
        state_now, flux = call(
            functools.partial(scan_kernel, lowest),
            (SMEM, SMEM) + (VMEM,) * 7, (VMEM,) * 2,
            [hold(state), hold(some)],
            [pltpu.VMEM(edge, F32)] * 3,
            aliases={2: 0},
            micros=3 * size,
        )(char_scale, span_ratio, state_now, ratio, speed_in, tail, head, before, after)
        flux, beyond, first_slope, last_slope = call(
            functools.partial(edge_kernel, lowest),
            (VMEM,) * 6, (VMEM,) * 4,
            [jax.ShapeDtypeStruct(some, F32)] * 4,
        )(flux, total, last, rows, even, odd)
        fluxes = [moved(flux if d < 3 else beyond, "stream", d) for d in range(1, sections)]
        parts.append((lowest, some, first_slope, last_slope, fluxes))
    begun = ()
    for lowest, some, first_slope, last_slope, fluxes in parts:
        begun = call(
            functools.partial(combine_kernel, lowest, len(begun)),
            (VMEM,) * 6 + (HBM,) * len(begun) + (VMEM,) * (sections - 1), (HBM,),
            [jax.ShapeDtypeStruct(state, F32)],
            [
                pltpu.VMEM((width_x, *some), F32),
                pltpu.VMEM(some, F32),
                pltpu.SemaphoreType.DMA,
            ],
            aliases={6: 0} if begun else None,
            limit=10 << 20,
            micros=some[0],
        )(state_now, ratio, first_slope, last_slope, even, odd, *begun, *fluxes)
    (done,) = begun
    return jnp.transpose(done, (0, 2, 1, 3))[None]


def solution(mesh):
    return jax.shard_map(
        on_device,
        mesh=mesh,
        in_specs=(
            P("block", "stream", None, None, "span"),
            P("block", "stream", None, "span"),
            P(),
            P(),
            P("block", "span", "stream", None, None),
            P("block", "span", "stream", None, None),
            P("block", "span", "stream", None, None),
            P("block", "span", "stream", None, None),
        ),
        out_specs=P("block", "stream", None, None, "span"),
        check_vma=False,
    )
```

```python
import functools
import jax
import jax.numpy as jnp
from jax import lax
from jax.experimental import pallas as pl
from jax.experimental.pallas import tpu as pltpu
from jax.sharding import PartitionSpec as P


LANES = 128
SUB = 8
STEPS = 16
LAG = 6
F32 = jnp.float32


def space(kind):
    return pl.BlockSpec(memory_space=kind)


SMEM, VMEM, HBM = pltpu.SMEM, pltpu.VMEM, pltpu.HBM

RING = ("block", "span")


def limited(first, second):
    return jnp.maximum(
        jnp.minimum(second, jnp.maximum(first, 0.0)), jnp.minimum(first, 0.0)
    )


def call(kernel, ins, outs, out_shape, scratch=(), aliases=None, limit=8 << 20, micros=0):
    return pl.pallas_call(
        kernel,
        out_shape=out_shape,
        in_specs=[space(k) for k in ins],
        out_specs=[space(k) for k in outs],
        scratch_shapes=list(scratch),
        input_output_aliases=aliases or {},
        compiler_params=pltpu.CompilerParams(vmem_limit_bytes=limit),
        cost_estimate=pl.CostEstimate(flops=0, transcendentals=0, bytes_accessed=int(micros * 3.0e6)),
    )


def inside(axis, distance):
    source = lax.axis_index(axis) - distance
    return jnp.where((source >= 0) & (source < lax.axis_size(axis)), 1.0, 0.0)


def present(ref, axis, distance):
    return ref[...] * inside(axis, distance)


def beside(side, even_ref, odd_ref):
    odd = lax.axis_index("stream") % 2
    return jnp.where(odd == (1 if side == "behind" else 0), even_ref[...], odd_ref[...])


def gather_kernel(turns, send_ref, flow_ref, *refs):
    *out_refs, sem = refs
    _, capacity, _ = out_refs[0].shape
    rows_y = flow_ref.shape[2]
    place = lax.axis_index(RING)

    for k, (out_ref, turn) in enumerate(zip(out_refs, turns)):
        for slot in range(capacity):
            tile = send_ref[place ^ turn, slot]
            pltpu.make_async_copy(
                flow_ref.at[tile // rows_y, :, pl.ds(tile % rows_y, 1), :],
                out_ref.at[:, slot : slot + 1, :],
                sem.at[k],
            ).start()
    for k, out_ref in enumerate(out_refs):
        pltpu.make_async_copy(out_ref, out_ref, sem.at[k]).wait()


def growth_kernel(scale_ref, flow_hbm, speed_hbm, flow_ref, speed_ref, ratio_ref, total_ref, last_ref, sem):
    width_x, components, rows_y, width_z = ratio_ref.shape
    speed_copy = pltpu.make_async_copy(speed_hbm, speed_ref, sem.at[0])
    flow_copy = pltpu.make_async_copy(flow_hbm, flow_ref, sem.at[1])
    speed_copy.start()
    flow_copy.start()
    speed_copy.wait()
    halves = rows_y // SUB

    @pl.loop(0, components * halves)
    def _(group):
        v = group // halves
        y = pl.ds(pl.multiple_of((group % halves) * SUB, SUB), SUB)
        scale = 100.0 * scale_ref[v]

        def step(k, run):
            speeds = [speed_ref[k * STEPS + i, y, :] for i in range(STEPS)]
            ratios = [1.0 / (1.0 + scale * speed) for speed in speeds]
            for ratio in ratios:
                run = run - ratio * run
            for i in range(STEPS):
                ratio_ref[k * STEPS + i, v, y, :] = ratios[i]
            return run

        start = jnp.ones((SUB, width_z), F32)
        total_ref[v, y, :] = lax.fori_loop(0, width_x // STEPS, step, start)
        last_ref[v, y, :] = 1.0 - ratio_ref[width_x - 1, v, y, :]

    flow_copy.wait()


def fill_kernel(turns, tile_ref, live_ref, weight_ref, flow_ref, *refs):
    arrived_refs = refs[: len(turns)]
    filled_ref = refs[len(turns)]
    rows_y = filled_ref.shape[2]
    components, capacity, _ = arrived_refs[0].shape
    place = lax.axis_index(RING)

    for turn, arrived_ref in zip(turns, arrived_refs):
        peer = place ^ turn

        count = live_ref[peer, 0]
        for slot in range(1, capacity):
            count = count + live_ref[peer, slot]

        @pl.loop(0, (count + 1) // 2)
        def _(pair):
            slots = [2 * pair, 2 * pair + 1]
            tiles = [tile_ref[peer, slot] for slot in slots]
            spots = [(tile // rows_y, pl.ds(tile % rows_y, 1)) for tile in tiles]
            weights = [
                jnp.where(live_ref[peer, slot] == 1, weight_ref[peer, slot], 0.0) for slot in slots
            ]
            mixed = [
                (1.0 - weight) * filled_ref[x, v, y, :] + weight * arrived_ref[v, pl.ds(slot, 1), :]
                for v in range(components)
                for slot, (x, y), weight in zip(slots, spots, weights)
            ]
            for v in range(components):
                for i, (x, y) in enumerate(spots):
                    filled_ref[x, v, y, :] = mixed[2 * v + i]


def last_fill_kernel(turns, total_ref, *refs):
    *fill_refs, rows_ref, even_ref, odd_ref, tail_ref, head_ref = refs
    fill_kernel(turns, *fill_refs)
    filled_ref = fill_refs[-1]
    width_x, components, rows_y, width_z = filled_ref.shape
    odd = lax.axis_index("stream") % 2
    even_ref[0] = filled_ref[(width_x - 1) * (1 - odd)]
    odd_ref[0] = filled_ref[(width_x - 1) * odd]
    even_ref[1] = total_ref[...]
    odd_ref[1] = total_ref[...]
    lane = lax.broadcasted_iota(jnp.int32, (rows_y, LANES), 1)
    for v in range(components):

        def pack(x, packed):
            tail, head = packed
            here = lane // 2 == x
            tail = jnp.where(
                here, pltpu.roll(filled_ref[x, v, :, width_z - LANES :], 2 * x + 2, 1), tail
            )
            head = jnp.where(here, pltpu.roll(filled_ref[x, v, :, :LANES], 2 * x + 1, 1), head)
            return tail, head

        zero = jnp.zeros((rows_y, LANES), F32)
        tail_ref[v], head_ref[v] = lax.fori_loop(0, width_x, pack, (zero, zero), unroll=32)
        for spot, x in enumerate((0, 1, width_x - 2, width_x - 1)):
            rows_ref[spot, v] = filled_ref[x, v]


def scan_kernel(
    lowest, scale_ref, span_ref, filled_ref, ratio_ref, speed_ref, tail_ref, head_ref, before_ref, after_ref,
    local_ref, out_ref, prior_ref, face_ref, diff_ref
):
    width_x, _, rows_y, width_z = local_ref.shape
    components = out_ref.shape[0]
    halves = rows_y // SUB
    blocks = width_z // LANES
    before = present(before_ref, "span", 1)
    after = present(after_ref, "span", -1)
    tail = tail_ref[...]
    head = head_ref[...]
    outer = 0.5 * (before - pltpu.roll(before, 1, 2))
    inner = 0.5 * (head - before)
    prior_ref[...] = before
    face_ref[...] = before + limited(outer, inner)
    diff_ref[...] = 0.5 * (after - tail)
    lane = lax.broadcasted_iota(jnp.int32, (SUB, LANES), 1)
    first = lane == 0
    final = lane == LANES - 1

    @pl.loop(0, components * halves)
    def _(group):
        v = lowest + group // halves
        y = pl.ds(pl.multiple_of((group % halves) * SUB, SUB), SUB)
        scale_z = 100.0 * (scale_ref[v] * span_ref[v])
        prior = prior_ref[v, y, :]
        face = face_ref[v, y, :]
        diff = diff_ref[v, y, :]
        every = range(blocks)

        def load(ref, *at):
            return [ref[(*at, y, slice(b * LANES, (b + 1) * LANES))] for b in every]

        def right(values, edge):
            moved_right = [edge] + [pltpu.roll(u, 1, 1) for u in values]
            return [jnp.where(first, moved_right[b], moved_right[b + 1]) for b in every]

        def left(values, edge):
            moved_left = [pltpu.roll(u, LANES - 1, 1) for u in values] + [edge]
            return [jnp.where(final, moved_left[b + 1], moved_left[b]) for b in every]

        inflow = [jnp.zeros((SUB, LANES), F32)] * blocks
        rise = inflow
        rows, falls, faces, known = {}, {}, {}, {}
        for tick in range(width_x + 3 * LAG):
            i = tick
            if i < width_x:
                rows[i] = load(filled_ref, i, v)
                back = right(rows[i], pltpu.roll(prior, LANES - 2 * i - 1, 1))
                falls[i] = [0.5 * (rows[i][b] - back[b]) for b in every]
            i = tick - LAG
            if 0 <= i < width_x:
                fall = falls.pop(i)
                grow = left(fall, pltpu.roll(diff, LANES - 2 * i - 2, 1))
                faces[i] = [rows[i][b] + limited(fall[b], grow[b]) for b in every]
            i = tick - 2 * LAG
            if 0 <= i < width_x:
                flat = faces.pop(i)
                shifted = right(flat, pltpu.roll(face, LANES - 2 * i - 1, 1))
                known[i] = [rows[i][b] + scale_z * (shifted[b] - flat[b]) for b in every]
            i = tick - 3 * LAG
            if i >= 0:
                u = rows.pop(i)
                later = rows.get(i + 1, u)
                rise_later = [0.5 * (later[b] - u[b]) for b in every]
                ratio = load(ratio_ref, i, v)
                cross = known.pop(i)
                slope = [limited(rise[b], rise_later[b]) for b in every]
                total = [inflow[b] + (cross[b] + slope[b]) for b in every]
                value = [ratio[b] * total[b] for b in every]
                inflow = [total[b] - value[b] for b in every]
                rise = rise_later
                for b in every:
                    local_ref[i, v, y, slice(b * LANES, (b + 1) * LANES)] = value[b] - slope[b]
        for b in every:
            out_ref[v - lowest, y, slice(b * LANES, (b + 1) * LANES)] = inflow[b]


def edge_kernel(
    lowest, flux_ref, total_ref, last_ref, rows_ref, even_ref, odd_ref,
    flux_out, beyond_out, first_out, last_out,
):
    part = pl.ds(lowest, flux_ref.shape[0])
    behind = beside("behind", even_ref.at[0, part], odd_ref.at[0, part]) * inside("stream", 1)
    ahead = beside("ahead", even_ref.at[0, part], odd_ref.at[0, part]) * inside("stream", -1)
    row = [rows_ref[k, part] for k in range(4)]
    slope_first = limited(0.5 * (row[0] - behind), 0.5 * (row[1] - row[0]))
    slope_last = limited(0.5 * (row[3] - row[2]), 0.5 * (ahead - row[3]))
    kept = last_ref[part] * slope_last
    flux = flux_ref[...] + total_ref[part] * slope_first + kept
    flux_out[...] = flux
    beyond_out[...] = beside("ahead", even_ref.at[1, part], odd_ref.at[1, part]) * flux
    first_out[...] = slope_first
    last_out[...] = kept


def combine_kernel(lowest, begun, local_ref, ratio_ref, first_ref, last_ref, even_ref, odd_ref, *refs):
    *flux_refs, out_hbm, done_ref, inflow_ref, sem = refs[begun:]
    width_x, _, _, _ = local_ref.shape
    components = first_ref.shape[0]
    flux = [present(ref, "stream", i + 1) for i, ref in enumerate(flux_refs)]
    beyond = sum(flux[2:], flux[1]) if len(flux) > 1 else 0.0
    behind = beside("behind", *(ref.at[1, pl.ds(lowest, components)] for ref in (even_ref, odd_ref)))
    inflow_ref[...] = first_ref[...] + flux[0] + behind * beyond
    part = 4

    def copy_of(k):
        rows = pl.ds(k * part, part)
        return pltpu.make_async_copy(
            done_ref.at[rows], out_hbm.at[rows, pl.ds(lowest, components)], sem
        )

    @pl.loop(0, width_x // part)
    def _(k):
        for v in range(components):
            inflow = inflow_ref[v]
            outs = []
            for i in range(part):
                gain = ratio_ref[k * part + i, lowest + v] * inflow
                outs.append(local_ref[k * part + i, lowest + v] + gain)
                inflow = inflow - gain
            for i in range(part):
                done_ref[k * part + i, v] = outs[i]
            inflow_ref[v] = inflow

        @pl.when(k == 0)
        def _():
            done_ref[0] = done_ref[0] - first_ref[...]

        @pl.when(k == width_x // part - 1)
        def _():
            done_ref[width_x - 1] = done_ref[width_x - 1] - last_ref[...]

        copy_of(k).start()

    @pl.loop(0, width_x // part)
    def _(k):
        copy_of(k).wait()


def moved(value, axis, distance):
    count = lax.axis_size(axis)
    return lax.ppermute(value, axis, [(i, (i + distance) % count) for i in range(count)])


def on_device(
    flow_state, wave_speed, char_scale, span_ratio, send_tile, recv_tile, recv_live, interp_weight
):
    _, width_x, rows_y, components, width_z = flow_state.shape
    peers, capacity = send_tile.shape[-2:]
    sections = lax.axis_size("stream")
    flow = pltpu.with_memory_space_constraint(jnp.transpose(flow_state[0], (0, 2, 1, 3)), HBM)
    speed = wave_speed[0]
    state = (width_x, components, rows_y, width_z)
    line = (components, rows_y, width_z)
    edge = (components, rows_y, LANES)
    hold = lambda shape: pltpu.VMEM(shape, F32)
    send, tile, live, weight = (
        t.reshape(peers, capacity) for t in (send_tile, recv_tile, recv_live, interp_weight)
    )
    assert peers & (peers - 1) == 0

    order = sorted(range(1, peers), key=lambda turn: (turn == 1, turn & 1, turn))
    near = peers // 2 - 1
    arrived = {}
    groups = [order[:near], order[near:] + [0]]
    for turns in groups:
        outgoing = call(
            functools.partial(gather_kernel, turns),
            (SMEM, HBM), (VMEM,) * len(turns),
            [jax.ShapeDtypeStruct((components, capacity, width_z), F32)] * len(turns),
            [pltpu.SemaphoreType.DMA((len(turns),))],
            micros=1,
        )(send, flow)
        for turn, tiles in zip(turns, outgoing):
            route = [(i, i ^ turn) for i in range(peers)]
            arrived[turn] = lax.ppermute(tiles, RING, route) if turn else tiles
    late = order[near:-1][-2:]
    early = [turn for turn in order + [0] if turn not in late]
    flow_in, speed_in, ratio, total, last = call(
        growth_kernel,
        (SMEM, HBM, HBM), (VMEM,) * 5,
        [hold(state), hold(speed.shape), hold(state), hold(line), hold(line)],
        [pltpu.SemaphoreType.DMA((2,))],
        micros=5,
    )(char_scale, flow, speed)
    (partly,) = call(
        functools.partial(fill_kernel, early),
        (SMEM,) * 3 + (VMEM,) * (1 + len(early)), (VMEM,),
        [hold(state)],
        aliases={3: 0},
        micros=2,
    )(tile, live, weight, flow_in, *(arrived[turn] for turn in early))
    filled, rows, even, odd, tail, head = call(
        functools.partial(last_fill_kernel, late),
        (VMEM,) + (SMEM,) * 3 + (VMEM,) * (1 + len(late)), (VMEM,) * 6,
        [hold(state), hold((4, *line)), hold((2, *line)), hold((2, *line)), hold(edge), hold(edge)],
        aliases={4: 0},
        micros=4,
    )(total, tile, live, weight, partly, *(arrived[turn] for turn in late))
    before = moved(tail, "span", 1)
    after = moved(head, "span", -1)
    met = []
    for message, shift in ((odd, 1), (even, 0)):
        others = [((i + shift) ^ 1) - shift for i in range(sections)]
        route = [(i, k if 0 <= k < sections else i) for i, k in enumerate(others)]
        met.append(lax.ppermute(message, "stream", route))
    odd, even = met
    assert sections <= 4
    split = (components + 1) // 2
    state_now, parts = filled, []
    for lowest, size in ((0, split), (split, components - split)):
        some = (size, rows_y, width_z)
        state_now, flux = call(
            functools.partial(scan_kernel, lowest),
            (SMEM, SMEM) + (VMEM,) * 7, (VMEM,) * 2,
            [hold(state), hold(some)],
            [pltpu.VMEM(edge, F32)] * 3,
            aliases={2: 0},
            micros=3 * size,
        )(char_scale, span_ratio, state_now, ratio, speed_in, tail, head, before, after)
        flux, beyond, first_slope, last_slope = call(
            functools.partial(edge_kernel, lowest),
            (VMEM,) * 6, (VMEM,) * 4,
            [jax.ShapeDtypeStruct(some, F32)] * 4,
        )(flux, total, last, rows, even, odd)
        fluxes = [moved(flux if d < 3 else beyond, "stream", d) for d in range(1, sections)]
        parts.append((lowest, some, first_slope, last_slope, fluxes))
    begun = ()
    for lowest, some, first_slope, last_slope, fluxes in parts:
        begun = call(
            functools.partial(combine_kernel, lowest, len(begun)),
            (VMEM,) * 6 + (HBM,) * len(begun) + (VMEM,) * (sections - 1), (HBM,),
            [jax.ShapeDtypeStruct(state, F32)],
            [
                pltpu.VMEM((width_x, *some), F32),
                pltpu.VMEM(some, F32),
                pltpu.SemaphoreType.DMA,
            ],
            aliases={6: 0} if begun else None,
            limit=10 << 20,
            micros=some[0],
        )(state_now, ratio, first_slope, last_slope, even, odd, *begun, *fluxes)
    (done,) = begun
    return jnp.transpose(done, (0, 2, 1, 3))[None]


def solution(mesh):
    return jax.shard_map(
        on_device,
        mesh=mesh,
        in_specs=(
            P("block", "stream", None, None, "span"),
            P("block", "stream", None, "span"),
            P(),
            P(),
            P("block", "span", "stream", None, None),
            P("block", "span", "stream", None, None),
            P("block", "span", "stream", None, None),
            P("block", "span", "stream", None, None),
        ),
        out_specs=P("block", "stream", None, None, "span"),
        check_vma=False,
    )
```

```python
import functools
import jax
import jax.numpy as jnp
from jax import lax
from jax.experimental import pallas as pl
from jax.experimental.pallas import tpu as pltpu
from jax.sharding import PartitionSpec as P


LANES = 128
SUB = 8
STEPS = 16
LAG = 7
F32 = jnp.float32


def space(kind):
    return pl.BlockSpec(memory_space=kind)


SMEM, VMEM, HBM = pltpu.SMEM, pltpu.VMEM, pltpu.HBM

RING = ("block", "span")


def limited(first, second):
    return jnp.maximum(
        jnp.minimum(second, jnp.maximum(first, 0.0)), jnp.minimum(first, 0.0)
    )


def call(kernel, ins, outs, out_shape, scratch=(), aliases=None, limit=8 << 20, micros=0):
    return pl.pallas_call(
        kernel,
        out_shape=out_shape,
        in_specs=[space(k) for k in ins],
        out_specs=[space(k) for k in outs],
        scratch_shapes=list(scratch),
        input_output_aliases=aliases or {},
        compiler_params=pltpu.CompilerParams(vmem_limit_bytes=limit),
        cost_estimate=pl.CostEstimate(flops=0, transcendentals=0, bytes_accessed=int(micros * 3.0e6)),
    )


def inside(axis, distance):
    source = lax.axis_index(axis) - distance
    return jnp.where((source >= 0) & (source < lax.axis_size(axis)), 1.0, 0.0)


def present(ref, axis, distance):
    return ref[...] * inside(axis, distance)


def beside(side, even_ref, odd_ref):
    odd = lax.axis_index("stream") % 2
    return jnp.where(odd == (1 if side == "behind" else 0), even_ref[...], odd_ref[...])


def gather_kernel(turns, send_ref, flow_ref, *refs):
    *out_refs, sem = refs
    _, capacity, _ = out_refs[0].shape
    rows_y = flow_ref.shape[2]
    place = lax.axis_index(RING)

    for k, (out_ref, turn) in enumerate(zip(out_refs, turns)):
        for slot in range(capacity):
            tile = send_ref[place ^ turn, slot]
            pltpu.make_async_copy(
                flow_ref.at[tile // rows_y, :, pl.ds(tile % rows_y, 1), :],
                out_ref.at[:, slot : slot + 1, :],
                sem.at[k],
            ).start()
    for k, out_ref in enumerate(out_refs):
        pltpu.make_async_copy(out_ref, out_ref, sem.at[k]).wait()


def growth_kernel(scale_ref, flow_hbm, speed_hbm, flow_ref, speed_ref, ratio_ref, total_ref, last_ref, sem):
    width_x, components, rows_y, width_z = ratio_ref.shape
    speed_copy = pltpu.make_async_copy(speed_hbm, speed_ref, sem.at[0])
    flow_copy = pltpu.make_async_copy(flow_hbm, flow_ref, sem.at[1])
    speed_copy.start()
    flow_copy.start()
    speed_copy.wait()
    halves = rows_y // SUB

    @pl.loop(0, components * halves)
    def _(group):
        v = group // halves
        y = pl.ds(pl.multiple_of((group % halves) * SUB, SUB), SUB)
        scale = 100.0 * scale_ref[v]

        def step(k, run):
            speeds = [speed_ref[k * STEPS + i, y, :] for i in range(STEPS)]
            ratios = [1.0 / (1.0 + scale * speed) for speed in speeds]
            for ratio in ratios:
                run = run - ratio * run
            for i in range(STEPS):
                ratio_ref[k * STEPS + i, v, y, :] = ratios[i]
            return run

        start = jnp.ones((SUB, width_z), F32)
        total_ref[v, y, :] = lax.fori_loop(0, width_x // STEPS, step, start)
        last_ref[v, y, :] = 1.0 - ratio_ref[width_x - 1, v, y, :]

    flow_copy.wait()


def fill_kernel(turns, tile_ref, live_ref, weight_ref, flow_ref, *refs):
    arrived_refs = refs[: len(turns)]
    filled_ref = refs[len(turns)]
    rows_y = filled_ref.shape[2]
    components, capacity, _ = arrived_refs[0].shape
    place = lax.axis_index(RING)

    for turn, arrived_ref in zip(turns, arrived_refs):
        peer = place ^ turn

        count = live_ref[peer, 0]
        for slot in range(1, capacity):
            count = count + live_ref[peer, slot]

        @pl.loop(0, (count + 1) // 2)
        def _(pair):
            slots = [2 * pair, 2 * pair + 1]
            tiles = [tile_ref[peer, slot] for slot in slots]
            spots = [(tile // rows_y, pl.ds(tile % rows_y, 1)) for tile in tiles]
            weights = [
                jnp.where(live_ref[peer, slot] == 1, weight_ref[peer, slot], 0.0) for slot in slots
            ]
            mixed = [
                (1.0 - weight) * filled_ref[x, v, y, :] + weight * arrived_ref[v, pl.ds(slot, 1), :]
                for v in range(components)
                for slot, (x, y), weight in zip(slots, spots, weights)
            ]
            for v in range(components):
                for i, (x, y) in enumerate(spots):
                    filled_ref[x, v, y, :] = mixed[2 * v + i]


def last_fill_kernel(turns, total_ref, *refs):
    *fill_refs, rows_ref, even_ref, odd_ref, tail_ref, head_ref = refs
    fill_kernel(turns, *fill_refs)
    filled_ref = fill_refs[-1]
    width_x, components, rows_y, width_z = filled_ref.shape
    odd = lax.axis_index("stream") % 2
    even_ref[0] = filled_ref[(width_x - 1) * (1 - odd)]
    odd_ref[0] = filled_ref[(width_x - 1) * odd]
    even_ref[1] = total_ref[...]
    odd_ref[1] = total_ref[...]
    lane = lax.broadcasted_iota(jnp.int32, (rows_y, LANES), 1)
    for v in range(components):

        def pack(x, packed):
            tail, head = packed
            here = lane // 2 == x
            tail = jnp.where(
                here, pltpu.roll(filled_ref[x, v, :, width_z - LANES :], 2 * x + 2, 1), tail
            )
            head = jnp.where(here, pltpu.roll(filled_ref[x, v, :, :LANES], 2 * x + 1, 1), head)
            return tail, head

        zero = jnp.zeros((rows_y, LANES), F32)
        tail_ref[v], head_ref[v] = lax.fori_loop(0, width_x, pack, (zero, zero), unroll=32)
        for spot, x in enumerate((0, 1, width_x - 2, width_x - 1)):
            rows_ref[spot, v] = filled_ref[x, v]


def scan_kernel(
    lowest, scale_ref, span_ref, filled_ref, ratio_ref, speed_ref, tail_ref, head_ref, before_ref, after_ref,
    local_ref, out_ref, prior_ref, face_ref, diff_ref
):
    width_x, _, rows_y, width_z = local_ref.shape
    components = out_ref.shape[0]
    halves = rows_y // SUB
    blocks = width_z // LANES
    before = present(before_ref, "span", 1)
    after = present(after_ref, "span", -1)
    tail = tail_ref[...]
    head = head_ref[...]
    outer = 0.5 * (before - pltpu.roll(before, 1, 2))
    inner = 0.5 * (head - before)
    prior_ref[...] = before
    face_ref[...] = before + limited(outer, inner)
    diff_ref[...] = 0.5 * (after - tail)
    lane = lax.broadcasted_iota(jnp.int32, (SUB, LANES), 1)
    first = lane == 0
    final = lane == LANES - 1

    @pl.loop(0, components * halves)
    def _(group):
        v = lowest + group // halves
        y = pl.ds(pl.multiple_of((group % halves) * SUB, SUB), SUB)
        scale_z = 100.0 * (scale_ref[v] * span_ref[v])
        prior = prior_ref[v, y, :]
        face = face_ref[v, y, :]
        diff = diff_ref[v, y, :]
        every = range(blocks)

        def load(ref, *at):
            return [ref[(*at, y, slice(b * LANES, (b + 1) * LANES))] for b in every]

        def right(values, edge):
            moved_right = [edge] + [pltpu.roll(u, 1, 1) for u in values]
            return [jnp.where(first, moved_right[b], moved_right[b + 1]) for b in every]

        def left(values, edge):
            moved_left = [pltpu.roll(u, LANES - 1, 1) for u in values] + [edge]
            return [jnp.where(final, moved_left[b + 1], moved_left[b]) for b in every]

        inflow = [jnp.zeros((SUB, LANES), F32)] * blocks
        rise = inflow
        rows, falls, faces, known = {}, {}, {}, {}
        for tick in range(width_x + 3 * LAG):
            i = tick
            if i < width_x:
                rows[i] = load(filled_ref, i, v)
                back = right(rows[i], pltpu.roll(prior, LANES - 2 * i - 1, 1))
                falls[i] = [0.5 * (rows[i][b] - back[b]) for b in every]
            i = tick - LAG
            if 0 <= i < width_x:
                fall = falls.pop(i)
                grow = left(fall, pltpu.roll(diff, LANES - 2 * i - 2, 1))
                faces[i] = [rows[i][b] + limited(fall[b], grow[b]) for b in every]
            i = tick - 2 * LAG
            if 0 <= i < width_x:
                flat = faces.pop(i)
                shifted = right(flat, pltpu.roll(face, LANES - 2 * i - 1, 1))
                known[i] = [rows[i][b] + scale_z * (shifted[b] - flat[b]) for b in every]
            i = tick - 3 * LAG
            if i >= 0:
                u = rows.pop(i)
                later = rows.get(i + 1, u)
                rise_later = [0.5 * (later[b] - u[b]) for b in every]
                ratio = load(ratio_ref, i, v)
                cross = known.pop(i)
                slope = [limited(rise[b], rise_later[b]) for b in every]
                total = [inflow[b] + (cross[b] + slope[b]) for b in every]
                value = [ratio[b] * total[b] for b in every]
                inflow = [total[b] - value[b] for b in every]
                rise = rise_later
                for b in every:
                    local_ref[i, v, y, slice(b * LANES, (b + 1) * LANES)] = value[b] - slope[b]
        for b in every:
            out_ref[v - lowest, y, slice(b * LANES, (b + 1) * LANES)] = inflow[b]


def edge_kernel(
    lowest, flux_ref, total_ref, last_ref, rows_ref, even_ref, odd_ref,
    flux_out, beyond_out, first_out, last_out,
):
    part = pl.ds(lowest, flux_ref.shape[0])
    behind = beside("behind", even_ref.at[0, part], odd_ref.at[0, part]) * inside("stream", 1)
    ahead = beside("ahead", even_ref.at[0, part], odd_ref.at[0, part]) * inside("stream", -1)
    row = [rows_ref[k, part] for k in range(4)]
    slope_first = limited(0.5 * (row[0] - behind), 0.5 * (row[1] - row[0]))
    slope_last = limited(0.5 * (row[3] - row[2]), 0.5 * (ahead - row[3]))
    kept = last_ref[part] * slope_last
    flux = flux_ref[...] + total_ref[part] * slope_first + kept
    flux_out[...] = flux
    beyond_out[...] = beside("ahead", even_ref.at[1, part], odd_ref.at[1, part]) * flux
    first_out[...] = slope_first
    last_out[...] = kept


def combine_kernel(lowest, begun, local_ref, ratio_ref, first_ref, last_ref, even_ref, odd_ref, *refs):
    *flux_refs, out_hbm, done_ref, inflow_ref, sem = refs[begun:]
    width_x, _, _, _ = local_ref.shape
    components = first_ref.shape[0]
    flux = [present(ref, "stream", i + 1) for i, ref in enumerate(flux_refs)]
    beyond = sum(flux[2:], flux[1]) if len(flux) > 1 else 0.0
    behind = beside("behind", *(ref.at[1, pl.ds(lowest, components)] for ref in (even_ref, odd_ref)))
    inflow_ref[...] = first_ref[...] + flux[0] + behind * beyond
    part = 4

    def copy_of(k):
        rows = pl.ds(k * part, part)
        return pltpu.make_async_copy(
            done_ref.at[rows], out_hbm.at[rows, pl.ds(lowest, components)], sem
        )

    @pl.loop(0, width_x // part)
    def _(k):
        for v in range(components):
            inflow = inflow_ref[v]
            outs = []
            for i in range(part):
                gain = ratio_ref[k * part + i, lowest + v] * inflow
                outs.append(local_ref[k * part + i, lowest + v] + gain)
                inflow = inflow - gain
            for i in range(part):
                done_ref[k * part + i, v] = outs[i]
            inflow_ref[v] = inflow

        @pl.when(k == 0)
        def _():
            done_ref[0] = done_ref[0] - first_ref[...]

        @pl.when(k == width_x // part - 1)
        def _():
            done_ref[width_x - 1] = done_ref[width_x - 1] - last_ref[...]

        copy_of(k).start()

    @pl.loop(0, width_x // part)
    def _(k):
        copy_of(k).wait()


def moved(value, axis, distance):
    count = lax.axis_size(axis)
    return lax.ppermute(value, axis, [(i, (i + distance) % count) for i in range(count)])


def on_device(
    flow_state, wave_speed, char_scale, span_ratio, send_tile, recv_tile, recv_live, interp_weight
):
    _, width_x, rows_y, components, width_z = flow_state.shape
    peers, capacity = send_tile.shape[-2:]
    sections = lax.axis_size("stream")
    flow = pltpu.with_memory_space_constraint(jnp.transpose(flow_state[0], (0, 2, 1, 3)), HBM)
    speed = wave_speed[0]
    state = (width_x, components, rows_y, width_z)
    line = (components, rows_y, width_z)
    edge = (components, rows_y, LANES)
    hold = lambda shape: pltpu.VMEM(shape, F32)
    send, tile, live, weight = (
        t.reshape(peers, capacity) for t in (send_tile, recv_tile, recv_live, interp_weight)
    )
    assert peers & (peers - 1) == 0

    order = sorted(range(1, peers), key=lambda turn: (turn == 1, turn & 1, turn))
    near = peers // 2 - 1
    arrived = {}
    groups = [order[:near], order[near:] + [0]]
    for turns in groups:
        outgoing = call(
            functools.partial(gather_kernel, turns),
            (SMEM, HBM), (VMEM,) * len(turns),
            [jax.ShapeDtypeStruct((components, capacity, width_z), F32)] * len(turns),
            [pltpu.SemaphoreType.DMA((len(turns),))],
            micros=1,
        )(send, flow)
        for turn, tiles in zip(turns, outgoing):
            route = [(i, i ^ turn) for i in range(peers)]
            arrived[turn] = lax.ppermute(tiles, RING, route) if turn else tiles
    late = order[near:-1][-2:]
    early = [turn for turn in order + [0] if turn not in late]
    flow_in, speed_in, ratio, total, last = call(
        growth_kernel,
        (SMEM, HBM, HBM), (VMEM,) * 5,
        [hold(state), hold(speed.shape), hold(state), hold(line), hold(line)],
        [pltpu.SemaphoreType.DMA((2,))],
        micros=5,
    )(char_scale, flow, speed)
    (partly,) = call(
        functools.partial(fill_kernel, early),
        (SMEM,) * 3 + (VMEM,) * (1 + len(early)), (VMEM,),
        [hold(state)],
        aliases={3: 0},
        micros=2,
    )(tile, live, weight, flow_in, *(arrived[turn] for turn in early))
    filled, rows, even, odd, tail, head = call(
        functools.partial(last_fill_kernel, late),
        (VMEM,) + (SMEM,) * 3 + (VMEM,) * (1 + len(late)), (VMEM,) * 6,
        [hold(state), hold((4, *line)), hold((2, *line)), hold((2, *line)), hold(edge), hold(edge)],
        aliases={4: 0},
        micros=4,
    )(total, tile, live, weight, partly, *(arrived[turn] for turn in late))
    before = moved(tail, "span", 1)
    after = moved(head, "span", -1)
    met = []
    for message, shift in ((odd, 1), (even, 0)):
        others = [((i + shift) ^ 1) - shift for i in range(sections)]
        route = [(i, k if 0 <= k < sections else i) for i, k in enumerate(others)]
        met.append(lax.ppermute(message, "stream", route))
    odd, even = met
    assert sections <= 4
    split = max(components - 1, 1)
    state_now, parts = filled, []
    for lowest, size in ((0, split), (split, components - split)):
        some = (size, rows_y, width_z)
        state_now, flux = call(
            functools.partial(scan_kernel, lowest),
            (SMEM, SMEM) + (VMEM,) * 7, (VMEM,) * 2,
            [hold(state), hold(some)],
            [pltpu.VMEM(edge, F32)] * 3,
            aliases={2: 0},
            micros=3 * size,
        )(char_scale, span_ratio, state_now, ratio, speed_in, tail, head, before, after)
        flux, beyond, first_slope, last_slope = call(
            functools.partial(edge_kernel, lowest),
            (VMEM,) * 6, (VMEM,) * 4,
            [jax.ShapeDtypeStruct(some, F32)] * 4,
        )(flux, total, last, rows, even, odd)
        fluxes = [moved(flux if d < 3 else beyond, "stream", d) for d in range(1, sections)]
        parts.append((lowest, some, first_slope, last_slope, fluxes))
    begun = ()
    for lowest, some, first_slope, last_slope, fluxes in parts:
        begun = call(
            functools.partial(combine_kernel, lowest, len(begun)),
            (VMEM,) * 6 + (HBM,) * len(begun) + (VMEM,) * (sections - 1), (HBM,),
            [jax.ShapeDtypeStruct(state, F32)],
            [
                pltpu.VMEM((width_x, *some), F32),
                pltpu.VMEM(some, F32),
                pltpu.SemaphoreType.DMA,
            ],
            aliases={6: 0} if begun else None,
            limit=12 << 20,
            micros=some[0],
        )(state_now, ratio, first_slope, last_slope, even, odd, *begun, *fluxes)
    (done,) = begun
    return jnp.transpose(done, (0, 2, 1, 3))[None]


def solution(mesh):
    return jax.shard_map(
        on_device,
        mesh=mesh,
        in_specs=(
            P("block", "stream", None, None, "span"),
            P("block", "stream", None, "span"),
            P(),
            P(),
            P("block", "span", "stream", None, None),
            P("block", "span", "stream", None, None),
            P("block", "span", "stream", None, None),
            P("block", "span", "stream", None, None),
        ),
        out_specs=P("block", "stream", None, None, "span"),
        check_vma=False,
    )
```

```python
import functools
import jax
import jax.numpy as jnp
from jax import lax
from jax.experimental import pallas as pl
from jax.experimental.pallas import tpu as pltpu
from jax.sharding import PartitionSpec as P


LANES = 128
SUB = 8
STEPS = 16
LAG = 7
F32 = jnp.float32


def space(kind):
    return pl.BlockSpec(memory_space=kind)


SMEM, VMEM, HBM = pltpu.SMEM, pltpu.VMEM, pltpu.HBM

RING = ("block", "span")


def limited(first, second):
    return jnp.maximum(
        jnp.minimum(second, jnp.maximum(first, 0.0)), jnp.minimum(first, 0.0)
    )


def call(kernel, ins, outs, out_shape, scratch=(), aliases=None, limit=8 << 20, micros=0):
    return pl.pallas_call(
        kernel,
        out_shape=out_shape,
        in_specs=[space(k) for k in ins],
        out_specs=[space(k) for k in outs],
        scratch_shapes=list(scratch),
        input_output_aliases=aliases or {},
        compiler_params=pltpu.CompilerParams(vmem_limit_bytes=limit),
        cost_estimate=pl.CostEstimate(flops=0, transcendentals=0, bytes_accessed=int(micros * 3.0e6)),
    )


def inside(axis, distance):
    source = lax.axis_index(axis) - distance
    return jnp.where((source >= 0) & (source < lax.axis_size(axis)), 1.0, 0.0)


def present(ref, axis, distance):
    return ref[...] * inside(axis, distance)


def beside(side, even_ref, odd_ref):
    odd = lax.axis_index("stream") % 2
    return jnp.where(odd == (1 if side == "behind" else 0), even_ref[...], odd_ref[...])


def gather_kernel(turns, send_ref, flow_ref, *refs):
    *out_refs, sem = refs
    _, capacity, _ = out_refs[0].shape
    rows_y = flow_ref.shape[2]
    place = lax.axis_index(RING)

    for k, (out_ref, turn) in enumerate(zip(out_refs, turns)):
        for slot in range(capacity):
            tile = send_ref[place ^ turn, slot]
            pltpu.make_async_copy(
                flow_ref.at[tile // rows_y, :, pl.ds(tile % rows_y, 1), :],
                out_ref.at[:, slot : slot + 1, :],
                sem.at[k],
            ).start()
    for k, out_ref in enumerate(out_refs):
        pltpu.make_async_copy(out_ref, out_ref, sem.at[k]).wait()


def growth_kernel(scale_ref, flow_hbm, speed_hbm, flow_ref, speed_ref, ratio_ref, total_ref, last_ref, sem):
    width_x, components, rows_y, width_z = ratio_ref.shape
    speed_copy = pltpu.make_async_copy(speed_hbm, speed_ref, sem.at[0])
    flow_copy = pltpu.make_async_copy(flow_hbm, flow_ref, sem.at[1])
    speed_copy.start()
    flow_copy.start()
    speed_copy.wait()
    halves = rows_y // SUB

    @pl.loop(0, components * halves)
    def _(group):
        v = group // halves
        y = pl.ds(pl.multiple_of((group % halves) * SUB, SUB), SUB)
        scale = 100.0 * scale_ref[v]

        def step(k, run):
            speeds = [speed_ref[k * STEPS + i, y, :] for i in range(STEPS)]
            ratios = [1.0 / (1.0 + scale * speed) for speed in speeds]
            for ratio in ratios:
                run = run - ratio * run
            for i in range(STEPS):
                ratio_ref[k * STEPS + i, v, y, :] = ratios[i]
            return run

        start = jnp.ones((SUB, width_z), F32)
        total_ref[v, y, :] = lax.fori_loop(0, width_x // STEPS, step, start)
        last_ref[v, y, :] = 1.0 - ratio_ref[width_x - 1, v, y, :]

    flow_copy.wait()


def fill_kernel(turns, tile_ref, live_ref, weight_ref, flow_ref, *refs):
    arrived_refs = refs[: len(turns)]
    filled_ref = refs[len(turns)]
    rows_y = filled_ref.shape[2]
    components, capacity, _ = arrived_refs[0].shape
    place = lax.axis_index(RING)

    for turn, arrived_ref in zip(turns, arrived_refs):
        peer = place ^ turn

        count = live_ref[peer, 0]
        for slot in range(1, capacity):
            count = count + live_ref[peer, slot]

        @pl.loop(0, (count + 1) // 2)
        def _(pair):
            slots = [2 * pair, 2 * pair + 1]
            tiles = [tile_ref[peer, slot] for slot in slots]
            spots = [(tile // rows_y, pl.ds(tile % rows_y, 1)) for tile in tiles]
            weights = [
                jnp.where(live_ref[peer, slot] == 1, weight_ref[peer, slot], 0.0) for slot in slots
            ]
            mixed = [
                (1.0 - weight) * filled_ref[x, v, y, :] + weight * arrived_ref[v, pl.ds(slot, 1), :]
                for v in range(components)
                for slot, (x, y), weight in zip(slots, spots, weights)
            ]
            for v in range(components):
                for i, (x, y) in enumerate(spots):
                    filled_ref[x, v, y, :] = mixed[2 * v + i]


def last_fill_kernel(turns, total_ref, *refs):
    *fill_refs, rows_ref, even_ref, odd_ref, tail_ref, head_ref = refs
    fill_kernel(turns, *fill_refs)
    filled_ref = fill_refs[-1]
    width_x, components, rows_y, width_z = filled_ref.shape
    odd = lax.axis_index("stream") % 2
    even_ref[0] = filled_ref[(width_x - 1) * (1 - odd)]
    odd_ref[0] = filled_ref[(width_x - 1) * odd]
    even_ref[1] = total_ref[...]
    odd_ref[1] = total_ref[...]
    lane = lax.broadcasted_iota(jnp.int32, (rows_y, LANES), 1)
    for v in range(components):

        def pack(x, packed):
            tail, head = packed
            here = lane // 2 == x
            tail = jnp.where(
                here, pltpu.roll(filled_ref[x, v, :, width_z - LANES :], 2 * x + 2, 1), tail
            )
            head = jnp.where(here, pltpu.roll(filled_ref[x, v, :, :LANES], 2 * x + 1, 1), head)
            return tail, head

        zero = jnp.zeros((rows_y, LANES), F32)
        tail_ref[v], head_ref[v] = lax.fori_loop(0, width_x, pack, (zero, zero), unroll=32)
        for spot, x in enumerate((0, 1, width_x - 2, width_x - 1)):
            rows_ref[spot, v] = filled_ref[x, v]


def scan_kernel(
    lowest, scale_ref, span_ref, filled_ref, ratio_ref, speed_ref, tail_ref, head_ref, before_ref, after_ref,
    local_ref, out_ref, prior_ref, face_ref, diff_ref
):
    width_x, _, rows_y, width_z = local_ref.shape
    components = out_ref.shape[0]
    halves = rows_y // SUB
    blocks = width_z // LANES
    before = present(before_ref, "span", 1)
    after = present(after_ref, "span", -1)
    tail = tail_ref[...]
    head = head_ref[...]
    outer = 0.5 * (before - pltpu.roll(before, 1, 2))
    inner = 0.5 * (head - before)
    prior_ref[...] = before
    face_ref[...] = before + limited(outer, inner)
    diff_ref[...] = 0.5 * (after - tail)
    lane = lax.broadcasted_iota(jnp.int32, (SUB, LANES), 1)
    first = lane == 0
    final = lane == LANES - 1

    @pl.loop(0, components * halves)
    def _(group):
        v = lowest + group // halves
        y = pl.ds(pl.multiple_of((group % halves) * SUB, SUB), SUB)
        scale_z = 100.0 * (scale_ref[v] * span_ref[v])
        prior = prior_ref[v, y, :]
        face = face_ref[v, y, :]
        diff = diff_ref[v, y, :]
        every = range(blocks)

        def load(ref, *at):
            return [ref[(*at, y, slice(b * LANES, (b + 1) * LANES))] for b in every]

        def right(values, edge):
            moved_right = [edge] + [pltpu.roll(u, 1, 1) for u in values]
            return [jnp.where(first, moved_right[b], moved_right[b + 1]) for b in every]

        def left(values, edge):
            moved_left = [pltpu.roll(u, LANES - 1, 1) for u in values] + [edge]
            return [jnp.where(final, moved_left[b + 1], moved_left[b]) for b in every]

        inflow = [jnp.zeros((SUB, LANES), F32)] * blocks
        rise = inflow
        rows, falls, faces, known = {}, {}, {}, {}
        for tick in range(width_x + 3 * LAG):
            i = tick
            if i < width_x:
                rows[i] = load(filled_ref, i, v)
                back = right(rows[i], pltpu.roll(prior, LANES - 2 * i - 1, 1))
                falls[i] = [0.5 * (rows[i][b] - back[b]) for b in every]
            i = tick - LAG
            if 0 <= i < width_x:
                fall = falls.pop(i)
                grow = left(fall, pltpu.roll(diff, LANES - 2 * i - 2, 1))
                faces[i] = [rows[i][b] + limited(fall[b], grow[b]) for b in every]
            i = tick - 2 * LAG
            if 0 <= i < width_x:
                flat = faces.pop(i)
                shifted = right(flat, pltpu.roll(face, LANES - 2 * i - 1, 1))
                known[i] = [rows[i][b] + scale_z * (shifted[b] - flat[b]) for b in every]
            i = tick - 3 * LAG
            if i >= 0:
                u = rows.pop(i)
                later = rows.get(i + 1, u)
                rise_later = [0.5 * (later[b] - u[b]) for b in every]
                ratio = load(ratio_ref, i, v)
                cross = known.pop(i)
                slope = [limited(rise[b], rise_later[b]) for b in every]
                total = [inflow[b] + (cross[b] + slope[b]) for b in every]
                value = [ratio[b] * total[b] for b in every]
                inflow = [total[b] - value[b] for b in every]
                rise = rise_later
                for b in every:
                    local_ref[i, v, y, slice(b * LANES, (b + 1) * LANES)] = value[b] - slope[b]
        for b in every:
            out_ref[v - lowest, y, slice(b * LANES, (b + 1) * LANES)] = inflow[b]


def edge_kernel(
    lowest, flux_ref, total_ref, last_ref, rows_ref, even_ref, odd_ref,
    flux_out, beyond_out, first_out, last_out,
):
    part = pl.ds(lowest, flux_ref.shape[0])
    behind = beside("behind", even_ref.at[0, part], odd_ref.at[0, part]) * inside("stream", 1)
    ahead = beside("ahead", even_ref.at[0, part], odd_ref.at[0, part]) * inside("stream", -1)
    row = [rows_ref[k, part] for k in range(4)]
    slope_first = limited(0.5 * (row[0] - behind), 0.5 * (row[1] - row[0]))
    slope_last = limited(0.5 * (row[3] - row[2]), 0.5 * (ahead - row[3]))
    kept = last_ref[part] * slope_last
    flux = flux_ref[...] + total_ref[part] * slope_first + kept
    flux_out[...] = flux
    beyond_out[...] = beside("ahead", even_ref.at[1, part], odd_ref.at[1, part]) * flux
    first_out[...] = slope_first
    last_out[...] = kept


def combine_kernel(lowest, begun, local_ref, ratio_ref, first_ref, last_ref, even_ref, odd_ref, *refs):
    *flux_refs, out_hbm, done_ref, inflow_ref, sem = refs[begun:]
    width_x, _, _, _ = local_ref.shape
    components = first_ref.shape[0]
    flux = [present(ref, "stream", i + 1) for i, ref in enumerate(flux_refs)]
    beyond = sum(flux[2:], flux[1]) if len(flux) > 1 else 0.0
    behind = beside("behind", *(ref.at[1, pl.ds(lowest, components)] for ref in (even_ref, odd_ref)))
    inflow_ref[...] = first_ref[...] + flux[0] + behind * beyond
    part = 4

    def copy_of(k):
        rows = pl.ds(k * part, part)
        return pltpu.make_async_copy(
            done_ref.at[rows], out_hbm.at[rows, pl.ds(lowest, components)], sem
        )

    @pl.loop(0, width_x // part)
    def _(k):
        for v in range(components):
            inflow = inflow_ref[v]
            outs = []
            for i in range(part):
                gain = ratio_ref[k * part + i, lowest + v] * inflow
                outs.append(local_ref[k * part + i, lowest + v] + gain)
                inflow = inflow - gain
            for i in range(part):
                done_ref[k * part + i, v] = outs[i]
            inflow_ref[v] = inflow

        @pl.when(k == 0)
        def _():
            done_ref[0] = done_ref[0] - first_ref[...]

        @pl.when(k == width_x // part - 1)
        def _():
            done_ref[width_x - 1] = done_ref[width_x - 1] - last_ref[...]

        copy_of(k).start()

    @pl.loop(0, width_x // part)
    def _(k):
        copy_of(k).wait()


def moved(value, axis, distance):
    count = lax.axis_size(axis)
    return lax.ppermute(value, axis, [(i, (i + distance) % count) for i in range(count)])


def on_device(
    flow_state, wave_speed, char_scale, span_ratio, send_tile, recv_tile, recv_live, interp_weight
):
    _, width_x, rows_y, components, width_z = flow_state.shape
    peers, capacity = send_tile.shape[-2:]
    sections = lax.axis_size("stream")
    flow = pltpu.with_memory_space_constraint(jnp.transpose(flow_state[0], (0, 2, 1, 3)), HBM)
    speed = wave_speed[0]
    state = (width_x, components, rows_y, width_z)
    line = (components, rows_y, width_z)
    edge = (components, rows_y, LANES)
    hold = lambda shape: pltpu.VMEM(shape, F32)
    send, tile, live, weight = (
        t.reshape(peers, capacity) for t in (send_tile, recv_tile, recv_live, interp_weight)
    )
    assert peers & (peers - 1) == 0

    far = lambda turn: bin(turn >> 1).count("1")
    order = sorted(range(1, peers), key=lambda turn: (turn == 1, turn & 1, -far(turn), turn))
    near = peers // 2 - 1
    arrived = {}
    groups = [order[:near], order[near:] + [0]]
    for turns in groups:
        outgoing = call(
            functools.partial(gather_kernel, turns),
            (SMEM, HBM), (VMEM,) * len(turns),
            [jax.ShapeDtypeStruct((components, capacity, width_z), F32)] * len(turns),
            [pltpu.SemaphoreType.DMA((len(turns),))],
            micros=1,
        )(send, flow)
        for turn, tiles in zip(turns, outgoing):
            route = [(i, i ^ turn) for i in range(peers)]
            arrived[turn] = lax.ppermute(tiles, RING, route) if turn else tiles
    late = order[near:-1][-2:]
    early = [turn for turn in order + [0] if turn not in late]
    flow_in, speed_in, ratio, total, last = call(
        growth_kernel,
        (SMEM, HBM, HBM), (VMEM,) * 5,
        [hold(state), hold(speed.shape), hold(state), hold(line), hold(line)],
        [pltpu.SemaphoreType.DMA((2,))],
        micros=5,
    )(char_scale, flow, speed)
    (partly,) = call(
        functools.partial(fill_kernel, early),
        (SMEM,) * 3 + (VMEM,) * (1 + len(early)), (VMEM,),
        [hold(state)],
        aliases={3: 0},
        micros=2,
    )(tile, live, weight, flow_in, *(arrived[turn] for turn in early))
    filled, rows, even, odd, tail, head = call(
        functools.partial(last_fill_kernel, late),
        (VMEM,) + (SMEM,) * 3 + (VMEM,) * (1 + len(late)), (VMEM,) * 6,
        [hold(state), hold((4, *line)), hold((2, *line)), hold((2, *line)), hold(edge), hold(edge)],
        aliases={4: 0},
        micros=4,
    )(total, tile, live, weight, partly, *(arrived[turn] for turn in late))
    before = moved(tail, "span", 1)
    after = moved(head, "span", -1)
    met = []
    for message, shift in ((odd, 1), (even, 0)):
        others = [((i + shift) ^ 1) - shift for i in range(sections)]
        route = [(i, k if 0 <= k < sections else i) for i, k in enumerate(others)]
        met.append(lax.ppermute(message, "stream", route))
    odd, even = met
    assert sections <= 4
    split = (components + 1) // 2
    state_now, parts = filled, []
    for lowest, size in ((0, split), (split, components - split)):
        some = (size, rows_y, width_z)
        state_now, flux = call(
            functools.partial(scan_kernel, lowest),
            (SMEM, SMEM) + (VMEM,) * 7, (VMEM,) * 2,
            [hold(state), hold(some)],
            [pltpu.VMEM(edge, F32)] * 3,
            aliases={2: 0},
            micros=3 * size,
        )(char_scale, span_ratio, state_now, ratio, speed_in, tail, head, before, after)
        flux, beyond, first_slope, last_slope = call(
            functools.partial(edge_kernel, lowest),
            (VMEM,) * 6, (VMEM,) * 4,
            [jax.ShapeDtypeStruct(some, F32)] * 4,
        )(flux, total, last, rows, even, odd)
        fluxes = [moved(flux if d < 3 else beyond, "stream", d) for d in range(1, sections)]
        parts.append((lowest, some, first_slope, last_slope, fluxes))
    begun = ()
    for lowest, some, first_slope, last_slope, fluxes in parts:
        begun = call(
            functools.partial(combine_kernel, lowest, len(begun)),
            (VMEM,) * 6 + (HBM,) * len(begun) + (VMEM,) * (sections - 1), (HBM,),
            [jax.ShapeDtypeStruct(state, F32)],
            [
                pltpu.VMEM((width_x, *some), F32),
                pltpu.VMEM(some, F32),
                pltpu.SemaphoreType.DMA,
            ],
            aliases={6: 0} if begun else None,
            limit=12 << 20,
            micros=some[0],
        )(state_now, ratio, first_slope, last_slope, even, odd, *begun, *fluxes)
    (done,) = begun
    return jnp.transpose(done, (0, 2, 1, 3))[None]


def solution(mesh):
    return jax.shard_map(
        on_device,
        mesh=mesh,
        in_specs=(
            P("block", "stream", None, None, "span"),
            P("block", "stream", None, "span"),
            P(),
            P(),
            P("block", "span", "stream", None, None),
            P("block", "span", "stream", None, None),
            P("block", "span", "stream", None, None),
            P("block", "span", "stream", None, None),
        ),
        out_specs=P("block", "stream", None, None, "span"),
        check_vma=False,
    )
```

```python
import functools
import jax
import jax.numpy as jnp
from jax import lax
from jax.experimental import pallas as pl
from jax.experimental.pallas import tpu as pltpu
from jax.sharding import PartitionSpec as P


LANES = 128
SUB = 8
STEPS = 16
LAG = 7
F32 = jnp.float32


def space(kind):
    return pl.BlockSpec(memory_space=kind)


SMEM, VMEM, HBM = pltpu.SMEM, pltpu.VMEM, pltpu.HBM

RING = ("block", "span")


def limited(first, second):
    return jnp.maximum(
        jnp.minimum(second, jnp.maximum(first, 0.0)), jnp.minimum(first, 0.0)
    )


def call(kernel, ins, outs, out_shape, scratch=(), aliases=None, limit=8 << 20, micros=0):
    return pl.pallas_call(
        kernel,
        out_shape=out_shape,
        in_specs=[space(k) for k in ins],
        out_specs=[space(k) for k in outs],
        scratch_shapes=list(scratch),
        input_output_aliases=aliases or {},
        compiler_params=pltpu.CompilerParams(vmem_limit_bytes=limit),
        cost_estimate=pl.CostEstimate(flops=0, transcendentals=0, bytes_accessed=int(micros * 3.0e6)),
    )


def inside(axis, distance):
    source = lax.axis_index(axis) - distance
    return jnp.where((source >= 0) & (source < lax.axis_size(axis)), 1.0, 0.0)


def present(ref, axis, distance):
    return ref[...] * inside(axis, distance)


def beside(side, even_ref, odd_ref):
    odd = lax.axis_index("stream") % 2
    return jnp.where(odd == (1 if side == "behind" else 0), even_ref[...], odd_ref[...])


def gather_kernel(turns, send_ref, flow_ref, *refs):
    *out_refs, sem = refs
    _, capacity, _ = out_refs[0].shape
    rows_y = flow_ref.shape[2]
    place = lax.axis_index(RING)

    for k, (out_ref, turn) in enumerate(zip(out_refs, turns)):
        for slot in range(capacity):
            tile = send_ref[place ^ turn, slot]
            pltpu.make_async_copy(
                flow_ref.at[tile // rows_y, :, pl.ds(tile % rows_y, 1), :],
                out_ref.at[:, slot : slot + 1, :],
                sem.at[k],
            ).start()
    for k, out_ref in enumerate(out_refs):
        pltpu.make_async_copy(out_ref, out_ref, sem.at[k]).wait()


def growth_kernel(scale_ref, flow_hbm, speed_hbm, flow_ref, speed_ref, ratio_ref, total_ref, last_ref, sem):
    width_x, components, rows_y, width_z = ratio_ref.shape
    speed_copy = pltpu.make_async_copy(speed_hbm, speed_ref, sem.at[0])
    flow_copy = pltpu.make_async_copy(flow_hbm, flow_ref, sem.at[1])
    speed_copy.start()
    flow_copy.start()
    speed_copy.wait()
    halves = rows_y // SUB

    @pl.loop(0, components * halves)
    def _(group):
        v = group // halves
        y = pl.ds(pl.multiple_of((group % halves) * SUB, SUB), SUB)
        scale = 100.0 * scale_ref[v]

        def step(k, run):
            speeds = [speed_ref[k * STEPS + i, y, :] for i in range(STEPS)]
            ratios = [1.0 / (1.0 + scale * speed) for speed in speeds]
            for ratio in ratios:
                run = run - ratio * run
            for i in range(STEPS):
                ratio_ref[k * STEPS + i, v, y, :] = ratios[i]
            return run

        start = jnp.ones((SUB, width_z), F32)
        total_ref[v, y, :] = lax.fori_loop(0, width_x // STEPS, step, start)
        last_ref[v, y, :] = 1.0 - ratio_ref[width_x - 1, v, y, :]

    flow_copy.wait()


def fill_kernel(turns, tile_ref, live_ref, weight_ref, flow_ref, *refs):
    arrived_refs = refs[: len(turns)]
    filled_ref = refs[len(turns)]
    rows_y = filled_ref.shape[2]
    components, capacity, _ = arrived_refs[0].shape
    place = lax.axis_index(RING)

    for turn, arrived_ref in zip(turns, arrived_refs):
        peer = place ^ turn

        count = live_ref[peer, 0]
        for slot in range(1, capacity):
            count = count + live_ref[peer, slot]

        @pl.loop(0, (count + 1) // 2)
        def _(pair):
            slots = [2 * pair, 2 * pair + 1]
            tiles = [tile_ref[peer, slot] for slot in slots]
            spots = [(tile // rows_y, pl.ds(tile % rows_y, 1)) for tile in tiles]
            weights = [
                jnp.where(live_ref[peer, slot] == 1, weight_ref[peer, slot], 0.0) for slot in slots
            ]
            mixed = [
                (1.0 - weight) * filled_ref[x, v, y, :] + weight * arrived_ref[v, pl.ds(slot, 1), :]
                for v in range(components)
                for slot, (x, y), weight in zip(slots, spots, weights)
            ]
            for v in range(components):
                for i, (x, y) in enumerate(spots):
                    filled_ref[x, v, y, :] = mixed[2 * v + i]


def last_fill_kernel(turns, total_ref, *refs):
    *fill_refs, rows_ref, even_ref, odd_ref, tail_ref, head_ref = refs
    fill_kernel(turns, *fill_refs)
    filled_ref = fill_refs[-1]
    width_x, components, rows_y, width_z = filled_ref.shape
    odd = lax.axis_index("stream") % 2
    even_ref[0] = filled_ref[(width_x - 1) * (1 - odd)]
    odd_ref[0] = filled_ref[(width_x - 1) * odd]
    even_ref[1] = total_ref[...]
    odd_ref[1] = total_ref[...]
    lane = lax.broadcasted_iota(jnp.int32, (rows_y, LANES), 1)
    for v in range(components):

        def pack(x, packed):
            tail, head = packed
            here = lane // 2 == x
            tail = jnp.where(
                here, pltpu.roll(filled_ref[x, v, :, width_z - LANES :], 2 * x + 2, 1), tail
            )
            head = jnp.where(here, pltpu.roll(filled_ref[x, v, :, :LANES], 2 * x + 1, 1), head)
            return tail, head

        zero = jnp.zeros((rows_y, LANES), F32)
        tail_ref[v], head_ref[v] = lax.fori_loop(0, width_x, pack, (zero, zero), unroll=32)
        for spot, x in enumerate((0, 1, width_x - 2, width_x - 1)):
            rows_ref[spot, v] = filled_ref[x, v]


def scan_kernel(
    lowest, scale_ref, span_ref, filled_ref, ratio_ref, speed_ref, tail_ref, head_ref, before_ref, after_ref,
    local_ref, out_ref, prior_ref, face_ref, diff_ref
):
    width_x, _, rows_y, width_z = local_ref.shape
    components = out_ref.shape[0]
    halves = rows_y // SUB
    blocks = width_z // LANES
    before = present(before_ref, "span", 1)
    after = present(after_ref, "span", -1)
    tail = tail_ref[...]
    head = head_ref[...]
    outer = 0.5 * (before - pltpu.roll(before, 1, 2))
    inner = 0.5 * (head - before)
    prior_ref[...] = before
    face_ref[...] = before + limited(outer, inner)
    diff_ref[...] = 0.5 * (after - tail)
    lane = lax.broadcasted_iota(jnp.int32, (SUB, LANES), 1)
    first = lane == 0
    final = lane == LANES - 1

    @pl.loop(0, components * halves)
    def _(group):
        v = lowest + group // halves
        y = pl.ds(pl.multiple_of((group % halves) * SUB, SUB), SUB)
        scale_z = 100.0 * (scale_ref[v] * span_ref[v])
        prior = prior_ref[v, y, :]
        face = face_ref[v, y, :]
        diff = diff_ref[v, y, :]
        every = range(blocks)

        def load(ref, *at):
            return [ref[(*at, y, slice(b * LANES, (b + 1) * LANES))] for b in every]

        def right(values, edge):
            moved_right = [edge] + [pltpu.roll(u, 1, 1) for u in values]
            return [jnp.where(first, moved_right[b], moved_right[b + 1]) for b in every]

        def left(values, edge):
            moved_left = [pltpu.roll(u, LANES - 1, 1) for u in values] + [edge]
            return [jnp.where(final, moved_left[b + 1], moved_left[b]) for b in every]

        inflow = [jnp.zeros((SUB, LANES), F32)] * blocks
        rise = inflow
        rows, falls, faces, known = {}, {}, {}, {}
        for tick in range(width_x + 3 * LAG):
            i = tick
            if i < width_x:
                rows[i] = load(filled_ref, i, v)
                back = right(rows[i], pltpu.roll(prior, LANES - 2 * i - 1, 1))
                falls[i] = [0.5 * (rows[i][b] - back[b]) for b in every]
            i = tick - LAG
            if 0 <= i < width_x:
                fall = falls.pop(i)
                grow = left(fall, pltpu.roll(diff, LANES - 2 * i - 2, 1))
                faces[i] = [rows[i][b] + limited(fall[b], grow[b]) for b in every]
            i = tick - 2 * LAG
            if 0 <= i < width_x:
                flat = faces.pop(i)
                shifted = right(flat, pltpu.roll(face, LANES - 2 * i - 1, 1))
                known[i] = [rows[i][b] + scale_z * (shifted[b] - flat[b]) for b in every]
            i = tick - 3 * LAG
            if i >= 0:
                u = rows.pop(i)
                later = rows.get(i + 1, u)
                rise_later = [0.5 * (later[b] - u[b]) for b in every]
                ratio = load(ratio_ref, i, v)
                cross = known.pop(i)
                slope = [limited(rise[b], rise_later[b]) for b in every]
                total = [inflow[b] + (cross[b] + slope[b]) for b in every]
                value = [ratio[b] * total[b] for b in every]
                inflow = [total[b] - value[b] for b in every]
                rise = rise_later
                for b in every:
                    local_ref[i, v, y, slice(b * LANES, (b + 1) * LANES)] = value[b] - slope[b]
        for b in every:
            out_ref[v - lowest, y, slice(b * LANES, (b + 1) * LANES)] = inflow[b]


def edge_kernel(
    lowest, total_ref, last_ref, rows_ref, even_ref, odd_ref, *refs
):
    *flux_refs, flux_out, beyond_out, first_out, last_out = refs
    part = pl.ds(lowest, flux_out.shape[0])
    behind = beside("behind", even_ref.at[0, part], odd_ref.at[0, part]) * inside("stream", 1)
    ahead = beside("ahead", even_ref.at[0, part], odd_ref.at[0, part]) * inside("stream", -1)
    row = [rows_ref[k, part] for k in range(4)]
    slope_first = limited(0.5 * (row[0] - behind), 0.5 * (row[1] - row[0]))
    slope_last = limited(0.5 * (row[3] - row[2]), 0.5 * (ahead - row[3]))
    kept = last_ref[part] * slope_last
    flux = jnp.concatenate([ref[...] for ref in flux_refs], axis=0)
    flux = flux + total_ref[part] * slope_first + kept
    flux_out[...] = flux
    beyond_out[...] = beside("ahead", even_ref.at[1, part], odd_ref.at[1, part]) * flux
    first_out[...] = slope_first
    last_out[...] = kept


def combine_kernel(lowest, begun, local_ref, ratio_ref, first_ref, last_ref, even_ref, odd_ref, *refs):
    *flux_refs, out_hbm, done_ref, inflow_ref, sem = refs[begun:]
    width_x, _, _, _ = local_ref.shape
    components = first_ref.shape[0]
    flux = [present(ref, "stream", i + 1) for i, ref in enumerate(flux_refs)]
    beyond = sum(flux[2:], flux[1]) if len(flux) > 1 else 0.0
    behind = beside("behind", *(ref.at[1, pl.ds(lowest, components)] for ref in (even_ref, odd_ref)))
    inflow_ref[...] = first_ref[...] + flux[0] + behind * beyond
    part = 4

    def copy_of(k):
        rows = pl.ds(k * part, part)
        return pltpu.make_async_copy(
            done_ref.at[rows], out_hbm.at[rows, pl.ds(lowest, components)], sem
        )

    @pl.loop(0, width_x // part)
    def _(k):
        for v in range(components):
            inflow = inflow_ref[v]
            outs = []
            for i in range(part):
                gain = ratio_ref[k * part + i, lowest + v] * inflow
                outs.append(local_ref[k * part + i, lowest + v] + gain)
                inflow = inflow - gain
            for i in range(part):
                done_ref[k * part + i, v] = outs[i]
            inflow_ref[v] = inflow

        @pl.when(k == 0)
        def _():
            done_ref[0] = done_ref[0] - first_ref[...]

        @pl.when(k == width_x // part - 1)
        def _():
            done_ref[width_x - 1] = done_ref[width_x - 1] - last_ref[...]

        copy_of(k).start()

    @pl.loop(0, width_x // part)
    def _(k):
        copy_of(k).wait()


def moved(value, axis, distance):
    count = lax.axis_size(axis)
    return lax.ppermute(value, axis, [(i, (i + distance) % count) for i in range(count)])


def on_device(
    flow_state, wave_speed, char_scale, span_ratio, send_tile, recv_tile, recv_live, interp_weight
):
    _, width_x, rows_y, components, width_z = flow_state.shape
    peers, capacity = send_tile.shape[-2:]
    sections = lax.axis_size("stream")
    flow = pltpu.with_memory_space_constraint(jnp.transpose(flow_state[0], (0, 2, 1, 3)), HBM)
    speed = wave_speed[0]
    state = (width_x, components, rows_y, width_z)
    line = (components, rows_y, width_z)
    edge = (components, rows_y, LANES)
    hold = lambda shape: pltpu.VMEM(shape, F32)
    send, tile, live, weight = (
        t.reshape(peers, capacity) for t in (send_tile, recv_tile, recv_live, interp_weight)
    )
    assert peers & (peers - 1) == 0

    far = lambda turn: bin(turn >> 1).count("1")
    order = sorted(range(1, peers), key=lambda turn: (turn == 1, turn & 1, -far(turn), turn))
    near = peers // 2 - 1
    send_hbm = pltpu.with_memory_space_constraint(send, HBM)
    arrived = {}
    groups = [order[:near], order[near:] + [0]]
    for turns in groups:
        outgoing = call(
            functools.partial(gather_kernel, turns),
            (SMEM, HBM), (VMEM,) * len(turns),
            [jax.ShapeDtypeStruct((components, capacity, width_z), F32)] * len(turns),
            [pltpu.SemaphoreType.DMA((len(turns),))],
            micros=1,
        )(send_hbm, flow)
        for turn, tiles in zip(turns, outgoing):
            route = [(i, i ^ turn) for i in range(peers)]
            arrived[turn] = lax.ppermute(tiles, RING, route) if turn else tiles
    late = order[near:-1][-2:]
    early = [turn for turn in order + [0] if turn not in late]
    flow_in, speed_in, ratio, total, last = call(
        growth_kernel,
        (SMEM, HBM, HBM), (VMEM,) * 5,
        [hold(state), hold(speed.shape), hold(state), hold(line), hold(line)],
        [pltpu.SemaphoreType.DMA((2,))],
        micros=5,
    )(char_scale, flow, speed)
    (partly,) = call(
        functools.partial(fill_kernel, early),
        (SMEM,) * 3 + (VMEM,) * (1 + len(early)), (VMEM,),
        [hold(state)],
        aliases={3: 0},
        micros=2,
    )(tile, live, weight, flow_in, *(arrived[turn] for turn in early))
    filled, rows, even, odd, tail, head = call(
        functools.partial(last_fill_kernel, late),
        (VMEM,) + (SMEM,) * 3 + (VMEM,) * (1 + len(late)), (VMEM,) * 6,
        [hold(state), hold((4, *line)), hold((2, *line)), hold((2, *line)), hold(edge), hold(edge)],
        aliases={4: 0},
        micros=4,
    )(total, tile, live, weight, partly, *(arrived[turn] for turn in late))
    before = moved(tail, "span", 1)
    after = moved(head, "span", -1)
    met = []
    for message, shift in ((odd, 1), (even, 0)):
        others = [((i + shift) ^ 1) - shift for i in range(sections)]
        route = [(i, k if 0 <= k < sections else i) for i, k in enumerate(others)]
        met.append(lax.ppermute(message, "stream", route))
    odd, even = met
    assert sections <= 4
    split = (components + 1) // 2
    state_now, fluxes = filled, []
    pieces = [(0, split)] + [(v, 1) for v in range(split, components)]
    for lowest, size in pieces:
        state_now, flux = call(
            functools.partial(scan_kernel, lowest),
            (SMEM, SMEM) + (VMEM,) * 7, (VMEM,) * 2,
            [hold(state), hold((size, rows_y, width_z))],
            [pltpu.VMEM(edge, F32)] * 3,
            aliases={2: 0},
            micros=3 * size,
        )(char_scale, span_ratio, state_now, ratio, speed_in, tail, head, before, after)
        fluxes.append(flux)
    parts = []
    for lowest, size, local in ((0, split, fluxes[:1]), (split, components - split, fluxes[1:])):
        some = (size, rows_y, width_z)
        flux, beyond, first_slope, last_slope = call(
            functools.partial(edge_kernel, lowest),
            (VMEM,) * (5 + len(local)), (VMEM,) * 4,
            [jax.ShapeDtypeStruct(some, F32)] * 4,
        )(total, last, rows, even, odd, *local)
        sent = [moved(flux if d < 3 else beyond, "stream", d) for d in range(1, sections)]
        parts.append((lowest, some, first_slope, last_slope, sent))
    begun = ()
    for lowest, some, first_slope, last_slope, fluxes in parts:
        begun = call(
            functools.partial(combine_kernel, lowest, len(begun)),
            (VMEM,) * 6 + (HBM,) * len(begun) + (VMEM,) * (sections - 1), (HBM,),
            [jax.ShapeDtypeStruct(state, F32)],
            [
                pltpu.VMEM((width_x, *some), F32),
                pltpu.VMEM(some, F32),
                pltpu.SemaphoreType.DMA,
            ],
            aliases={6: 0} if begun else None,
            limit=12 << 20,
            micros=some[0],
        )(state_now, ratio, first_slope, last_slope, even, odd, *begun, *fluxes)
    (done,) = begun
    return jnp.transpose(done, (0, 2, 1, 3))[None]


def solution(mesh):
    return jax.shard_map(
        on_device,
        mesh=mesh,
        in_specs=(
            P("block", "stream", None, None, "span"),
            P("block", "stream", None, "span"),
            P(),
            P(),
            P("block", "span", "stream", None, None),
            P("block", "span", "stream", None, None),
            P("block", "span", "stream", None, None),
            P("block", "span", "stream", None, None),
        ),
        out_specs=P("block", "stream", None, None, "span"),
        check_vma=False,
    )
```

```python
import functools
import jax
import jax.numpy as jnp
from jax import lax
from jax.experimental import pallas as pl
from jax.experimental.pallas import tpu as pltpu
from jax.sharding import PartitionSpec as P


LANES = 128
SUB = 8
STEPS = 16
LAG = 7
F32 = jnp.float32


def space(kind):
    return pl.BlockSpec(memory_space=kind)


SMEM, VMEM, HBM = pltpu.SMEM, pltpu.VMEM, pltpu.HBM

RING = ("block", "span")


def limited(first, second):
    return jnp.maximum(
        jnp.minimum(second, jnp.maximum(first, 0.0)), jnp.minimum(first, 0.0)
    )


def call(kernel, ins, outs, out_shape, scratch=(), aliases=None, limit=8 << 20, micros=0):
    return pl.pallas_call(
        kernel,
        out_shape=out_shape,
        in_specs=[space(k) for k in ins],
        out_specs=[space(k) for k in outs],
        scratch_shapes=list(scratch),
        input_output_aliases=aliases or {},
        compiler_params=pltpu.CompilerParams(vmem_limit_bytes=limit),
        cost_estimate=pl.CostEstimate(flops=0, transcendentals=0, bytes_accessed=int(micros * 3.0e6)),
    )


def inside(axis, distance):
    source = lax.axis_index(axis) - distance
    return jnp.where((source >= 0) & (source < lax.axis_size(axis)), 1.0, 0.0)


def present(ref, axis, distance):
    return ref[...] * inside(axis, distance)


def beside(side, even_ref, odd_ref):
    odd = lax.axis_index("stream") % 2
    return jnp.where(odd == (1 if side == "behind" else 0), even_ref[...], odd_ref[...])


def gather_kernel(turns, send_ref, flow_ref, *refs):
    *out_refs, sem = refs
    _, capacity, _ = out_refs[0].shape
    rows_y = flow_ref.shape[2]
    place = lax.axis_index(RING)

    for k, (out_ref, turn) in enumerate(zip(out_refs, turns)):
        for slot in range(capacity):
            tile = send_ref[place ^ turn, slot]
            pltpu.make_async_copy(
                flow_ref.at[tile // rows_y, :, pl.ds(tile % rows_y, 1), :],
                out_ref.at[:, slot : slot + 1, :],
                sem.at[k],
            ).start()
    for k, out_ref in enumerate(out_refs):
        pltpu.make_async_copy(out_ref, out_ref, sem.at[k]).wait()


def growth_kernel(scale_ref, flow_hbm, speed_hbm, flow_ref, speed_ref, ratio_ref, total_ref, last_ref, sem):
    width_x, components, rows_y, width_z = ratio_ref.shape
    speed_copy = pltpu.make_async_copy(speed_hbm, speed_ref, sem.at[0])
    flow_copy = pltpu.make_async_copy(flow_hbm, flow_ref, sem.at[1])
    speed_copy.start()
    flow_copy.start()
    speed_copy.wait()
    halves = rows_y // SUB

    @pl.loop(0, components * halves)
    def _(group):
        v = group // halves
        y = pl.ds(pl.multiple_of((group % halves) * SUB, SUB), SUB)
        scale = 100.0 * scale_ref[v]

        def step(k, run):
            speeds = [speed_ref[k * STEPS + i, y, :] for i in range(STEPS)]
            ratios = [1.0 / (1.0 + scale * speed) for speed in speeds]
            for ratio in ratios:
                run = run - ratio * run
            for i in range(STEPS):
                ratio_ref[k * STEPS + i, v, y, :] = ratios[i]
            return run

        start = jnp.ones((SUB, width_z), F32)
        total_ref[v, y, :] = lax.fori_loop(0, width_x // STEPS, step, start)
        last_ref[v, y, :] = 1.0 - ratio_ref[width_x - 1, v, y, :]

    flow_copy.wait()


def fill_kernel(turns, tile_ref, live_ref, weight_ref, flow_ref, *refs):
    arrived_refs = refs[: len(turns)]
    filled_ref = refs[len(turns)]
    rows_y = filled_ref.shape[2]
    components, capacity, _ = arrived_refs[0].shape
    place = lax.axis_index(RING)

    for turn, arrived_ref in zip(turns, arrived_refs):
        peer = place ^ turn

        count = live_ref[peer, 0]
        for slot in range(1, capacity):
            count = count + live_ref[peer, slot]

        @pl.loop(0, (count + 1) // 2)
        def _(pair):
            slots = [2 * pair, 2 * pair + 1]
            tiles = [tile_ref[peer, slot] for slot in slots]
            spots = [(tile // rows_y, pl.ds(tile % rows_y, 1)) for tile in tiles]
            weights = [
                jnp.where(live_ref[peer, slot] == 1, weight_ref[peer, slot], 0.0) for slot in slots
            ]
            mixed = [
                (1.0 - weight) * filled_ref[x, v, y, :] + weight * arrived_ref[v, pl.ds(slot, 1), :]
                for v in range(components)
                for slot, (x, y), weight in zip(slots, spots, weights)
            ]
            for v in range(components):
                for i, (x, y) in enumerate(spots):
                    filled_ref[x, v, y, :] = mixed[2 * v + i]


def last_fill_kernel(turns, *refs):
    *fill_refs, rows_ref, even_ref, odd_ref, tail_ref, head_ref = refs
    fill_kernel(turns, *fill_refs)
    filled_ref = fill_refs[-1]
    width_x, components, rows_y, width_z = filled_ref.shape
    odd = lax.axis_index("stream") % 2
    even_ref[...] = filled_ref[(width_x - 1) * (1 - odd)]
    odd_ref[...] = filled_ref[(width_x - 1) * odd]
    lane = lax.broadcasted_iota(jnp.int32, (rows_y, LANES), 1)
    for v in range(components):

        def pack(x, packed):
            tail, head = packed
            here = lane // 2 == x
            tail = jnp.where(
                here, pltpu.roll(filled_ref[x, v, :, width_z - LANES :], 2 * x + 2, 1), tail
            )
            head = jnp.where(here, pltpu.roll(filled_ref[x, v, :, :LANES], 2 * x + 1, 1), head)
            return tail, head

        zero = jnp.zeros((rows_y, LANES), F32)
        tail_ref[v], head_ref[v] = lax.fori_loop(0, width_x, pack, (zero, zero), unroll=32)
        for spot, x in enumerate((0, 1, width_x - 2, width_x - 1)):
            rows_ref[spot, v] = filled_ref[x, v]


def scan_kernel(
    lowest, scale_ref, span_ref, filled_ref, ratio_ref, speed_ref, tail_ref, head_ref, before_ref, after_ref,
    local_ref, out_ref, prior_ref, face_ref, diff_ref
):
    width_x, _, rows_y, width_z = local_ref.shape
    components = out_ref.shape[0]
    halves = rows_y // SUB
    blocks = width_z // LANES
    before = present(before_ref, "span", 1)
    after = present(after_ref, "span", -1)
    tail = tail_ref[...]
    head = head_ref[...]
    outer = 0.5 * (before - pltpu.roll(before, 1, 2))
    inner = 0.5 * (head - before)
    prior_ref[...] = before
    face_ref[...] = before + limited(outer, inner)
    diff_ref[...] = 0.5 * (after - tail)
    lane = lax.broadcasted_iota(jnp.int32, (SUB, LANES), 1)
    first = lane == 0
    final = lane == LANES - 1

    @pl.loop(0, components * halves)
    def _(group):
        v = lowest + group // halves
        y = pl.ds(pl.multiple_of((group % halves) * SUB, SUB), SUB)
        scale_z = 100.0 * (scale_ref[v] * span_ref[v])
        prior = prior_ref[v, y, :]
        face = face_ref[v, y, :]
        diff = diff_ref[v, y, :]
        every = range(blocks)

        def load(ref, *at):
            return [ref[(*at, y, slice(b * LANES, (b + 1) * LANES))] for b in every]

        def right(values, edge):
            moved_right = [edge] + [pltpu.roll(u, 1, 1) for u in values]
            return [jnp.where(first, moved_right[b], moved_right[b + 1]) for b in every]

        def left(values, edge):
            moved_left = [pltpu.roll(u, LANES - 1, 1) for u in values] + [edge]
            return [jnp.where(final, moved_left[b + 1], moved_left[b]) for b in every]

        inflow = [jnp.zeros((SUB, LANES), F32)] * blocks
        rise = inflow
        rows, falls, faces, known = {}, {}, {}, {}
        for tick in range(width_x + 3 * LAG):
            i = tick
            if i < width_x:
                rows[i] = load(filled_ref, i, v)
                back = right(rows[i], pltpu.roll(prior, LANES - 2 * i - 1, 1))
                falls[i] = [0.5 * (rows[i][b] - back[b]) for b in every]
            i = tick - LAG
            if 0 <= i < width_x:
                fall = falls.pop(i)
                grow = left(fall, pltpu.roll(diff, LANES - 2 * i - 2, 1))
                faces[i] = [rows[i][b] + limited(fall[b], grow[b]) for b in every]
            i = tick - 2 * LAG
            if 0 <= i < width_x:
                flat = faces.pop(i)
                shifted = right(flat, pltpu.roll(face, LANES - 2 * i - 1, 1))
                known[i] = [rows[i][b] + scale_z * (shifted[b] - flat[b]) for b in every]
            i = tick - 3 * LAG
            if i >= 0:
                u = rows.pop(i)
                later = rows.get(i + 1, u)
                rise_later = [0.5 * (later[b] - u[b]) for b in every]
                ratio = load(ratio_ref, i, v)
                cross = known.pop(i)
                slope = [limited(rise[b], rise_later[b]) for b in every]
                total = [inflow[b] + (cross[b] + slope[b]) for b in every]
                value = [ratio[b] * total[b] for b in every]
                inflow = [total[b] - value[b] for b in every]
                rise = rise_later
                for b in every:
                    local_ref[i, v, y, slice(b * LANES, (b + 1) * LANES)] = value[b] - slope[b]
        for b in every:
            out_ref[v - lowest, y, slice(b * LANES, (b + 1) * LANES)] = inflow[b]


def edge_kernel(
    lowest, flux_ref, total_ref, last_ref, rows_ref, even_ref, odd_ref,
    even_total_ref, odd_total_ref, flux_out, beyond_out, first_out, last_out,
):
    part = pl.ds(lowest, flux_ref.shape[0])
    behind = beside("behind", even_ref.at[part], odd_ref.at[part]) * inside("stream", 1)
    ahead = beside("ahead", even_ref.at[part], odd_ref.at[part]) * inside("stream", -1)
    row = [rows_ref[k, part] for k in range(4)]
    slope_first = limited(0.5 * (row[0] - behind), 0.5 * (row[1] - row[0]))
    slope_last = limited(0.5 * (row[3] - row[2]), 0.5 * (ahead - row[3]))
    kept = last_ref[part] * slope_last
    flux = flux_ref[...] + total_ref[part] * slope_first + kept
    flux_out[...] = flux
    beyond_out[...] = beside("ahead", even_total_ref.at[part], odd_total_ref.at[part]) * flux
    first_out[...] = slope_first
    last_out[...] = kept


def combine_kernel(lowest, begun, local_ref, ratio_ref, first_ref, last_ref, even_ref, odd_ref, *refs):
    *flux_refs, out_hbm, done_ref, inflow_ref, sem = refs[begun:]
    width_x, _, _, _ = local_ref.shape
    components = first_ref.shape[0]
    flux = [present(ref, "stream", i + 1) for i, ref in enumerate(flux_refs)]
    beyond = sum(flux[2:], flux[1]) if len(flux) > 1 else 0.0
    behind = beside("behind", *(ref.at[pl.ds(lowest, components)] for ref in (even_ref, odd_ref)))
    inflow_ref[...] = first_ref[...] + flux[0] + behind * beyond
    part = 4

    def copy_of(k):
        rows = pl.ds(k * part, part)
        return pltpu.make_async_copy(
            done_ref.at[rows], out_hbm.at[rows, pl.ds(lowest, components)], sem
        )

    @pl.loop(0, width_x // part)
    def _(k):
        for v in range(components):
            inflow = inflow_ref[v]
            outs = []
            for i in range(part):
                gain = ratio_ref[k * part + i, lowest + v] * inflow
                outs.append(local_ref[k * part + i, lowest + v] + gain)
                inflow = inflow - gain
            for i in range(part):
                done_ref[k * part + i, v] = outs[i]
            inflow_ref[v] = inflow

        @pl.when(k == 0)
        def _():
            done_ref[0] = done_ref[0] - first_ref[...]

        @pl.when(k == width_x // part - 1)
        def _():
            done_ref[width_x - 1] = done_ref[width_x - 1] - last_ref[...]

        copy_of(k).start()

    @pl.loop(0, width_x // part)
    def _(k):
        copy_of(k).wait()


def moved(value, axis, distance):
    count = lax.axis_size(axis)
    return lax.ppermute(value, axis, [(i, (i + distance) % count) for i in range(count)])


def meet(value, shift):
    count = lax.axis_size("stream")
    others = [((i + shift) ^ 1) - shift for i in range(count)]
    return lax.ppermute(value, "stream", [(i, k if 0 <= k < count else i) for i, k in enumerate(others)])


def on_device(
    flow_state, wave_speed, char_scale, span_ratio, send_tile, recv_tile, recv_live, interp_weight
):
    _, width_x, rows_y, components, width_z = flow_state.shape
    peers, capacity = send_tile.shape[-2:]
    sections = lax.axis_size("stream")
    flow = pltpu.with_memory_space_constraint(jnp.transpose(flow_state[0], (0, 2, 1, 3)), HBM)
    speed = wave_speed[0]
    state = (width_x, components, rows_y, width_z)
    line = (components, rows_y, width_z)
    edge = (components, rows_y, LANES)
    hold = lambda shape: pltpu.VMEM(shape, F32)
    send, tile, live, weight = (
        t.reshape(peers, capacity) for t in (send_tile, recv_tile, recv_live, interp_weight)
    )
    assert peers & (peers - 1) == 0

    far = lambda turn: bin(turn >> 1).count("1")
    order = sorted(range(1, peers), key=lambda turn: (turn == 1, turn & 1, -far(turn), turn))
    near = peers // 2 - 1
    send_hbm = pltpu.with_memory_space_constraint(send, HBM)
    arrived = {}
    groups = [order[:near], order[near:] + [0]]
    for turns in groups:
        outgoing = call(
            functools.partial(gather_kernel, turns),
            (SMEM, HBM), (VMEM,) * len(turns),
            [jax.ShapeDtypeStruct((components, capacity, width_z), F32)] * len(turns),
            [pltpu.SemaphoreType.DMA((len(turns),))],
            micros=1,
        )(send_hbm, flow)
        for turn, tiles in zip(turns, outgoing):
            route = [(i, i ^ turn) for i in range(peers)]
            arrived[turn] = lax.ppermute(tiles, RING, route) if turn else tiles
    late = order[near:-1][-2:]
    early = [turn for turn in order + [0] if turn not in late]
    flow_in, speed_in, ratio, total, last = call(
        growth_kernel,
        (SMEM, HBM, HBM), (VMEM,) * 5,
        [hold(state), hold(speed.shape), hold(state), hold(line), hold(line)],
        [pltpu.SemaphoreType.DMA((2,))],
        micros=5,
    )(char_scale, flow, speed)
    odd_total, even_total = meet(total, 1), meet(total, 0)
    (partly,) = call(
        functools.partial(fill_kernel, early),
        (SMEM,) * 3 + (VMEM,) * (1 + len(early)), (VMEM,),
        [hold(state)],
        aliases={3: 0},
        micros=2,
    )(tile, live, weight, flow_in, *(arrived[turn] for turn in early))
    filled, rows, even, odd, tail, head = call(
        functools.partial(last_fill_kernel, late),
        (SMEM,) * 3 + (VMEM,) * (1 + len(late)), (VMEM,) * 6,
        [hold(state), hold((4, *line)), hold(line), hold(line), hold(edge), hold(edge)],
        aliases={3: 0},
        micros=4,
    )(tile, live, weight, partly, *(arrived[turn] for turn in late))
    before = moved(tail, "span", 1)
    after = moved(head, "span", -1)
    odd = meet(odd, 1)
    even = meet(even, 0)
    assert sections <= 4
    split = (components + 1) // 2
    state_now, parts = filled, []
    for lowest, size in ((0, split), (split, components - split)):
        some = (size, rows_y, width_z)
        state_now, flux = call(
            functools.partial(scan_kernel, lowest),
            (SMEM, SMEM) + (VMEM,) * 7, (VMEM,) * 2,
            [hold(state), hold(some)],
            [pltpu.VMEM(edge, F32)] * 3,
            aliases={2: 0},
            micros=3 * size,
        )(char_scale, span_ratio, state_now, ratio, speed_in, tail, head, before, after)
        flux, beyond, first_slope, last_slope = call(
            functools.partial(edge_kernel, lowest),
            (VMEM,) * 8, (VMEM,) * 4,
            [jax.ShapeDtypeStruct(some, F32)] * 4,
        )(flux, total, last, rows, even, odd, even_total, odd_total)
        fluxes = [moved(flux if d < 3 else beyond, "stream", d) for d in range(1, sections)]
        parts.append((lowest, some, first_slope, last_slope, fluxes))
    begun = ()
    for lowest, some, first_slope, last_slope, fluxes in parts:
        begun = call(
            functools.partial(combine_kernel, lowest, len(begun)),
            (VMEM,) * 6 + (HBM,) * len(begun) + (VMEM,) * (sections - 1), (HBM,),
            [jax.ShapeDtypeStruct(state, F32)],
            [
                pltpu.VMEM((width_x, *some), F32),
                pltpu.VMEM(some, F32),
                pltpu.SemaphoreType.DMA,
            ],
            aliases={6: 0} if begun else None,
            limit=12 << 20,
            micros=some[0],
        )(state_now, ratio, first_slope, last_slope, even_total, odd_total, *begun, *fluxes)
    (done,) = begun
    return jnp.transpose(done, (0, 2, 1, 3))[None]


def solution(mesh):
    return jax.shard_map(
        on_device,
        mesh=mesh,
        in_specs=(
            P("block", "stream", None, None, "span"),
            P("block", "stream", None, "span"),
            P(),
            P(),
            P("block", "span", "stream", None, None),
            P("block", "span", "stream", None, None),
            P("block", "span", "stream", None, None),
            P("block", "span", "stream", None, None),
        ),
        out_specs=P("block", "stream", None, None, "span"),
        check_vma=False,
    )
```
